32 devices in a mesh: batch: 4 (over y, x), segment: 8 (over z, core).
Axes of the slice: x: 2, y: 2, z: 4, core: 2. Of those that a mesh axis runs over, the one named last changes fastest.
Arguments:
- tokens: bfloat16 [16, 1024, 1024], P('batch', 'segment'), may hold values from -6 to 6
- doc_ids: int32 [16, 1024], P('batch'), may hold values from 0 to 3, as said below
- knn_index: int32 [16, 1024, 8, 32], P('batch', 'segment'), may hold values from 0 to 255, as said below
- mem_keys: bfloat16 [256, 1024], P('segment'), may hold values from -6 to 6
- mem_values: bfloat16 [256, 1024], P('segment'), may hold values from -6 to 6
- qkv_weight: bfloat16 [8, 256, 3072], P('segment', None, 'batch'), may hold values from -0.1875 to 0.1875
- out_weight: bfloat16 [8, 256, 1024], P('segment', None, 'batch'), may hold values from -0.75 to 0.75
- in_weight: bfloat16 [8, 256, 4096], P('segment', None, 'batch'), may hold values from -0.1875 to 0.1875
- down_weight: bfloat16 [8, 1024, 1024], P('segment', None, 'batch'), may hold values from -0.09375 to 0.09375
- norm_gain: bfloat16 [8, 2, 256], P('segment', None, 'batch'), may hold values from 0.5 to 1.5
- norm_bias: bfloat16 [8, 2, 256], P('segment', None, 'batch'), may hold values from -2 to 2
- rel_table: float32 [2, 32, 8], replicated, may hold values from -4 to 4
- mem_gate: float32 [8], replicated, may hold values from -2 to 2
- cotangent: bfloat16 [16, 1024, 1024], P('batch', 'segment'), may hold values from -6 to 6
Outputs:
- mixed: bfloat16 [16, 1024, 1024], P('batch', 'segment')
- input_grad: bfloat16 [16, 1024, 1024], P('batch', 'segment')
- qkv_grad: float32 [8, 256, 3072], P('segment', None, 'batch')
- out_grad: float32 [8, 256, 1024], P('segment', None, 'batch')
- in_grad: float32 [8, 256, 4096], P('segment', None, 'batch')
- down_grad: float32 [8, 1024, 1024], P('segment', None, 'batch')
- gain_grad: float32 [8, 2, 256], P('segment', None, 'batch')
- bias_grad: float32 [8, 2, 256], P('segment', None, 'batch')
- table_grad: float32 [2, 32, 8], replicated
- gate_grad: float32 [8], replicated
The draws below stay inside these ranges and needn't reach their ends.
Inputs may be any that keep to these rules, and one draw needn't show every extreme that they name: `doc_ids`: along a sequence the document numbers never fall; among the 4 sequences of each index of batch one, drawn from the seed, is a single document. `knn_index`: the 32 slots of one token and head are distinct.
All inputs are finite; a program needn't handle non-finite values.
Results may differ from the reference program's by a relative error of at most 0.019.
Values may be sent and summed in bfloat16 or wider, within the bound.
No kernel may reach another device: no remote copies, remote signals or barrier semaphores. Data moves between devices by JAX's collectives and lax.ppermute only.
A program may use at most 512 MiB of HBM per device.

```python
import math
import jax
import jax.numpy as jnp
import numpy as np
from jax import lax

D = 1024
HEADS = 8
HD = 128
FF = 4096
WIN = 512
TOPK = 32
BUCKETS = 32
LAYERS = 2
DOCS = 4
STRETCHES = 4
SEQ_DEV = 4
LEN = 1024
NSEQ = 16
MEM = 256
N_SEGMENT = 8


def draw_doc_ids(key, part):
    cut_key, pick_key = jax.random.split(jax.random.fold_in(key, 7))
    cuts = jax.random.randint(cut_key, (NSEQ, DOCS - 1), 1, LEN, dtype=jnp.int32)
    groups = NSEQ // SEQ_DEV
    pick = jax.random.randint(pick_key, (groups, 1), 0, SEQ_DEV, dtype=jnp.int32)
    whole = (jnp.arange(SEQ_DEV, dtype=jnp.int32)[None, :] == pick).reshape(NSEQ)
    cuts = jnp.where(whole[:, None], LEN, cuts)
    positions = jnp.arange(LEN, dtype=jnp.int32)
    return jnp.sum((positions[None, :, None] >= cuts[:, None, :]).astype(jnp.int32), axis=-1).astype(jnp.int32)


def draw_knn_index(key, part):
    group_size = MEM // TOPK
    first_key, second_key = jax.random.split(key)
    starts = jax.random.randint(first_key, (NSEQ, LEN, HEADS, 1), 0, MEM, dtype=jnp.int32)
    jitter = jax.random.randint(second_key, (NSEQ, LEN, HEADS, TOPK), 0, group_size, dtype=jnp.int32)
    starts = starts.at[0, 0, 0, 0].set(0)
    jitter = jitter.at[0, 0, 0, 0].set(0)
    jitter = jitter.at[0, 0, 0, TOPK - 1].set(group_size - 1)
    offsets = jnp.arange(TOPK, dtype=jnp.int32) * group_size
    return ((starts + offsets + jitter) % MEM).astype(jnp.int32)


def shard_levels(rng, extent, shards, smallest, high):
    def one(dim, blocks):
        heights = jax.random.uniform(jax.random.fold_in(jax.random.fold_in(rng, 6), dim), (blocks,), jnp.float32, smallest / len(shards), high / len(shards))
        return jnp.repeat(jnp.exp(heights), extent[dim] // blocks).reshape((-1,) + (1,) * (len(extent) - dim - 1))

    gain = one(*shards[0])
    for cut in shards[1:]:
        gain = gain * one(*cut)
    return gain


def noise(stream_key, dims, scale, limit, cuts=(), kind=jnp.bfloat16):
    array = jax.random.normal(stream_key, dims, jnp.float32) * scale
    if len(cuts) > 0:
        array = shard_levels(stream_key, dims, cuts, -0.22, 0.18) * array
    return jnp.clip(array, min=-limit, max=limit).astype(kind)


def setup_inputs(seed: int = 0) -> dict:
    key_list = jax.random.split(jax.random.key(seed), 15)
    tokens = noise(key_list[0], (NSEQ, LEN, D), 1.0, 6.0, ((0, 4), (1, 8)))
    doc_ids = draw_doc_ids(jax.random.fold_in(key_list[14], 71), 0)
    knn_index = draw_knn_index(jax.random.fold_in(key_list[14], 71), 0)
    mem_keys = noise(key_list[3], (MEM, D), 1.0, 6.0, ((0, 8),))
    mem_values = noise(key_list[4], (MEM, D), 1.0, 6.0, ((0, 8),))
    qkv_weight = noise(key_list[5], (N_SEGMENT, D // STRETCHES, 3 * D), D ** -0.5, 0.1875, ((0, 8), (2, 4)))
    out_weight = noise(key_list[6], (N_SEGMENT, D // STRETCHES, D), (D // 16) ** -0.5, 0.75, ((0, 8), (2, 4)))
    in_weight = noise(key_list[7], (N_SEGMENT, D // STRETCHES, FF), D ** -0.5, 0.1875, ((0, 8), (2, 4)))
    down_weight = noise(key_list[8], (N_SEGMENT, FF // STRETCHES, D), FF ** -0.5, 0.09375, ((0, 8), (2, 4)))
    norm_gain = jnp.clip(1.0 + 0.1 * jax.random.normal(key_list[9], (N_SEGMENT, 2, D // STRETCHES), jnp.float32), 0.5, 1.5).astype(jnp.bfloat16)
    norm_bias = noise(key_list[10], (N_SEGMENT, 2, D // STRETCHES), 0.3, 2.0, ((0, 8), (2, 4)))
    rel_table = noise(key_list[11], (LAYERS, BUCKETS, HEADS), 1.0, 4.0, (), jnp.float32)
    mem_gate = jnp.clip(jax.random.uniform(key_list[12], (HEADS,), jnp.float32, -2.0, 2.0), -2.0, 2.0)
    cotangent = noise(key_list[13], (NSEQ, LEN, D), 1.0, 6.0, ((0, 4), (1, 8)))
    return dict(tokens=tokens, doc_ids=doc_ids, knn_index=knn_index, mem_keys=mem_keys, mem_values=mem_values, qkv_weight=qkv_weight, out_weight=out_weight, in_weight=in_weight, down_weight=down_weight, norm_gain=norm_gain, norm_bias=norm_bias, rel_table=rel_table, mem_gate=mem_gate, cotangent=cotangent)


norm_eps = 1e-05
big_negative = -1e+30
bucket_edges = np.ceil(16.0 * 8.0 ** (np.arange(1, 16) / 16.0)).astype(np.int32)
highest = lax.Precision.HIGHEST

@jax.custom_vjp
def low(v):
    return lax.optimization_barrier(v.astype(jnp.bfloat16)).astype(jnp.float32)

@jax.custom_vjp
def low_back(v):
    return v

def low_keep(v):
    return (low(v), None)

def low_pass(kept, grad):
    return (grad,)

def back_keep(v):
    return (v, None)

def back_low(kept, grad):
    return (low(grad),)
low.defvjp(low_keep, low_pass)
low_back.defvjp(back_keep, back_low)

def both_round(values):
    return low_back(low(values))

def bucket_of(distance):
    edges = jnp.asarray(bucket_edges)
    beyond = lax.optimization_barrier(jnp.sum((distance[..., None] >= edges).astype(jnp.int32), axis=-1))
    return jnp.where(distance < 16, distance, 16 + beyond).astype(jnp.int32)

def segment_to_layers(stored):
    rest = stored.shape[1:]
    grouped = stored.reshape((STRETCHES, LAYERS) + rest)
    return jnp.moveaxis(grouped, 1, 0).reshape((LAYERS, STRETCHES * rest[0]) + rest[1:])

def gains_to_layers(stored):
    grouped = stored.reshape(STRETCHES, LAYERS, 2, stored.shape[2])
    return jnp.transpose(grouped, (1, 2, 0, 3)).reshape(LAYERS, 2, STRETCHES * stored.shape[2])

def layer_norm(values, gain_row, shift_row):
    center = values - lax.optimization_barrier(jnp.mean(values, axis=-1, keepdims=True))
    return center * lax.rsqrt(lax.optimization_barrier(jnp.mean(center * center, axis=-1, keepdims=True)) + norm_eps) * gain_row + shift_row

def matmul(left, right):
    return jnp.dot(left, right, precision=highest)

def softmax_rows(scores):
    raised = jnp.exp(scores - lax.optimization_barrier(jnp.max(scores, axis=-1, keepdims=True)))
    return raised / lax.optimization_barrier(jnp.sum(raised, axis=-1, keepdims=True))

def local_attention(queries, key_rows, value_rows, table_now, documents):
    length = queries.shape[0]
    blocks = length // WIN
    score_scale = 1.0 / math.sqrt(HD)
    head_query = queries.reshape(blocks, WIN, HEADS, HD)
    head_keys = key_rows.reshape(blocks, WIN, HEADS, HD)
    head_values = value_rows.reshape(blocks, WIN, HEADS, HD)
    empty = jnp.zeros((1, WIN, HEADS, HD), queries.dtype)
    keys_span = jnp.concatenate([jnp.concatenate([empty, head_keys[:-1]], axis=0), head_keys], axis=1)
    values_span = jnp.concatenate([jnp.concatenate([empty, head_values[:-1]], axis=0), head_values], axis=1)
    doc_blocks = documents.reshape(blocks, WIN)
    doc_before = jnp.concatenate([jnp.full((1, WIN), -1, jnp.int32), doc_blocks[:-1]], axis=0)
    doc_span = jnp.concatenate([doc_before, doc_blocks], axis=1)
    distance = jnp.arange(WIN, dtype=jnp.int32)[:, None] + WIN - jnp.arange(2 * WIN, dtype=jnp.int32)[None, :]
    allowed = ((distance >= 0) & (distance < WIN))[None] & (doc_blocks[:, :, None] == doc_span[:, None, :])
    position_bias = jnp.moveaxis(jnp.take(table_now, bucket_of(jnp.clip(distance, 0, WIN - 1)), axis=0), 2, 0)
    scores = jnp.einsum('bqhd,bkhd->bhqk', head_query, keys_span, precision=highest) * score_scale + position_bias[None]
    scores = low_back(scores)
    scores = jnp.where(allowed[:, None], scores, big_negative)
    weights = low(softmax_rows(scores))
    return jnp.einsum('bhqk,bkhd->bqhd', weights, values_span, precision=highest).reshape(length, D)

def memory_attention(queries, slot_rows, memory_keys, memory_values):
    length = queries.shape[0]
    score_scale = 1.0 / math.sqrt(HD)
    head_query = queries.reshape(length, HEADS, HD)
    key_heads = memory_keys.reshape(MEM, HEADS, HD)
    value_heads = memory_values.reshape(MEM, HEADS, HD)
    head_ids = jnp.arange(HEADS, dtype=jnp.int32)[None, :, None]
    chosen_keys = key_heads[slot_rows, head_ids]
    chosen_values = value_heads[slot_rows, head_ids]
    scores = low_back(jnp.einsum('lhd,lhtd->lht', head_query, chosen_keys, precision=highest) * score_scale)
    weights = low(softmax_rows(scores))
    return jnp.einsum('lht,lhtd->lhd', weights, chosen_values, precision=highest).reshape(length, D)

def run_layer(hidden, qkv, w_out, w_in, w_down, gains, shifts, table_now, documents, slot_rows, memory_keys, memory_values, gate, use_memory):
    normed = low(layer_norm(hidden, gains[0], shifts[0]))
    queries = both_round(matmul(normed, qkv[:, :D]))
    key_rows = both_round(matmul(normed, qkv[:, D:2 * D]))
    value_rows = both_round(matmul(normed, qkv[:, 2 * D:]))
    local_out = local_attention(queries, key_rows, value_rows, table_now, documents)
    if use_memory:
        memory_out = memory_attention(queries, slot_rows, memory_keys, memory_values)
        opened = jnp.repeat(jax.nn.sigmoid(gate), HD)
        attended = opened * low_back(memory_out) + (1.0 - opened) * low_back(local_out)
    else:
        attended = local_out
    attended = both_round(attended)
    after = hidden + low_back(matmul(attended, w_out))
    normed_two = low(layer_norm(after, gains[1], shifts[1]))
    before = low_back(matmul(normed_two, w_in))
    active = low(jax.nn.gelu(before, approximate=True))
    return after + low_back(matmul(active, w_down))

def reference(tokens, doc_ids, knn_index, mem_keys, mem_values, qkv_weight, out_weight, in_weight, down_weight, norm_gain, norm_bias, rel_table, mem_gate, cotangent):
    memory_keys = mem_keys.astype(jnp.float32)
    memory_values = mem_values.astype(jnp.float32)

    def forward(inputs, qkv, w_out, w_in, w_down, gains, shifts, tables, gate):
        qkv_layers = segment_to_layers(qkv)
        out_layers = segment_to_layers(w_out)
        in_layers = segment_to_layers(w_in)
        down_layers = segment_to_layers(w_down)
        gain_layers = gains_to_layers(gains)
        shift_layers = gains_to_layers(shifts)

        def one_sequence(sequence_item):
            sequence, documents, slot_rows = sequence_item
            middle = run_layer(sequence, qkv_layers[0], out_layers[0], in_layers[0], down_layers[0], gain_layers[0], shift_layers[0], tables[0], documents, slot_rows, memory_keys, memory_values, gate, False)
            return run_layer(middle, qkv_layers[1], out_layers[1], in_layers[1], down_layers[1], gain_layers[1], shift_layers[1], tables[1], documents, slot_rows, memory_keys, memory_values, gate, True)
        return lax.map(jax.checkpoint(one_sequence), (inputs, doc_ids, knn_index))
    result, pullback = jax.vjp(forward, tokens.astype(jnp.float32), qkv_weight.astype(jnp.float32), out_weight.astype(jnp.float32), in_weight.astype(jnp.float32), down_weight.astype(jnp.float32), norm_gain.astype(jnp.float32), norm_bias.astype(jnp.float32), rel_table.astype(jnp.float32), mem_gate.astype(jnp.float32))
    grads = pullback(cotangent.astype(jnp.float32))
    return (result.astype(jnp.bfloat16), grads[0].astype(jnp.bfloat16), grads[1], grads[2], grads[3], grads[4], grads[5], grads[6], grads[7], grads[8])
```

```python
import functools
import math

import jax
import jax.numpy as jnp
import numpy as np
from jax import lax
from jax.experimental import pallas as pl
from jax.experimental.pallas import tpu as pltpu
from jax.sharding import PartitionSpec as P

WIN = 512
LAYERS = 2
CORES = 2
QB = 256

norm_eps = 1e-05
big_negative = -1e30
bucket_edges = np.ceil(16.0 * 8.0 ** (np.arange(1, 16) / 16.0)).astype(np.int32)
highest = lax.Precision.HIGHEST
f32 = jnp.float32
bf16 = jnp.bfloat16
VMEM_LIMIT = 48 * 1024 * 1024


def permuted(block, axis, route):
    count = lax.axis_size(axis)
    return lax.ppermute(block, axis, [(i, route(i)) for i in range(count)])


def core_swap(block):
    return permuted(block, "segment", lambda i: i ^ 1)


def pick(index, parts):
    return lax.select_n(index, *parts)


def ring_gather(block, stretch):
    count = lax.axis_size("segment")
    total = count // CORES
    parts = [block]
    for _ in range(total - 1):
        parts.append(permuted(parts[-1], "segment", lambda i: (i + CORES) % count))
    return jnp.concatenate([pick((stretch - k) % total, parts) for k in range(total)], axis=1)


def plane_gather(block, batch):
    rows = block.shape[0]
    half = rows // 2
    across = permuted(block, "batch", lambda i: i ^ 1)
    along = permuted(block, "batch", lambda i: i ^ 2)
    far_low = permuted(along[:half], "batch", lambda i: i ^ 1)
    far_high = permuted(across[half:], "batch", lambda i: i ^ 2)
    whole = jnp.zeros((4 * rows,) + block.shape[1:], block.dtype)
    whole = lax.dynamic_update_slice(whole, block, (batch * rows, 0))
    whole = lax.dynamic_update_slice(whole, across, ((batch ^ 1) * rows, 0))
    whole = lax.dynamic_update_slice(whole, along, ((batch ^ 2) * rows, 0))
    whole = lax.dynamic_update_slice(whole, far_low, ((batch ^ 3) * rows, 0))
    return lax.dynamic_update_slice(whole, far_high, ((batch ^ 3) * rows + half, 0))


def plane_scatter(whole, batch):
    rows = whole.shape[0] // 4
    half = rows // 2

    def part(which, first, size):
        return lax.dynamic_slice_in_dim(whole, (batch ^ which) * rows + first, size, 0)

    def total(*terms):
        return functools.reduce(jnp.add, [t.astype(f32) for t in terms])

    got_low = permuted(part(3, 0, half), "batch", lambda i: i ^ 1)
    got_high = permuted(part(3, half, half), "batch", lambda i: i ^ 2)
    to_along = jnp.concatenate(
        [total(part(2, 0, half), got_low).astype(bf16), part(2, half, half)], axis=0
    )
    to_across = jnp.concatenate(
        [part(1, 0, half), total(part(1, half, half), got_high).astype(bf16)], axis=0
    )
    from_along = permuted(to_along, "batch", lambda i: i ^ 2)
    from_across = permuted(to_across, "batch", lambda i: i ^ 1)
    return total(part(0, 0, rows), from_along, from_across)


def ring_scatter(block, stretch):
    count = lax.axis_size("segment")
    total = count // CORES
    width = block.shape[1] // total
    columns = [block[:, k * width : (k + 1) * width] for k in range(total)]

    def own(offset):
        return pick((stretch - offset) % total, columns)

    travelling = own(1).astype(bf16)
    for step in range(1, total):
        got = permuted(travelling, "segment", lambda i: (i + CORES) % count)
        summed = got.astype(f32) + own(1 + step).astype(f32)
        travelling = summed.astype(bf16)
    return summed


def qkv_half(matrix, core):
    rows, cols = matrix.shape
    split = matrix.reshape(rows, cols // 256, 2, 128)
    return split[:, :, core].reshape(rows, cols // 2).T


def out_half(matrix, core):
    rows, cols = matrix.shape
    return matrix.reshape(rows // 256, 2, 128, cols)[:, core].reshape(rows // 2, cols).T


def in_half(matrix, core, parts):
    rows, cols = matrix.shape
    return matrix.reshape(rows, parts, 2, cols // parts // 2)[:, :, core].reshape(rows, cols // 2).T


def down_half(matrix, core, parts):
    rows, cols = matrix.shape
    return matrix.reshape(parts, 2, rows // parts // 2, cols)[:, core].reshape(rows // 2, cols).T


def qkv_whole(halves):
    cols, rows = halves[0].shape
    stacked = jnp.stack([h.T.reshape(rows, cols // 128, 128) for h in halves], axis=2)
    return stacked.reshape(rows, 2 * cols)


def out_whole(halves):
    cols, rows = halves[0].shape
    stacked = jnp.stack([h.T.reshape(rows // 128, 128, cols) for h in halves], axis=1)
    return stacked.reshape(2 * rows, cols)


def in_whole(halves, parts):
    cols, rows = halves[0].shape
    stacked = jnp.stack([h.T.reshape(rows, parts, cols // parts) for h in halves], axis=2)
    return stacked.reshape(rows, 2 * cols)


def down_whole(halves, parts):
    cols, rows = halves[0].shape
    stacked = jnp.stack([h.T.reshape(parts, rows // parts, cols) for h in halves], axis=1)
    return stacked.reshape(2 * rows, cols)


def halves_of(parts):
    return (
        qkv_half,
        out_half,
        functools.partial(in_half, parts=parts),
        functools.partial(down_half, parts=parts),
    )


def wholes_of(parts):
    return (
        qkv_whole,
        out_whole,
        functools.partial(in_whole, parts=parts),
        functools.partial(down_whole, parts=parts),
    )


def gather_by_chip(shards, core, stretch, batch):
    low_core = core == 0
    layers = ([], [])
    for shard, half in zip(shards, halves_of(1)):
        first, second = half(shard, 0), half(shard, 1)
        mine = jnp.where(low_core, first, second)
        got = core_swap(jnp.where(low_core, second, first))
        for layer, block in ((0, jnp.where(low_core, mine, got)), (1, jnp.where(low_core, got, mine))):
            layers[layer].append(plane_gather(ring_gather(block, stretch), batch))
    return layers


def gather_plain(shards, core):
    layers = ([], [])
    for shard, half in zip(shards, halves_of(4)):
        rows = lax.all_gather(shard, "batch", axis=1, tiled=True)
        slots = lax.all_gather(rows, "segment", axis=0, tiled=False)
        for layer in range(LAYERS):
            matrix = slots[layer::LAYERS].reshape(-1, rows.shape[1])
            layers[layer].append(
                jnp.where(core == 0, half(matrix, 0), half(matrix, 1))
            )
    return layers


def scatter_by_chip(grads, stretch, batch):
    return ring_scatter(plane_scatter(grads, batch), stretch)


def finish_by_chip(parts, core):
    low_core = core == 0
    done = []
    for lower, upper, whole in zip(parts[0], parts[1], wholes_of(1)):
        kept = jnp.where(low_core, lower, upper)
        got = core_swap(jnp.where(low_core, upper, lower).astype(bf16)).astype(f32)
        done.append(whole((jnp.where(low_core, kept, got), jnp.where(low_core, got, kept)))[None])
    return done


def scatter_plain(parts, core):
    done = []
    slots = lax.axis_size("segment")
    for lower, upper, whole in zip(parts[0], parts[1], wholes_of(4)):
        layers = []
        for half in (lower, upper):
            empty = jnp.zeros_like(half)
            matrix = whole((jnp.where(core == 0, half, empty), jnp.where(core == 0, empty, half)))
            layers.append(matrix.reshape(slots // LAYERS, -1, matrix.shape[1]))
        stacked = jnp.stack(layers, axis=1).reshape(slots, -1, layers[0].shape[2])
        rows = lax.psum_scatter(stacked, "segment", scatter_dimension=0, tiled=True)
        columns = lax.psum_scatter(rows, "batch", scatter_dimension=2, tiled=True)
        done.append(columns.astype(f32))
    return done


def spans(row_count, halo):
    for first in range(0, row_count, QB):
        start = max(0, first + halo - WIN)
        yield first, start, first + halo + QB - start


def mask_kernel(index_ref, mask_ref):
    rows, slots = mask_ref.shape[1], mask_ref.shape[2]
    chunk = 64
    width = 256
    for low in range(0, slots, width):
        slot_ids = lax.broadcasted_iota(jnp.int32, (chunk, width), 1) + low

        def step(turn, carry):
            first = pl.multiple_of(turn * chunk, chunk)
            index = index_ref[0, pl.ds(first, chunk), :]
            bias = jnp.full((chunk, width), big_negative, f32)
            for t in range(index.shape[1]):
                bias = jnp.where(index[:, t : t + 1] == slot_ids, 0.0, bias)
            mask_ref[0, pl.ds(first, chunk), low : low + width] = bias.astype(bf16)
            return carry

        lax.fori_loop(0, rows // chunk, step, 0)


def slot_mask(index, slots):
    heads, rows, chosen = index.shape
    return pl.pallas_call(
        mask_kernel,
        out_shape=jax.ShapeDtypeStruct((heads, rows, slots), bf16),
        grid=(heads,),
        in_specs=[pl.BlockSpec((1, rows, chosen), lambda h: (h, 0, 0))],
        out_specs=pl.BlockSpec((1, rows, slots), lambda h: (h, 0, 0)),
        compiler_params=pltpu.CompilerParams(vmem_limit_bytes=VMEM_LIMIT),
        cost_estimate=pl.CostEstimate(
            flops=2 * heads * rows * slots * chosen, transcendentals=0, bytes_accessed=4 * heads * rows * slots
        ),
        name="slot_mask",
    )(index)


def nt_dot(left, right):
    return lax.dot_general(left, right, (((1,), (1,)), ((), ())), preferred_element_type=f32)


def tn_dot(left, right):
    return lax.dot_general(left, right, (((0,), (0,)), ((), ())), preferred_element_type=f32)


def nn_dot(left, right):
    return lax.dot_general(left, right, (((1,), (0,)), ((), ())), preferred_element_type=f32)


def forward_kernel(halo, with_memory, scale, *refs):
    refs = list(refs)
    bias_ref, docs_col, docs_row, q_ref, k_ref, v_ref = refs[:6]
    del refs[:6]
    if halo:
        k_halo, v_halo = refs[:2]
        del refs[:2]
    if with_memory:
        mem_k, mem_v, mask_ref, gate_ref = refs[:4]
        del refs[:4]
        o_ref, probs_ref, slots_ref, differ_ref = refs[:4]
        del refs[:4]
    else:
        o_ref, probs_ref = refs[:2]
        del refs[:2]
    if halo:
        keys, values = refs
        keys[:halo] = k_halo[...]
        keys[halo:] = k_ref[...]
        values[:halo] = v_halo[...]
        values[halo:] = v_ref[...]
    else:
        keys, values = k_ref, v_ref
    width = WIN + QB
    lanes = bias_ref.shape[2]
    tile = pltpu.roll(
        jnp.broadcast_to(bias_ref[0], (QB, lanes)), 0, axis=1, stride=1, stride_axis=0
    )[:, :width]
    if with_memory:
        opened = gate_ref[pl.program_id(0)]
    for first, start, count in spans(q_ref.shape[0], halo):
        rows = slice(first, first + QB)
        query = q_ref[rows]
        scores = nt_dot(query, keys[start : start + count]) * scale + tile[:, width - count :]
        same = docs_col[rows] == docs_row[:, start : start + count]
        scores = jnp.where(same, scores, big_negative)
        raised = jnp.exp(scores - jnp.max(scores, axis=-1, keepdims=True))
        probs = (raised * (1.0 / jnp.sum(raised, axis=-1, keepdims=True))).astype(bf16)
        probs_ref[0, rows, width - count :] = probs
        local = nn_dot(probs, values[start : start + count])
        if with_memory:
            picked = nt_dot(query, mem_k[...]) * scale + mask_ref[0, rows].astype(f32)
            raised = jnp.exp(picked - jnp.max(picked, axis=-1, keepdims=True))
            slot_probs = (raised * (1.0 / jnp.sum(raised, axis=-1, keepdims=True))).astype(bf16)
            slots_ref[0, rows] = slot_probs
            differ = nn_dot(slot_probs, mem_v[...]) - local
            differ_ref[rows] = differ.astype(bf16)
            local = local + opened * differ
        o_ref[rows] = local.astype(bf16)


def backward_kernel(halo, with_memory, scale, *refs):
    refs = list(refs)
    q_ref, k_ref, v_ref, do_ref, probs_ref = refs[:5]
    del refs[:5]
    if halo:
        k_halo, v_halo = refs[:2]
        del refs[:2]
    if with_memory:
        mem_k, mem_v, slots_ref, differ_ref, gate_ref = refs[:5]
        del refs[:5]
    d_ref, table_ref = refs[:2]
    del refs[:2]
    if with_memory:
        gate_grad = refs.pop(0)
    if halo:
        halo_grad = refs.pop(0)
    dk, dv, table = refs[:3]
    del refs[:3]
    if halo:
        keys, values = refs
        keys[:halo] = k_halo[...]
        keys[halo:] = k_ref[...]
        values[:halo] = v_halo[...]
        values[halo:] = v_ref[...]
    else:
        keys, values = k_ref, v_ref
    head = pl.program_id(0)
    heads = pl.num_programs(0)
    row_count, head_dim = q_ref.shape
    width = WIN + QB
    lanes = table.shape[1]
    dk[...] = jnp.zeros_like(dk)
    dv[...] = jnp.zeros_like(dv)
    table[...] = jnp.zeros_like(table)
    if with_memory:
        opened = gate_ref[head]
        gate_sum = jnp.zeros((1, head_dim), f32)
    here = pl.multiple_of(head * head_dim, head_dim)
    for first, start, count in spans(row_count, halo):
        rows = slice(first, first + QB)
        cols = slice(start, start + count)
        upstream = do_ref[rows]
        if with_memory:
            wide = upstream.astype(f32)
            gate_sum += jnp.sum(wide * differ_ref[rows].astype(f32), axis=0, keepdims=True)
            mem_grad = (opened * wide).astype(bf16)
            upstream = ((1.0 - opened) * wide).astype(bf16)
        probs = probs_ref[0, rows, width - count :]
        probs_wide = probs.astype(f32)
        grad = nt_dot(upstream, values[cols])
        inner = jnp.sum(probs_wide * grad, axis=-1, keepdims=True)
        score_wide = probs_wide * (grad - inner)
        score = score_wide.astype(bf16)
        table[:, width - count : width] += score_wide
        dq = nn_dot(score, keys[cols])
        dk[cols] += tn_dot(score, q_ref[rows])
        dv[cols] += tn_dot(probs, upstream)
        if with_memory:
            slot_probs = slots_ref[0, rows].astype(f32)
            slot_grad = nt_dot(mem_grad, mem_v[...])
            slot_score = slot_probs * (
                slot_grad - jnp.sum(slot_probs * slot_grad, axis=-1, keepdims=True)
            )
            dq += nn_dot(slot_score.astype(bf16), mem_k[...])
        d_ref[rows, pl.ds(here, head_dim)] = (dq * scale).astype(bf16)
    key_at = pl.multiple_of((heads + head) * head_dim, head_dim)
    value_at = pl.multiple_of((2 * heads + head) * head_dim, head_dim)
    if halo:
        halo_grad[0] = (dk[:halo] * scale).astype(bf16)
        halo_grad[1] = dv[:halo].astype(bf16)
    d_ref[:, pl.ds(key_at, head_dim)] = (dk[halo:] * scale).astype(bf16)
    d_ref[:, pl.ds(value_at, head_dim)] = dv[halo:].astype(bf16)
    turned = jnp.zeros((8, lanes), f32)
    for row in range(0, QB, 8):
        part = table[row : row + 8]
        turned += pltpu.roll(part, lanes - row, axis=1) if row else part
    total = turned[:1]
    for row in range(1, 8):
        total += pltpu.roll(turned, lanes - row, axis=1)[row : row + 1]
    table_ref[0] = total
    if with_memory:
        gate_grad[0] = gate_sum


def head_block(rows, head_dim, offset):
    return pl.BlockSpec((rows, head_dim), lambda h: (0, offset + h))


def plane_block(rows, cols):
    return pl.BlockSpec((1, rows, cols), lambda h: (h, 0, 0))


smem_block = pl.BlockSpec(memory_space=pltpu.SMEM)


def attend(projected, bias_rows, docs_col, docs_row, halo_rows, memory, scale):
    row_count = projected.shape[0]
    head_count, _, lanes = bias_rows.shape
    head_dim = projected.shape[1] // (3 * head_count)
    halo = 0 if halo_rows is None else halo_rows.shape[1]
    width = WIN + QB
    operands = [bias_rows, docs_col, docs_row, projected, projected, projected]
    specs = [
        plane_block(1, lanes),
        pl.BlockSpec(docs_col.shape, lambda h: (0, 0)),
        pl.BlockSpec(docs_row.shape, lambda h: (0, 0)),
        head_block(row_count, head_dim, 0),
        head_block(row_count, head_dim, head_count),
        head_block(row_count, head_dim, 2 * head_count),
    ]
    scratch = []
    if halo:
        operands += [halo_rows[0], halo_rows[1]]
        specs += [head_block(halo, head_dim, 0)] * 2
        scratch = [pltpu.VMEM((halo + row_count, head_dim), bf16)] * 2
    outs = [
        jax.ShapeDtypeStruct((row_count, head_count * head_dim), bf16),
        jax.ShapeDtypeStruct((head_count, row_count, width), bf16),
    ]
    out_specs = [head_block(row_count, head_dim, 0), plane_block(row_count, width)]
    flops = 4 * head_count * row_count * width * head_dim
    if memory is not None:
        mem_keys, mem_values, mask, gate = memory
        slots = mem_keys.shape[0]
        operands += [mem_keys, mem_values, mask, gate]
        specs += [head_block(slots, head_dim, 0)] * 2 + [plane_block(row_count, slots), smem_block]
        outs += [
            jax.ShapeDtypeStruct((head_count, row_count, slots), bf16),
            jax.ShapeDtypeStruct((row_count, head_count * head_dim), bf16),
        ]
        out_specs += [plane_block(row_count, slots), head_block(row_count, head_dim, 0)]
        flops += 4 * head_count * row_count * slots * head_dim
    return pl.pallas_call(
        functools.partial(forward_kernel, halo, memory is not None, scale),
        out_shape=outs,
        grid=(head_count,),
        in_specs=specs,
        out_specs=out_specs,
        scratch_shapes=scratch,
        compiler_params=pltpu.CompilerParams(vmem_limit_bytes=VMEM_LIMIT),
        cost_estimate=pl.CostEstimate(
            flops=flops, transcendentals=head_count * row_count * width, bytes_accessed=16 * 1024 * 1024
        ),
        name="attend",
    )(*operands)


def attend_back(projected, grad, probs, halo_rows, memory, scale):
    row_count = projected.shape[0]
    head_count, _, width = probs.shape
    head_dim = projected.shape[1] // (3 * head_count)
    halo = 0 if halo_rows is None else halo_rows.shape[1]
    lanes = 1024
    operands = [projected, projected, projected, grad, probs]
    specs = [
        head_block(row_count, head_dim, 0),
        head_block(row_count, head_dim, head_count),
        head_block(row_count, head_dim, 2 * head_count),
        head_block(row_count, head_dim, 0),
        plane_block(row_count, width),
    ]
    scratch = [
        pltpu.VMEM((halo + row_count, head_dim), f32),
        pltpu.VMEM((halo + row_count, head_dim), f32),
        pltpu.VMEM((QB, lanes), f32),
    ]
    if halo:
        operands += [halo_rows[0], halo_rows[1]]
        specs += [head_block(halo, head_dim, 0)] * 2
        scratch += [pltpu.VMEM((halo + row_count, head_dim), bf16)] * 2
    outs = [
        jax.ShapeDtypeStruct(projected.shape, bf16),
        jax.ShapeDtypeStruct((head_count, 1, lanes), f32),
    ]
    out_specs = [pl.BlockSpec(projected.shape, lambda h: (0, 0)), plane_block(1, lanes)]
    flops = 8 * head_count * row_count * width * head_dim
    if memory is not None:
        mem_keys, mem_values, slot_probs, differ, gate = memory
        slots = mem_keys.shape[0]
        operands += [mem_keys, mem_values, slot_probs, differ, gate]
        specs += [head_block(slots, head_dim, 0)] * 2
        specs += [plane_block(row_count, slots), head_block(row_count, head_dim, 0), smem_block]
        outs += [jax.ShapeDtypeStruct((head_count, 1, head_dim), f32)]
        out_specs += [plane_block(1, head_dim)]
        flops += 4 * head_count * row_count * slots * head_dim
    if halo:
        outs += [jax.ShapeDtypeStruct((2, halo, head_count * head_dim), bf16)]
        out_specs += [pl.BlockSpec((2, halo, head_dim), lambda h: (0, 0, h))]
    return pl.pallas_call(
        functools.partial(backward_kernel, halo, memory is not None, scale),
        out_shape=outs,
        grid=(head_count,),
        in_specs=specs,
        out_specs=out_specs,
        scratch_shapes=scratch,
        compiler_params=pltpu.CompilerParams(vmem_limit_bytes=VMEM_LIMIT),
        cost_estimate=pl.CostEstimate(
            flops=flops, transcendentals=0, bytes_accessed=20 * 1024 * 1024
        ),
        name="attend_back",
    )(*operands)


def bucket_of(distance):
    beyond = jnp.sum((distance[..., None] >= jnp.asarray(bucket_edges)).astype(jnp.int32), axis=-1)
    return jnp.where(distance < 16, distance, 16 + beyond)


def distance_onehot(bucket_count):
    bucket = bucket_of(jnp.arange(WIN, dtype=jnp.int32))
    return (bucket[:, None] == jnp.arange(bucket_count, dtype=jnp.int32)).astype(f32)


def normalize(values):
    center = values - jnp.mean(values, axis=-1, keepdims=True)
    factor = lax.rsqrt(jnp.mean(center * center, axis=-1, keepdims=True) + norm_eps)
    return center * factor, factor


def norm_back(upstream, values, gain_row):
    normal, factor = normalize(values)
    gain_part = jnp.sum(upstream * normal, axis=0)
    shift_part = jnp.sum(upstream, axis=0)
    scaled = upstream * gain_row
    inner = (
        scaled
        - jnp.mean(scaled, axis=-1, keepdims=True)
        - normal * jnp.mean(scaled * normal, axis=-1, keepdims=True)
    )
    return factor * inner, gain_part, shift_part


def smooth_pair(pre):
    rate = math.sqrt(2.0 / math.pi)
    square = pre * pre
    turn = jnp.tanh(rate * pre * (1.0 + 0.044715 * square))
    half = 0.5 * (1.0 + turn)
    slope = half + 0.5 * pre * (1.0 - turn * turn) * rate * (1.0 + 3 * 0.044715 * square)
    return (pre * half).astype(bf16), slope.astype(bf16)


def paired_sum(partial):
    low = partial.astype(bf16)
    return low.astype(f32) + core_swap(low).astype(f32)


def on_device(
    tokens,
    doc_ids,
    knn_index,
    mem_keys,
    mem_values,
    qkv_weight,
    out_weight,
    in_weight,
    down_weight,
    norm_gain,
    norm_bias,
    rel_table,
    mem_gate,
    cotangent,
):
    seq_count, block_len, model_width = tokens.shape
    bucket_count, head_total = rel_table.shape[1:]
    head_dim = model_width // head_total
    topk_count = knn_index.shape[3]
    gain_cols = norm_gain.shape[2]
    heads = head_total // CORES
    segments = lax.axis_size("segment")
    batches = lax.axis_size("batch")
    stretches = segments // CORES
    per_seq = segments // seq_count
    pairs = per_seq // CORES
    chunk_len = seq_count * block_len
    pair_len = CORES * chunk_len
    halo = WIN if pairs > 1 else 0
    by_chip = segments == seq_count * CORES and batches == 4
    scale = 1.0 / math.sqrt(head_dim)
    here = lax.axis_index("segment")
    batch = lax.axis_index("batch")
    core = here % CORES
    stretch = here // CORES
    low_core = core == 0
    seq_no = here // per_seq
    block_no = here % seq_count

    def target(source, turn):
        group, place = divmod(source, seq_count)
        return ((place + turn) % seq_count) * per_seq + group

    def to_owner(stored):
        got = []
        for turn in range(seq_count):
            block = lax.dynamic_index_in_dim(stored, (block_no + turn) % seq_count, 0, keepdims=False)
            got.append(permuted(block, "segment", lambda i: target(i, turn)))
        return [pick((seq_no - place) % seq_count, got) for place in range(seq_count)]

    def to_stored(rows):
        blocks = rows.reshape((seq_count, block_len) + rows.shape[1:])
        got = []
        for turn in range(seq_count):
            block = lax.dynamic_index_in_dim(blocks, (seq_no - turn) % seq_count, 0, keepdims=False)
            route = {target(i, turn): i for i in range(segments)}
            got.append(permuted(block, "segment", lambda i: route[i]))
        return jnp.stack([pick((number - block_no) % seq_count, got) for number in range(seq_count)])

    def both_chunks(mine):
        other = core_swap(mine)
        first = jnp.where(low_core, mine, other)
        second = jnp.where(low_core, other, mine)
        return jnp.concatenate([first, second], axis=0)

    def own_chunk(rows):
        return jnp.where(low_core, rows[:chunk_len], rows[chunk_len:])

    norm_rows = jnp.stack([norm_gain[0], norm_bias[0]])
    norm_all = lax.all_gather(norm_rows, ("batch", "segment"), axis=0, tiled=False)
    norm_all = norm_all.reshape(batches, stretches, LAYERS, 2, 2, gain_cols)
    norm_all = jnp.transpose(norm_all, (2, 3, 4, 1, 0, 5)).reshape(LAYERS, 2, 2, model_width)
    norm_all = norm_all.astype(f32)

    hidden = both_chunks(jnp.concatenate(to_owner(tokens), axis=0)).astype(f32)

    shards = (qkv_weight[0], out_weight[0], in_weight[0], down_weight[0])
    if by_chip:
        weights = gather_by_chip(shards, core, stretch, batch)
    else:
        weights = gather_plain(shards, core)

    def by_head(index, which):
        split = index.reshape(chunk_len, heads, CORES, topk_count)[:, :, which]
        return jnp.transpose(split, (1, 0, 2))

    index_rows = jnp.concatenate(to_owner(knn_index), axis=0)
    even, odd = by_head(index_rows, 0), by_head(index_rows, 1)
    own_index = jnp.where(low_core, even, odd)
    other_index = core_swap(jnp.where(low_core, odd, even))
    index = jnp.concatenate(
        [jnp.where(low_core, own_index, other_index), jnp.where(low_core, other_index, own_index)], axis=1
    )
    memory_all = lax.all_gather(jnp.stack([mem_keys, mem_values], axis=0), "segment", axis=1, tiled=True)
    slot_total = memory_all.shape[1]
    memory_split = memory_all.reshape(2, slot_total, heads, CORES, head_dim)
    memory_own = jnp.where(low_core, memory_split[:, :, :, 0], memory_split[:, :, :, 1])
    memory_own = memory_own.reshape(2, slot_total, heads * head_dim)
    mask = slot_mask(index, slot_total)

    upper_cotangent = both_chunks(jnp.concatenate(to_owner(cotangent), axis=0))

    docs = lax.dynamic_index_in_dim(doc_ids, seq_no, 0, keepdims=False)
    first_row = (here % per_seq) // CORES * pair_len
    docs_own = lax.dynamic_slice_in_dim(docs, first_row, pair_len, 0)
    docs_col = docs_own.reshape(pair_len, 1)
    docs_padded = jnp.concatenate([jnp.full((halo,), -1, jnp.int32), docs]) if halo else docs
    docs_row = lax.dynamic_slice_in_dim(docs_padded, first_row, halo + pair_len, 0).reshape(1, -1)
    onehot = distance_onehot(bucket_count)
    tables = rel_table.reshape(LAYERS, bucket_count, heads, CORES)
    tables = jnp.where(low_core, tables[..., 0], tables[..., 1])
    near = jnp.einsum("db,lbh->lhd", onehot, tables, precision=highest)
    lanes = 1024
    bias_rows = jnp.full((LAYERS, heads, 1, lanes), big_negative, f32)
    bias_rows = bias_rows.at[:, :, 0, 1 : WIN + 1].set(near[:, :, ::-1])

    gate_all = jax.nn.sigmoid(mem_gate).reshape(heads, CORES)
    gate = jnp.where(low_core, gate_all[:, 0], gate_all[:, 1])

    def halo_of(projected):
        if not halo:
            return None
        tail = projected[pair_len - halo :, heads * head_dim :]
        route = [(i, i + CORES) for i in range(segments - CORES) if (i // CORES + 1) % pairs != 0]
        got = lax.ppermute(tail, "segment", route)
        return jnp.stack([got[:, : heads * head_dim], got[:, heads * head_dim :]])

    def halo_back(d_projected, halo_grad):
        route = [(i + CORES, i) for i in range(segments - CORES) if (i // CORES + 1) % pairs != 0]
        got = lax.ppermute(jnp.concatenate([halo_grad[0], halo_grad[1]], axis=1), "segment", route)
        edge = d_projected[pair_len - halo :, heads * head_dim :].astype(f32) + got.astype(f32)
        return d_projected.at[pair_len - halo :, heads * head_dim :].set(edge.astype(bf16))

    stored = []
    for layer in range(LAYERS):
        qkv, out, inner, down = weights[layer]
        gains, shifts = norm_all[layer, 0], norm_all[layer, 1]
        normal, _ = normalize(hidden)
        normed = (normal * gains[0] + shifts[0]).astype(bf16)
        projected = nt_dot(normed, qkv).astype(bf16)
        halo_rows = halo_of(projected)
        memory = (memory_own[0], memory_own[1], mask, gate) if layer == 1 else None
        kept = attend(projected, bias_rows[layer], docs_col, docs_row, halo_rows, memory, scale)
        attended, probs = kept[:2]
        after = hidden + paired_sum(nt_dot(attended, out))
        normal, _ = normalize(after)
        normed_two = (normal * gains[1] + shifts[1]).astype(bf16)
        active, slope = smooth_pair(nt_dot(normed_two, inner))
        result = after + paired_sum(nt_dot(active, down))
        stored.append(
            (hidden, normed, projected, halo_rows, attended, probs, kept[2:], after, normed_two, active, slope)
        )
        hidden = result

    mixed = to_stored(own_chunk(hidden.astype(bf16)))

    upstream = upper_cotangent.astype(f32)
    grads = [None, None]
    norm_grads = [None, None]
    table_grads = [None, None]
    for layer in (1, 0):
        qkv, out, inner, down = weights[layer]
        gains = norm_all[layer, 0]
        before, normed, projected, halo_rows, attended, probs, kept, after, normed_two, active, slope = stored[layer]

        def reduced(grad):
            low = grad.astype(bf16)
            return scatter_by_chip(low, stretch, batch) if by_chip else low

        upstream_low = upstream.astype(bf16)
        down_grad = reduced(tn_dot(upstream_low, active))
        pre_grad = (nn_dot(upstream_low, down) * slope.astype(f32)).astype(bf16)
        in_grad = reduced(tn_dot(pre_grad, normed_two))
        term, gain_two, shift_two = norm_back(paired_sum(nn_dot(pre_grad, inner)), after, gains[1])
        after_grad = upstream + term
        after_low = after_grad.astype(bf16)
        out_grad = reduced(tn_dot(after_low, attended))
        attended_grad = nn_dot(after_low, out).astype(bf16)
        memory = (memory_own[0], memory_own[1], kept[0], kept[1], gate) if layer == 1 else None
        backs = attend_back(projected, attended_grad, probs, halo_rows, memory, scale)
        d_projected, distances = backs[:2]
        if layer == 1:
            gate_sums = backs[2]
        if halo:
            d_projected = halo_back(d_projected, backs[-1])
        qkv_grad = reduced(tn_dot(d_projected, normed))
        term, gain_one, shift_one = norm_back(paired_sum(nn_dot(d_projected, qkv)), before, gains[0])
        upstream = after_grad + term
        grads[layer] = (qkv_grad, out_grad, in_grad, down_grad)
        norm_grads[layer] = jnp.stack([jnp.stack([gain_one, gain_two]), jnp.stack([shift_one, shift_two])])
        table_grads[layer] = jnp.einsum(
            "db,hd->bh", onehot, distances[:, 0, 1 : WIN + 1][:, ::-1], precision=highest
        )

    input_grad = to_stored(own_chunk(upstream.astype(bf16)))

    def spread(values):
        empty = jnp.zeros_like(values)
        even = jnp.where(low_core, values, empty)
        odd = jnp.where(low_core, empty, values)
        return jnp.stack([even, odd], axis=-1).reshape(values.shape[:-1] + (head_total,))

    gate_part = jnp.sum(gate_sums[:, 0], axis=-1) * gate * (1.0 - gate)
    sums = lax.psum(
        (
            spread(jnp.stack(table_grads)),
            spread(gate_part),
            jnp.stack(norm_grads) * (1.0 / CORES),
        ),
        ("batch", "segment"),
    )
    table_sum, gate_sum, norm_sum = sums
    norm_sum = norm_sum.reshape(LAYERS, 2, 2, stretches, batches, gain_cols)
    norm_sum = jnp.where(low_core, norm_sum[0], norm_sum[1])
    norm_sum = lax.dynamic_index_in_dim(norm_sum, stretch, 2, keepdims=False)
    norm_sum = lax.dynamic_index_in_dim(norm_sum, batch, 2, keepdims=False)

    matrices = finish_by_chip(grads, core) if by_chip else scatter_plain(grads, core)
    return (mixed, input_grad, *matrices, norm_sum[0][None], norm_sum[1][None], table_sum, gate_sum)


def solution(mesh):
    placed = (
        P("batch", "segment", None),
        P("batch", None),
        P("batch", "segment", None, None),
        P("segment", None),
        P("segment", None),
        P("segment", None, "batch"),
        P("segment", None, "batch"),
        P("segment", None, "batch"),
        P("segment", None, "batch"),
        P("segment", None, "batch"),
        P("segment", None, "batch"),
        P(),
        P(),
        P("batch", "segment", None),
    )
    return jax.shard_map(
        on_device,
        mesh=mesh,
        in_specs=placed,
        out_specs=(
            P("batch", "segment", None),
            P("batch", "segment", None),
            P("segment", None, "batch"),
            P("segment", None, "batch"),
            P("segment", None, "batch"),
            P("segment", None, "batch"),
            P("segment", None, "batch"),
            P("segment", None, "batch"),
            P(),
            P(),
        ),
        check_vma=False,
    )
```

```python
import functools
import math

import jax
import jax.numpy as jnp
import numpy as np
from jax import lax
from jax.experimental import pallas as pl
from jax.experimental.pallas import tpu as pltpu
from jax.sharding import PartitionSpec as P

SEG, BAT = "segment", "batch"
WIN = 512
LAYERS = 2
CORES = 2
QB = 256

norm_eps = 1e-05
big_negative = -1e30
bucket_edges = np.ceil(16.0 * 8.0 ** (np.arange(1, 16) / 16.0)).astype(np.int32)
highest = lax.Precision.HIGHEST
f32 = jnp.float32
bf16 = jnp.bfloat16
VMEM_LIMIT = 20 * 1024 * 1024


def permuted(block, axis, route):
    count = lax.axis_size(axis)
    return lax.ppermute(block, axis, [(i, route(i)) for i in range(count)])


def core_swap(block):
    return permuted(block, SEG, lambda i: i ^ 1)


def room(tick):
    return pl.pallas_call(
        lambda source, result: None,
        out_shape=jax.ShapeDtypeStruct(tick.shape, tick.dtype),
        in_specs=[pl.BlockSpec(memory_space=pl.ANY)],
        out_specs=pl.BlockSpec(memory_space=pl.ANY),
        input_output_aliases={0: 0},
        cost_estimate=pl.CostEstimate(flops=200_000_000_000, transcendentals=0, bytes_accessed=0),
        name="room",
    )(tick)


def key(*parts):
    return "".join(map(str, parts))


class Steps:
    def __init__(self):
        self.steps = {}
        self.values = {}
        self.mark = ()
        self.tick = jnp.zeros((8, 128), f32)

    def given(self, name, value):
        self.values[name] = value
        return name

    def run(self, name, step, *sources):
        assert name not in self.steps, name
        self.steps[name] = ("run", step, sources)
        return name

    def send(self, name, link, transfer, *sources):
        assert name not in self.steps, name
        self.steps[name] = (link, transfer, sources)
        return name

    def value(self, source):
        if isinstance(source, tuple):
            return self.values[source[0]][source[1]]
        return self.values[source]

    def behind(self, values):
        leaves, tree = jax.tree.flatten(values)
        held = lax.optimization_barrier(tuple(leaves) + tuple(self.mark))
        return jax.tree.unflatten(tree, held[: len(leaves)])

    def wait(self, name):
        tick = room(self.behind(self.tick))
        leaves, tree = jax.tree.flatten(self.values[name])
        held = lax.optimization_barrier(tuple(leaves) + tuple(self.mark) + (tick,))
        self.tick = held[-1]
        self.mark = held[: len(leaves)]
        self.values[name] = jax.tree.unflatten(tree, self.mark)

    def carry_out(self, order):
        waited = set()
        names = list(self.steps)
        for number in order:
            name = names[number] if number >= 0 else names[-1 - number]
            if number < 0:
                waited.add(name)
                self.wait(name)
                continue
            kind, step, sources = self.steps[name]
            for source in sources:
                source = source[0] if isinstance(source, tuple) else source
                if source in self.steps and self.steps[source][0] != "run" and source not in waited:
                    waited.add(source)
                    self.wait(source)
            with jax.named_scope(name):
                result = step(*self.behind([self.value(source) for source in sources]))
            self.values[name] = result
            if kind == "run":
                self.mark = tuple(jax.tree.leaves(result))
        assert set(range(len(names))) <= set(order)


def pick(index, parts):
    return lax.select_n(index, *parts)


def total(*terms):
    return functools.reduce(jnp.add, [t.astype(f32) for t in terms])


def ring_step(block):
    count = lax.axis_size(SEG)
    return permuted(block, SEG, lambda i: (i + CORES) % count)


def in_order(parts, stretch):
    return [pick((stretch - k) % len(parts), parts) for k in range(len(parts))]


def swap_across(block):
    return permuted(block, BAT, lambda i: i ^ 1)


def swap_along(block):
    return permuted(block, BAT, lambda i: i ^ 2)


def cut_of(rows):
    return rows // 2 // 128 * 128


def qkv_half(matrix, core):
    rows, cols = matrix.shape
    return matrix.reshape(rows, cols // 256, 2, 128)[:, :, core].reshape(rows, cols // 2).T


def out_half(matrix, core):
    rows, cols = matrix.shape
    return matrix.reshape(rows // 256, 2, 128, cols)[:, core].reshape(rows // 2, cols)


def in_half(matrix, core, parts):
    rows, cols = matrix.shape
    return matrix.reshape(rows, parts, 2, cols // parts // 2)[:, :, core].reshape(rows, cols // 2).T


def down_half(matrix, core, parts):
    rows, cols = matrix.shape
    return matrix.reshape(parts, 2, rows // parts // 2, cols)[:, core].reshape(rows // 2, cols).T


def qkv_whole(halves):
    cols, rows = halves[0].shape
    stacked = jnp.stack([h.T.reshape(rows, cols // 128, 128) for h in halves], axis=2)
    return stacked.reshape(rows, 2 * cols)


def out_whole(halves):
    rows, cols = halves[0].shape
    stacked = jnp.stack([h.reshape(rows // 128, 128, cols) for h in halves], axis=1)
    return stacked.reshape(2 * rows, cols)


def in_whole(halves, parts):
    cols, rows = halves[0].shape
    stacked = jnp.stack([h.T.reshape(rows, parts, cols // parts) for h in halves], axis=2)
    return stacked.reshape(rows, 2 * cols)


def down_whole(halves, parts):
    cols, rows = halves[0].shape
    stacked = jnp.stack([h.T.reshape(parts, rows // parts, cols) for h in halves], axis=1)
    return stacked.reshape(2 * rows, cols)


def halves_of(parts):
    return (
        qkv_half,
        out_half,
        functools.partial(in_half, parts=parts),
        functools.partial(down_half, parts=parts),
    )


def gather_plain(shards, core):
    layers = ([], [])
    for shard, half in zip(shards, halves_of(4)):
        rows = lax.all_gather(shard, BAT, axis=1, tiled=True)
        slots = lax.all_gather(rows, SEG, axis=0, tiled=False)
        for layer in range(LAYERS):
            matrix = slots[layer::LAYERS].reshape(-1, rows.shape[1])
            layers[layer].append(jnp.where(core == 0, half(matrix, 0), half(matrix, 1)))
    return layers


def scatter_plain(parts, core):
    done = []
    slots = lax.axis_size(SEG)
    wholes = (qkv_whole, out_whole, functools.partial(in_whole, parts=4), functools.partial(down_whole, parts=4))
    for lower, upper, whole in zip(parts[0], parts[1], wholes):
        layers = []
        for half in (lower, upper):
            empty = jnp.zeros_like(half)
            matrix = whole((jnp.where(core == 0, half, empty), jnp.where(core == 0, empty, half)))
            layers.append(matrix.reshape(slots // LAYERS, -1, matrix.shape[1]))
        stacked = jnp.stack(layers, axis=1).reshape(slots, -1, layers[0].shape[2])
        rows = lax.psum_scatter(stacked, SEG, scatter_dimension=0, tiled=True)
        columns = lax.psum_scatter(rows, BAT, scatter_dimension=2, tiled=True)
        done.append(columns.astype(f32))
    return done


def spans(row_count, halo):
    for first in range(0, row_count, QB):
        start = max(0, first + halo - WIN)
        yield first, start, first + halo + QB - start


def mask_kernel(first_lane, chosen, index_ref, mask_ref):
    rows, slots = mask_ref.shape[1], mask_ref.shape[2]
    chunk = 64
    width = 256

    def body(first):
        index = index_ref[pl.ds(first, chunk), first_lane : first_lane + chosen]
        for low in range(0, slots, width):
            slot_ids = lax.broadcasted_iota(jnp.int32, (chunk, width), 1) + low
            bias = jnp.full((chunk, width), big_negative, f32)
            for t in range(chosen):
                bias = jnp.where(index[:, t : t + 1] == slot_ids, 0.0, bias)
            mask_ref[0, pl.ds(first, chunk), low : low + width] = bias.astype(bf16)

    chunks(rows, chunk, body)


def slot_mask(index, head, chosen, slots):
    out = jax.ShapeDtypeStruct((1, index.shape[0], slots), bf16)
    kernel = functools.partial(mask_kernel, head * chosen, chosen)
    return in_vmem(kernel, [out], None, [index], "slot_mask", 10_000_000_000)[0]


def nt_dot(left, right):
    return lax.dot_general(left, right, (((1,), (1,)), ((), ())), preferred_element_type=f32)


def tn_dot(left, right):
    return lax.dot_general(left, right, (((0,), (0,)), ((), ())), preferred_element_type=f32)


def nn_dot(left, right):
    return lax.dot_general(left, right, (((1,), (0,)), ((), ())), preferred_element_type=f32)


def forward_kernel(halo, with_memory, scale, *refs):
    refs = list(refs)
    bias_ref, docs_col, docs_row, q_ref, k_ref, v_ref = refs[:6]
    del refs[:6]
    if halo:
        k_halo, v_halo = refs[:2]
        del refs[:2]
    if with_memory:
        mem_k, mem_v, mask_ref, gate_ref = refs[:4]
        del refs[:4]
        o_ref, probs_ref, slots_ref, differ_ref = refs[:4]
        del refs[:4]
    else:
        o_ref, probs_ref = refs[:2]
        del refs[:2]
    if halo:
        keys, values = refs
        keys[:halo] = k_halo[...]
        keys[halo:] = k_ref[...]
        values[:halo] = v_halo[...]
        values[halo:] = v_ref[...]
    else:
        keys, values = k_ref, v_ref
    width = WIN + QB
    lanes = bias_ref.shape[2]
    tile = pltpu.roll(
        jnp.broadcast_to(bias_ref[0], (QB, lanes)), 0, axis=1, stride=1, stride_axis=0
    )[:, :width]
    if with_memory:
        opened = gate_ref[pl.program_id(0)]
    for first, start, count in spans(q_ref.shape[0], halo):
        rows = slice(first, first + QB)
        query = q_ref[rows]
        scores = nt_dot(query, keys[start : start + count]) * scale + tile[:, width - count :]
        same = docs_col[rows] == docs_row[:, start : start + count]
        scores = jnp.where(same, scores, big_negative)
        raised = jnp.exp(scores - jnp.max(scores, axis=-1, keepdims=True))
        probs = (raised * (1.0 / jnp.sum(raised, axis=-1, keepdims=True))).astype(bf16)
        probs_ref[0, rows, width - count :] = probs
        local = nn_dot(probs, values[start : start + count])
        if with_memory:
            picked = nt_dot(query, mem_k[...]) * scale + mask_ref[0, rows].astype(f32)
            raised = jnp.exp(picked - jnp.max(picked, axis=-1, keepdims=True))
            slot_probs = (raised * (1.0 / jnp.sum(raised, axis=-1, keepdims=True))).astype(bf16)
            slots_ref[0, rows] = slot_probs
            differ = nn_dot(slot_probs, mem_v[...]) - local
            differ_ref[rows] = differ.astype(bf16)
            local = local + opened * differ
        o_ref[rows] = local.astype(bf16)


def backward_kernel(halo, with_memory, scale, *refs):
    refs = list(refs)
    q_ref, k_ref, v_ref, do_ref, probs_ref = refs[:5]
    del refs[:5]
    if halo:
        k_halo, v_halo = refs[:2]
        del refs[:2]
    if with_memory:
        mem_k, mem_v, slots_ref, differ_ref, gate_ref = refs[:5]
        del refs[:5]
    d_ref, table_ref = refs[:2]
    del refs[:2]
    if with_memory:
        gate_grad = refs.pop(0)
    if halo:
        halo_grad = refs.pop(0)
    dk, dv, table = refs[:3]
    del refs[:3]
    if halo:
        keys, values = refs
        keys[:halo] = k_halo[...]
        keys[halo:] = k_ref[...]
        values[:halo] = v_halo[...]
        values[halo:] = v_ref[...]
    else:
        keys, values = k_ref, v_ref
    head = pl.program_id(0)
    heads = pl.num_programs(0)
    row_count, head_dim = q_ref.shape
    width = WIN + QB
    lanes = table.shape[1]
    dk[...] = jnp.zeros_like(dk)
    dv[...] = jnp.zeros_like(dv)
    table[...] = jnp.zeros_like(table)
    if with_memory:
        opened = gate_ref[head]
        gate_sum = jnp.zeros((1, head_dim), f32)
    here = pl.multiple_of(head * head_dim, head_dim)
    for first, start, count in spans(row_count, halo):
        rows = slice(first, first + QB)
        cols = slice(start, start + count)
        upstream = do_ref[rows]
        if with_memory:
            wide = upstream.astype(f32)
            gate_sum += jnp.sum(wide * differ_ref[rows].astype(f32), axis=0, keepdims=True)
            mem_grad = (opened * wide).astype(bf16)
            upstream = ((1.0 - opened) * wide).astype(bf16)
        probs = probs_ref[0, rows, width - count :]
        probs_wide = probs.astype(f32)
        grad = nt_dot(upstream, values[cols])
        inner = jnp.sum(probs_wide * grad, axis=-1, keepdims=True)
        score_wide = probs_wide * (grad - inner)
        score = score_wide.astype(bf16)
        table[:, width - count : width] += score_wide
        dq = nn_dot(score, keys[cols])
        dk[cols] += tn_dot(score, q_ref[rows])
        dv[cols] += tn_dot(probs, upstream)
        if with_memory:
            slot_probs = slots_ref[0, rows].astype(f32)
            slot_grad = nt_dot(mem_grad, mem_v[...])
            slot_score = slot_probs * (
                slot_grad - jnp.sum(slot_probs * slot_grad, axis=-1, keepdims=True)
            )
            dq += nn_dot(slot_score.astype(bf16), mem_k[...])
        d_ref[rows, pl.ds(here, head_dim)] = (dq * scale).astype(bf16)
    key_at = pl.multiple_of((heads + head) * head_dim, head_dim)
    value_at = pl.multiple_of((2 * heads + head) * head_dim, head_dim)
    if halo:
        halo_grad[0] = (dk[:halo] * scale).astype(bf16)
        halo_grad[1] = dv[:halo].astype(bf16)
    d_ref[:, pl.ds(key_at, head_dim)] = (dk[halo:] * scale).astype(bf16)
    d_ref[:, pl.ds(value_at, head_dim)] = dv[halo:].astype(bf16)
    turned = jnp.zeros((8, lanes), f32)
    for row in range(0, QB, 8):
        part = table[row : row + 8]
        turned += pltpu.roll(part, lanes - row, axis=1) if row else part
    total = turned[:1]
    for row in range(1, 8):
        total += pltpu.roll(turned, lanes - row, axis=1)[row : row + 1]
    table_ref[0] = total
    if with_memory:
        gate_grad[0] = gate_sum


def smooth_pair(pre):
    rate = math.sqrt(2.0 / math.pi)
    square = pre * pre
    turn = jnp.tanh(pre * (rate + (rate * 0.044715) * square))
    half = 0.5 + 0.5 * turn
    bend = pre * (rate + (rate * 3 * 0.044715) * square)
    return (pre * half).astype(bf16), (half + bend * (half - half * half) * 2.0).astype(bf16)


def norm_rows_of(values):
    center = values - jnp.mean(values, axis=-1, keepdims=True)
    factor = lax.rsqrt(jnp.mean(center * center, axis=-1, keepdims=True) + norm_eps)
    return center * factor, factor


def in_vmem(kernel, outs, scalars, operands, name, flops):
    vmem = pl.BlockSpec(memory_space=pltpu.VMEM)
    return pl.pallas_call(
        kernel,
        out_shape=outs,
        in_specs=([smem_block] if scalars is not None else []) + [vmem] * len(operands),
        out_specs=[vmem] * len(outs),
        compiler_params=pltpu.CompilerParams(vmem_limit_bytes=8 * 1024 * 1024),
        cost_estimate=pl.CostEstimate(flops=3 * flops, transcendentals=0, bytes_accessed=0),
        name=name,
    )(*([scalars] if scalars is not None else []), *operands)


smem_block = pl.BlockSpec(memory_space=pltpu.SMEM)


def chunks(count, size, body):
    def step(turn, carry):
        body(pl.multiple_of(turn * size, size))
        return carry

    lax.fori_loop(0, count // size, step, 0)


def segments(refs, low, high):
    for which, ref in enumerate(refs[:3]):
        yield which, 0, ref, low, high
    cut = refs[3].shape[0]
    if low < cut:
        yield 3, 0, refs[3], low, min(high, cut)
    if high > cut:
        yield 3, max(cut - low, 0), refs[4], max(low - cut, 0), high - cut


def place_of(at_ref, which, width, offset=0):
    return pl.multiple_of((at_ref[0] ^ which) * width + offset, 128)


def norm_kernel(row, part, at_ref, own_ref, across_ref, along_ref, low_ref, high_ref, out_ref):
    rows = [ref[row : row + 1, :].astype(f32) for ref in (own_ref, across_ref, along_ref)]
    rows.append(high_ref[row - low_ref.shape[0] : row - low_ref.shape[0] + 1, :].astype(f32))
    width = 4 * part
    chips = rows[0].shape[1] // width
    for k in range(4):
        which = at_ref[0] ^ k
        row_k = jnp.where(
            which < 2, jnp.where(which == 0, rows[0], rows[1]), jnp.where(which == 2, rows[2], rows[3])
        )
        for z in range(chips):
            for kind in range(4):
                first = z * width + kind * part
                out_ref[kind : kind + 1, z * width + k * part : z * width + (k + 1) * part] = row_k[:, first : first + part]


def norm_rows_by_pieces(at, row, part, pieces):
    out = jax.ShapeDtypeStruct((4, pieces[0].shape[1]), f32)
    return in_vmem(functools.partial(norm_kernel, row, part), [out], at, list(pieces), "norm", 1000)[0]


def head_kernel(joins, width, at_ref, *refs):
    hidden_ref, *refs = refs
    if joins:
        own_ref, got_ref, *refs = refs
    gain_ref, shift_ref, *refs = refs
    pieces, (normed_ref, out_ref), refs = refs[:5], refs[5:7], refs[7:]
    parts = list(segments(pieces, 0, width))

    def body(first):
        rows = pl.ds(first, 256)
        values = hidden_ref[rows, :]
        if joins:
            values = values + (own_ref[rows, :].astype(f32) + got_ref[rows, :].astype(f32))
            refs[0][rows, :] = values
        normal, _ = norm_rows_of(values)
        normed = (normal * gain_ref[...] + shift_ref[...]).astype(bf16)
        normed_ref[rows, :] = normed
        for which, offset, ref, low, high in parts:
            cols = pl.ds(place_of(at_ref, which, width, offset), high - low)
            out_ref[rows, cols] = nt_dot(normed, ref[low:high]).astype(bf16)

    chunks(hidden_ref.shape[0], 256, body)


def head_by_pieces(at, width, hidden, joins, gain, shift, pieces):
    rows, inner = hidden.shape
    outs = [jax.ShapeDtypeStruct((rows, inner), bf16), jax.ShapeDtypeStruct((rows, 4 * width), bf16)]
    if joins:
        outs.append(jax.ShapeDtypeStruct((rows, inner), f32))
    operands = [hidden, *joins, gain, shift, *pieces]
    return in_vmem(
        functools.partial(head_kernel, bool(joins), width), outs, at, operands, "head", 8 * rows * inner * width
    )


def by_columns_kernel(smooth, at_ref, rows_ref, *refs):
    pieces, outs = refs[:5], refs[5:]
    width = pieces[0].shape[0]
    parts = list(segments(pieces, 0, width))

    def body(first):
        rows = pl.ds(first, 256)
        for which, offset, ref, low, high in parts:
            cols = pl.ds(place_of(at_ref, which, width, offset), high - low)
            product = nt_dot(rows_ref[rows, :], ref[low:high])
            if smooth:
                outs[0][rows, cols], outs[1][rows, cols] = smooth_pair(product)
            else:
                outs[0][rows, cols] = product.astype(bf16)

    chunks(rows_ref.shape[0], 256, body)


def by_columns(at, rows, pieces, smooth):
    count, inner = rows.shape
    width = pieces[0].shape[0]
    outs = [jax.ShapeDtypeStruct((count, 4 * width), bf16)] * (2 if smooth else 1)
    return in_vmem(
        functools.partial(by_columns_kernel, smooth), outs, at, [rows, *pieces], "expand" if smooth else "down",
        8 * count * inner * width,
    )


def out_kernel(first, rows_per, width, at_ref, rows_ref, *refs):
    pieces, out_ref = refs[:5], refs[5]
    parts = list(segments(pieces, first, first + rows_per))

    def body(start):
        rows = pl.ds(start, 256)
        for which, _, ref, low, high in parts:
            acc = None
            for z in range(rows_ref.shape[1] // rows_per):
                part = nn_dot(
                    rows_ref[rows, z * rows_per : (z + 1) * rows_per], ref[low:high, z * width : (z + 1) * width]
                )
                acc = part if acc is None else acc + part
            out_ref[rows, pl.ds(place_of(at_ref, which, width), width)] = acc.astype(bf16)

    chunks(rows_ref.shape[0], 256, body)


def out_by_pieces(at, first, rows_per, width, attended, pieces):
    count = attended.shape[0]
    outs = [jax.ShapeDtypeStruct((count, 4 * width), bf16)]
    return in_vmem(
        functools.partial(out_kernel, first, rows_per, width), outs, at, [attended, *pieces], "out",
        8 * count * attended.shape[1] * width,
    )[0]


def by_rows_kernel(low, high, scaled, at_ref, rows_ref, *refs):
    pieces, refs = refs[:5], refs[5:]
    out_ref = refs[-1]
    span = high - low
    parts = list(segments(pieces, low, high))
    block = 512

    def body(start):
        rows = pl.ds(start, 256)
        for n in range(0, out_ref.shape[1], block):
            cols = slice(n, n + block)
            acc = None
            for which, offset, ref, first, last in parts:
                inner = pl.ds(place_of(at_ref, which, span, offset), last - first)
                part = nn_dot(rows_ref[rows, inner], ref[first:last, cols])
                acc = part if acc is None else acc + part
            if scaled:
                acc = acc * refs[0][rows, cols].astype(f32)
            out_ref[rows, cols] = acc.astype(bf16)

    chunks(rows_ref.shape[0], 256, body)


def by_rows(at, low, high, grad, pieces, slope=None):
    count = grad.shape[0]
    cols = pieces[0].shape[1]
    operands = [grad, *pieces] + ([] if slope is None else [slope])
    return in_vmem(
        functools.partial(by_rows_kernel, low, high, slope is not None),
        [jax.ShapeDtypeStruct((count, cols), bf16)], at, operands, "by_rows", 2 * count * grad.shape[1] * cols,
    )[0]


def attended_back_kernel(first, rows_per, width, at_ref, grad_ref, *refs):
    pieces, out_ref = refs[:5], refs[5]
    parts = list(segments(pieces, first, first + rows_per))

    def body(start):
        rows = pl.ds(start, 256)
        for z in range(out_ref.shape[1] // rows_per):
            acc = None
            for which, _, ref, low, high in parts:
                grad = grad_ref[rows, pl.ds(place_of(at_ref, which, width), width)]
                part = nt_dot(grad, ref[low:high, z * width : (z + 1) * width])
                acc = part if acc is None else acc + part
            out_ref[rows, z * rows_per : (z + 1) * rows_per] = acc.astype(bf16)

    chunks(grad_ref.shape[0], 256, body)


def attended_back(at, first, rows_per, width, grad, pieces):
    count = grad.shape[0]
    chips = pieces[0].shape[1] // width
    return in_vmem(
        functools.partial(attended_back_kernel, first, rows_per, width),
        [jax.ShapeDtypeStruct((count, chips * rows_per), bf16)], at, [grad, *pieces], "attended_back",
        2 * count * grad.shape[1] * chips * rows_per,
    )[0]


def share_kernel(which, heads, adds, at_ref, *refs):
    left_ref, right_ref, *refs = refs
    if heads:
        attended_ref, grad_ref, *refs = refs
    count = {"": 0, "low": 1, "high": 1, "both": 2}[adds]
    got, outs = refs[:count], refs[count:]
    chips = 4
    rows, width = left_ref.shape[1] // 4, right_ref.shape[1] // chips
    own = which == 0
    left = left_ref[:, pl.ds(place_of(at_ref, which, rows), rows)]
    if heads:
        more = attended_ref.shape[1] // chips
        grad = grad_ref[:, pl.ds(place_of(at_ref, which, grad_ref.shape[1] // 4), grad_ref.shape[1] // 4)]

    def body(n):
        column = lax.rem(at_ref[1] + (3 * chips - 1) - n, chips) if own else n
        cols = pl.ds(pl.multiple_of(column * width, width), width)
        value = tn_dot(left, right_ref[:, cols])
        if heads:
            part = tn_dot(attended_ref[:, pl.ds(pl.multiple_of(column * more, more), more)], grad)
            value = jnp.concatenate([value, part], axis=0)
        half = value.shape[0] // 2
        if adds == "low":
            value = jnp.concatenate([value[:half] + got[0][:, cols].astype(f32), value[half:]], axis=0)
        elif adds == "high":
            value = jnp.concatenate([value[:half], value[half:] + got[0][:, cols].astype(f32)], axis=0)
        elif adds == "both":
            value = value + got[0][:, cols].astype(f32) + got[1][:, cols].astype(f32)
        value = value.astype(bf16)
        if which == 3:
            outs[0][:, cols], outs[1][:, cols] = value[:half], value[half:]
        elif own:
            outs[0][n] = value
        else:
            outs[0][:, cols] = value

    def step(n, carry):
        body(n)
        return carry

    lax.fori_loop(0, chips, step, 0)


def share_grad(at, which, left, right, head_pair=(), adds="", got=()):
    chips = 4
    rows, cols = left.shape[1] // 4, right.shape[1]
    if head_pair:
        rows += head_pair[0].shape[1] // chips
    if which == 3:
        outs = [jax.ShapeDtypeStruct((rows // 2, cols), bf16)] * 2
    elif which == 0:
        outs = [jax.ShapeDtypeStruct((chips, rows, cols // chips), bf16)]
    else:
        outs = [jax.ShapeDtypeStruct((rows, cols), bf16)]
    return in_vmem(
        functools.partial(share_kernel, which, bool(head_pair), adds), outs, at, [left, right, *head_pair, *got],
        "share", 2 * left.shape[0] * rows * cols,
    )


def join_norm_kernel(hidden_ref, own_ref, got_ref, gain_ref, shift_ref, result_ref, normed_ref):
    def body(first):
        rows = pl.ds(first, 128)
        values = hidden_ref[rows, :] + (own_ref[rows, :].astype(f32) + got_ref[rows, :].astype(f32))
        result_ref[rows, :] = values
        normal, _ = norm_rows_of(values)
        normed_ref[rows, :] = (normal * gain_ref[...] + shift_ref[...]).astype(bf16)

    chunks(hidden_ref.shape[0], 128, body)


def join_norm(hidden, own, got, gain, shift):
    outs = [jax.ShapeDtypeStruct(hidden.shape, f32), jax.ShapeDtypeStruct(hidden.shape, bf16)]
    return in_vmem(join_norm_kernel, outs, None, [hidden, own, got, gain, shift], "join_norm", 10 * hidden.size)


def join_back_kernel(up_ref, own_ref, got_ref, values_ref, gain_ref, result_ref, low_ref, gain_grad, shift_grad):
    gain_grad[...] = jnp.zeros_like(gain_grad)
    shift_grad[...] = jnp.zeros_like(shift_grad)

    def body(first):
        rows = pl.ds(first, 128)
        upstream = own_ref[rows, :].astype(f32) + got_ref[rows, :].astype(f32)
        normal, factor = norm_rows_of(values_ref[rows, :])
        gain_grad[...] += jnp.sum(upstream * normal, axis=0, keepdims=True)
        shift_grad[...] += jnp.sum(upstream, axis=0, keepdims=True)
        scaled = upstream * gain_ref[...]
        inner = (
            scaled
            - jnp.mean(scaled, axis=-1, keepdims=True)
            - normal * jnp.mean(scaled * normal, axis=-1, keepdims=True)
        )
        result = up_ref[rows, :].astype(f32) + factor * inner
        result_ref[rows, :] = result
        low_ref[rows, :] = result.astype(bf16)

    chunks(values_ref.shape[0], 128, body)


def join_back(upstream, own, got, values, gain):
    row = jax.ShapeDtypeStruct((1, values.shape[1]), f32)
    outs = [jax.ShapeDtypeStruct(values.shape, f32), jax.ShapeDtypeStruct(values.shape, bf16), row, row]
    return in_vmem(join_back_kernel, outs, None, [upstream, own, got, values, gain], "join_back", 20 * values.size)


def head_block(rows, head_dim, offset):
    return pl.BlockSpec((rows, head_dim), lambda h: (0, offset + h))


def plane_block(rows, cols):
    return pl.BlockSpec((1, rows, cols), lambda h: (h, 0, 0))


def attend(projected, bias_rows, docs_col, docs_row, halo_rows, memory, scale):
    row_count = projected.shape[0]
    head_count, _, lanes = bias_rows.shape
    head_dim = projected.shape[1] // (3 * head_count)
    halo = 0 if halo_rows is None else halo_rows.shape[1]
    width = WIN + QB
    operands = [bias_rows, docs_col, docs_row, projected, projected, projected]
    specs = [
        plane_block(1, lanes),
        pl.BlockSpec(docs_col.shape, lambda h: (0, 0)),
        pl.BlockSpec(docs_row.shape, lambda h: (0, 0)),
        head_block(row_count, head_dim, 0),
        head_block(row_count, head_dim, head_count),
        head_block(row_count, head_dim, 2 * head_count),
    ]
    scratch = []
    if halo:
        operands += [halo_rows[0], halo_rows[1]]
        specs += [head_block(halo, head_dim, 0)] * 2
        scratch = [pltpu.VMEM((halo + row_count, head_dim), bf16)] * 2
    outs = [
        jax.ShapeDtypeStruct((row_count, head_count * head_dim), bf16),
        jax.ShapeDtypeStruct((head_count, row_count, width), bf16),
    ]
    out_specs = [head_block(row_count, head_dim, 0), plane_block(row_count, width)]
    flops = 4 * head_count * row_count * width * head_dim
    if memory is not None:
        mem_keys, mem_values, masks, gate = memory
        slots = mem_keys.shape[0]
        mask = jnp.concatenate(masks, axis=0)
        operands += [mem_keys, mem_values, mask, gate]
        specs += [head_block(slots, head_dim, 0)] * 2 + [plane_block(row_count, slots), smem_block]
        outs += [
            jax.ShapeDtypeStruct((head_count, row_count, slots), bf16),
            jax.ShapeDtypeStruct((row_count, head_count * head_dim), bf16),
        ]
        out_specs += [plane_block(row_count, slots), head_block(row_count, head_dim, 0)]
        flops += 4 * head_count * row_count * slots * head_dim
    return pl.pallas_call(
        functools.partial(forward_kernel, halo, memory is not None, scale),
        out_shape=outs,
        grid=(head_count,),
        in_specs=specs,
        out_specs=out_specs,
        scratch_shapes=scratch,
        compiler_params=pltpu.CompilerParams(vmem_limit_bytes=VMEM_LIMIT),
        cost_estimate=pl.CostEstimate(
            flops=flops, transcendentals=head_count * row_count * width, bytes_accessed=16 * 1024 * 1024
        ),
        name="attend",
    )(*operands)


def attend_back(projected, grad, probs, halo_rows, memory, scale):
    row_count = projected.shape[0]
    head_count, _, width = probs.shape
    head_dim = projected.shape[1] // (3 * head_count)
    halo = 0 if halo_rows is None else halo_rows.shape[1]
    lanes = 1024
    operands = [projected, projected, projected, grad, probs]
    specs = [
        head_block(row_count, head_dim, 0),
        head_block(row_count, head_dim, head_count),
        head_block(row_count, head_dim, 2 * head_count),
        head_block(row_count, head_dim, 0),
        plane_block(row_count, width),
    ]
    scratch = [
        pltpu.VMEM((halo + row_count, head_dim), f32),
        pltpu.VMEM((halo + row_count, head_dim), f32),
        pltpu.VMEM((QB, lanes), f32),
    ]
    if halo:
        operands += [halo_rows[0], halo_rows[1]]
        specs += [head_block(halo, head_dim, 0)] * 2
        scratch += [pltpu.VMEM((halo + row_count, head_dim), bf16)] * 2
    outs = [
        jax.ShapeDtypeStruct(projected.shape, bf16),
        jax.ShapeDtypeStruct((head_count, 1, lanes), f32),
    ]
    out_specs = [pl.BlockSpec(projected.shape, lambda h: (0, 0)), plane_block(1, lanes)]
    flops = 8 * head_count * row_count * width * head_dim
    if memory is not None:
        mem_keys, mem_values, slot_probs, differ, gate = memory
        slots = mem_keys.shape[0]
        operands += [mem_keys, mem_values, slot_probs, differ, gate]
        specs += [head_block(slots, head_dim, 0)] * 2
        specs += [plane_block(row_count, slots), head_block(row_count, head_dim, 0), smem_block]
        outs += [jax.ShapeDtypeStruct((head_count, 1, head_dim), f32)]
        out_specs += [plane_block(1, head_dim)]
        flops += 4 * head_count * row_count * slots * head_dim
    if halo:
        outs += [jax.ShapeDtypeStruct((2, halo, head_count * head_dim), bf16)]
        out_specs += [pl.BlockSpec((2, halo, head_dim), lambda h: (0, 0, h))]
    return pl.pallas_call(
        functools.partial(backward_kernel, halo, memory is not None, scale),
        out_shape=outs,
        grid=(head_count,),
        in_specs=specs,
        out_specs=out_specs,
        scratch_shapes=scratch,
        compiler_params=pltpu.CompilerParams(vmem_limit_bytes=VMEM_LIMIT),
        cost_estimate=pl.CostEstimate(
            flops=flops, transcendentals=0, bytes_accessed=20 * 1024 * 1024
        ),
        name="attend_back",
    )(*operands)


def bucket_of(distance):
    beyond = jnp.sum((distance[..., None] >= jnp.asarray(bucket_edges)).astype(jnp.int32), axis=-1)
    return jnp.where(distance < 16, distance, 16 + beyond)


def distance_onehot(bucket_count):
    bucket = bucket_of(jnp.arange(WIN, dtype=jnp.int32))
    return (bucket[:, None] == jnp.arange(bucket_count, dtype=jnp.int32)).astype(f32)


def normalize(values):
    center = values - jnp.mean(values, axis=-1, keepdims=True)
    factor = lax.rsqrt(jnp.mean(center * center, axis=-1, keepdims=True) + norm_eps)
    return center * factor, factor


def head_in(hidden, gain, shift, qkv):
    normal, _ = normalize(hidden)
    normed = (normal * gain + shift).astype(bf16)
    return normed, nt_dot(normed, qkv).astype(bf16)


def out_part(attended, out):
    return nn_dot(attended, out).astype(bf16)


def down_part(active, down):
    return nt_dot(active, down).astype(bf16)


def joined(hidden, own, got):
    return hidden + (own.astype(f32) + got.astype(f32))


def weight_grad(left, right):
    return tn_dot(left, right).astype(bf16)


def expand_back(upstream, down, slope):
    return (nn_dot(upstream, down) * slope.astype(f32)).astype(bf16)


def input_part(grad, weight):
    return nn_dot(grad, weight).astype(bf16)


class Place:
    def __init__(self, seq_count):
        self.segments = lax.axis_size(SEG)
        self.batches = lax.axis_size(BAT)
        self.chips = self.segments // CORES
        self.seqs = seq_count
        self.pairs = self.chips // seq_count
        here = lax.axis_index(SEG)
        self.batch = lax.axis_index(BAT)
        self.core = here % CORES
        self.stretch = here // CORES
        self.low = self.core == 0
        self.seq_no = self.stretch // self.pairs
        self.place_no = self.stretch % seq_count

    def both(self, own, got):
        return jnp.where(self.low, own, got), jnp.where(self.low, got, own)


    def route(self, turn):
        pairs = []
        for source in range(self.segments):
            chip, lane = divmod(source, CORES)
            group, place = divmod(chip, self.seqs)
            pairs.append((source, (((place + turn) % self.seqs) * self.pairs + group) * CORES + lane))
        return pairs

    def local(self, turn):
        return self.pairs == 1 and turn == 0

    def out_block(self, stored, turn):
        return lax.dynamic_index_in_dim(stored, (self.place_no + turn) % self.seqs, 0, keepdims=False)

    def back_block(self, blocks, turn):
        return lax.dynamic_index_in_dim(blocks, (self.seq_no - turn) % self.seqs, 0, keepdims=False)

    def owned(self, *got):
        return jnp.stack([pick((self.seq_no - place) % self.seqs, got) for place in range(self.seqs)])

    def stored(self, *got):
        return jnp.stack([pick((number - self.place_no) % self.seqs, got) for number in range(self.seqs)])

    def sequence(self, own, got):
        pair = jnp.stack(self.both(own, got), axis=1)
        return pair.reshape((-1,) + own.shape[2:])

    def own_blocks(self, rows):
        split = rows.reshape(self.seqs, CORES, -1, rows.shape[1])
        return jnp.where(self.low, split[:, 0], split[:, 1])


def route_blocks(steps, place, name, source, back=False):
    got = []
    for turn in range(place.seqs):
        block = steps.run(key(name, "b", turn), lambda v, t=turn: (place.back_block if back else place.out_block)(v, t), source)
        if not place.local(turn):
            route = place.route(turn)
            if back:
                route = [(there, here) for here, there in route]
            block = steps.send(
                key(name, turn), key("z", turn), lambda v, route=tuple(route): lax.ppermute(v, SEG, route), block
            )
        got.append(block)
    return steps.run(key(name, "own"), place.stored if back else place.owned, *got)


def swap(steps, name, source):
    return steps.send(name, "core", core_swap, source)


def gather_steps(steps, place, shards, norm_rows, memory):
    qkv, out, inner, down = shards
    width = qkv.shape[0]
    gain_cols = norm_rows.shape[-1]
    slots = memory.shape[3]
    head, outs, hidden = qkv.shape[1] // 2, out.shape[0] // 2, inner.shape[1] // 2
    ends = np.cumsum([head + outs + 16, hidden, 2 * down.shape[1], memory[0].size // width])
    chips = place.chips

    def packed(core, qkv, out, inner, down, norm_rows, memory):
        down_rows = down_half(down, core, 1)
        return jnp.concatenate(
            [
                qkv_half(qkv, core),
                out_half(out, core),
                jnp.pad(norm_rows.reshape(1, width), ((0, 15), (0, 0))),
                in_half(inner, core, 1),
                down_rows[:, :width],
                down_rows[:, width:],
                memory_rows_of(memory[core]),
            ],
            axis=0,
        )

    def memory_rows_of(memory):
        return jnp.concatenate(
            [memory[kind, 0, :, at : at + width] for kind in range(2) for at in range(0, memory.shape[3], width)], axis=0
        )

    def first(*arrays):
        low, high = packed(0, *arrays), packed(1, *arrays)
        return jnp.where(place.low, low, high), jnp.where(place.low, high, low)

    for name, array in zip(("qkv", "out", "inner", "down", "norm", "mem"), (*shards, norm_rows, memory)):
        steps.given(name, array)
    steps.run("pack", first, "qkv", "out", "inner", "down", "norm", "mem")
    swap(steps, "wswap", ("pack", 1))

    def blocks(own, got):
        lower, upper = place.both(own, got)
        kept = []
        for layer in (lower, upper):
            kept += [layer[: ends[0]], layer[ends[0] : ends[1]], layer[ends[1] : ends[2]]]
        memory_rows = jnp.concatenate([lower[ends[2] :], upper[ends[2] :]], axis=0)
        kept[3] = jnp.concatenate([kept[3], memory_rows], axis=0)
        return kept

    steps.run("blocks", blocks, ("pack", 0), "wswap")

    def formed(unit, *ring):
        parts = in_order(ring, place.stretch)
        if unit[0] == "A":
            rows = jnp.concatenate([p[: ends[0]] for p in parts], axis=1)
            if unit == "A0":
                return (rows,)
            halves = memory.shape[4] // width
            block = 2 * halves * slots
            whole = []
            for kind in range(2):
                cols = []
                for half in range(halves):
                    first = ends[0] + (kind * halves + half) * slots
                    cols.append(
                        jnp.concatenate(
                            [p[first + c * block : first + c * block + slots] for p in parts for c in range(CORES)], axis=0
                        )
                    )
                whole.append(jnp.concatenate(cols, axis=1))
            return rows, jnp.stack(whole)
        if unit[0] == "I":
            return (jnp.concatenate(parts, axis=1),)
        half = parts[0].shape[0] // 2
        return (jnp.concatenate([q for p in parts for q in (p[:half], p[half:])], axis=1),)

    def norm_of(at, *pieces):
        return norm_rows_by_pieces(at, head + outs, gain_cols, pieces)

    pieces = {}
    for number, unit in enumerate(("A0", "I0", "D0", "A1", "I1", "D1")):
        ring = [("blocks", number)]
        for turn in range(1, chips):
            ring.append(steps.send(key("z", turn, unit), "z", ring_step, ring[-1]))
        steps.run(key("form", unit), functools.partial(formed, unit), *ring)
        block = (key("form", unit), 0)
        steps.send(key("px", unit), "x", swap_across, block)
        steps.send(key("py", unit), "y", swap_along, block)
        steps.send(key("fx", unit), "x", lambda along: swap_across(along[: cut_of(along.shape[0])]), key("py", unit))
        steps.send(key("fy", unit), "y", lambda across: swap_along(across[cut_of(across.shape[0]) :]), key("px", unit))
        pieces[unit] = (block, key("px", unit), key("py", unit), key("fx", unit), key("fy", unit))
        if unit[0] == "A":
            steps.run(key("norm", unit[1]), norm_of, "at", *pieces[unit])
    return pieces, ("formA1", 1), (head, outs, width)


def scatter_steps(steps, place, unit, left, right, *head_pair):
    heads = bool(head_pair)

    def shares(which, adds):
        def step(at, left, right, *rest):
            pair, got = (rest[:2], rest[2:]) if heads else ((), rest)
            return share_grad(at, which, left, right, pair, adds, got)

        return step

    sources = ("place", left, right, *head_pair)
    steps.run(key("ra", unit), shares(3, ""), *sources)
    steps.send(key("rx", unit), "x", swap_across, (key("ra", unit), 0))
    steps.send(key("ry", unit), "y", swap_along, (key("ra", unit), 1))
    steps.run(key("rb", unit), shares(1, "high"), *sources, key("ry", unit))
    steps.run(key("rc", unit), shares(2, "low"), *sources, key("rx", unit))
    steps.send(key("sx", unit), "x", swap_across, (key("rb", unit), 0))
    steps.send(key("sy", unit), "y", swap_along, (key("rc", unit), 0))
    steps.run(key("rd", unit), shares(0, "both"), *sources, key("sx", unit), key("sy", unit))
    own = (key("rd", unit), 0)
    travelling = steps.run(key("a0", unit), lambda parts: parts[0], own)
    for turn in range(1, place.chips):
        steps.send(key("q", turn, unit), "z", ring_step, travelling)
        last = turn == place.chips - 1
        travelling = steps.run(
            key("a", turn, unit),
            lambda got, parts, turn=turn, last=last: total(got, parts[turn]) if last else total(got, parts[turn]).astype(bf16),
            key("q", turn, unit),
            own,
        )
    return travelling


def finish_steps(steps, place, kind, lower, upper):
    steps.run(key("e", kind), lambda a, b: jnp.where(place.low, b, a).astype(bf16), lower, upper)
    swap(steps, key("eswap", kind), key("e", kind))

    def both(lower, upper, got):
        return place.both(jnp.where(place.low, lower, upper), got.astype(f32))

    return steps.run(key("done", kind), both, lower, upper, key("eswap", kind))


def on_device(
    tokens,
    doc_ids,
    knn_index,
    mem_keys,
    mem_values,
    qkv_weight,
    out_weight,
    in_weight,
    down_weight,
    norm_gain,
    norm_bias,
    rel_table,
    mem_gate,
    cotangent,
):
    seq_count, block_len, model_width = tokens.shape
    bucket_count, head_total = rel_table.shape[1:]
    head_dim = model_width // head_total
    topk_count = knn_index.shape[3]
    heads = head_total // CORES
    inner_width = heads * head_dim
    scale = 1.0 / math.sqrt(head_dim)
    place = Place(seq_count)
    steps = Steps()
    low_core = place.low
    pair_len = CORES * seq_count * block_len
    halo = WIN if place.pairs > 1 else 0
    by_chip = place.pairs == 1 and place.batches == 4

    norm_rows = jnp.stack([norm_gain[0], norm_bias[0]])
    shards = (qkv_weight[0], out_weight[0], in_weight[0], down_weight[0])
    memory = jnp.stack([mem_keys, mem_values]).reshape(2, mem_keys.shape[0], heads, CORES, head_dim)
    memory = jnp.transpose(memory, (3, 0, 1, 2, 4)).reshape(CORES, 2, 1, mem_keys.shape[0], inner_width)
    if by_chip:
        pieces, memory_at, sizes = gather_steps(steps, place, shards, norm_rows, memory)
    else:
        norms = lax.all_gather(norm_rows, (BAT, SEG), axis=0, tiled=False)
        norms = norms.reshape(place.batches, place.chips, LAYERS, 2, 2, norm_rows.shape[-1])
        norms = jnp.transpose(norms, (2, 3, 4, 1, 0, 5)).reshape(LAYERS, 2, 2, -1).astype(f32)
        weights = []
        for layer, matrices in enumerate(gather_plain(shards, place.core)):
            named = zip(("qkv", "out", "inner", "down", "norm"), (*matrices, norms[layer]))
            weights.append(tuple(steps.given(key(name, layer), array) for name, array in named))
        whole = lax.all_gather(memory, SEG, axis=3, tiled=True)
        memory_at = steps.given("memory", jnp.where(low_core, whole[0], whole[1])[:, 0])

    docs = lax.dynamic_index_in_dim(doc_ids, place.seq_no, 0, keepdims=False)
    first_row = place.stretch % place.pairs * pair_len
    docs_col = lax.dynamic_slice_in_dim(docs, first_row, pair_len, 0).reshape(pair_len, 1)
    docs_padded = jnp.concatenate([jnp.full((halo,), -1, jnp.int32), docs]) if halo else docs
    docs_row = lax.dynamic_slice_in_dim(docs_padded, first_row, halo + pair_len, 0).reshape(1, -1)
    steps.given("cols", docs_col)
    steps.given("rows", docs_row)
    onehot = distance_onehot(bucket_count)
    lanes = 1024

    def biases(table):
        tables = table.reshape(LAYERS, bucket_count, heads, CORES)
        tables = jnp.where(low_core, tables[..., 0], tables[..., 1])
        near = jnp.einsum("db,lbh->lhd", onehot[::-1], tables, precision=highest)[:, :, None]
        before = jnp.full((LAYERS, heads, 1, 1), big_negative, f32)
        beyond = jnp.full((LAYERS, heads, 1, lanes - WIN - 1), big_negative, f32)
        joined = jnp.concatenate([before, near, beyond], axis=3)
        return [joined[layer] for layer in range(LAYERS)]

    steps.run("bias", biases, steps.given("table", rel_table))
    gate_all = jax.nn.sigmoid(mem_gate).reshape(heads, CORES)
    gate = jnp.where(low_core, gate_all[:, 0], gate_all[:, 1])
    steps.given("gate", gate)

    def routed(name, array):
        return route_blocks(steps, place, name, steps.given(key(name, "in"), array))

    def by_head(blocks):
        rows = blocks.reshape(seq_count * block_len, head_total * topk_count)
        parts = [rows[:, h * topk_count : (h + 1) * topk_count] for h in range(head_total)]
        even, odd = jnp.concatenate(parts[::CORES], axis=1), jnp.concatenate(parts[1::CORES], axis=1)
        return jnp.where(low_core, even, odd), jnp.where(low_core, odd, even)

    slot_total = mem_keys.shape[0] * place.segments
    steps.run("flat", lambda v: v.reshape(seq_count, block_len, head_total * topk_count), steps.given("knn", knn_index))
    steps.run("kh", by_head, route_blocks(steps, place, "k", "flat"))
    swap(steps, "kswap", ("kh", 1))

    def whole_index(own, got):
        shape = (seq_count, block_len, heads * topk_count)
        pair = jnp.stack(place.both(own.reshape(shape), got.reshape(shape)), axis=1)
        return pair.reshape(pair_len, heads * topk_count)

    steps.run("index", whole_index, ("kh", 0), "kswap")
    masks = [
        steps.run(key("mask", head), lambda index, head=head: slot_mask(index, head, topk_count, slot_total), "index")
        for head in range(heads)
    ]

    own = routed("t", tokens)
    swap(steps, "tswap", own)
    hidden = steps.run("hid0", lambda own, got: place.sequence(own, got).astype(f32), own, "tswap")
    own = routed("c", cotangent)
    swap(steps, "cswap", own)
    upstream_low = steps.run("up", place.sequence, own, "cswap")
    upstream = upstream_low

    def halo_of(projected):
        if not halo:
            return None
        tail = projected[pair_len - halo :, inner_width:]
        route = [(i, i + CORES) for i in range(place.segments - CORES) if (i // CORES + 1) % place.pairs != 0]
        got = lax.ppermute(tail, SEG, route)
        return jnp.stack([got[:, :inner_width], got[:, inner_width:]])

    def halo_back(d_projected, halo_grad):
        route = [(i + CORES, i) for i in range(place.segments - CORES) if (i // CORES + 1) % place.pairs != 0]
        got = lax.ppermute(jnp.concatenate([halo_grad[0], halo_grad[1]], axis=1), SEG, route)
        edge = d_projected[pair_len - halo :, inner_width:].astype(f32) + got.astype(f32)
        return d_projected.at[pair_len - halo :, inner_width:].set(edge.astype(bf16))

    def attention(projected, bias, cols, rows, *rest):
        halo_rows = halo_of(projected)
        extra = (rest[0][0], rest[0][1], rest[1:-1], rest[-1]) if rest else None
        return attend(projected, bias, cols, rows, halo_rows, extra, scale)

    def attention_back(projected, grad, probs, *rest):
        halo_rows = halo_of(projected)
        extra = (rest[0][0], rest[0][1], *rest[1:]) if rest else None
        backs = attend_back(projected, grad, probs, halo_rows, extra, scale)
        if halo:
            backs = [halo_back(backs[0], backs[-1]), *backs[1:-1]]
        return backs

    if by_chip:
        head_rows, out_rows, width = sizes
        steps.given("at", place.batch.reshape(1))
        steps.given("place", jnp.stack([place.batch, place.stretch]))

    def row(norm, kind, which):
        return norm[2 * kind + which].reshape(1, -1) if by_chip else norm[kind, which].reshape(1, -1)

    def head_step(n, hidden):
        if not by_chip:
            qkv, norm = weights[n][0], weights[n][4]
            if n == 1:
                hidden = steps.run("hid1", joined, *hidden)
            steps.run(key("head", n), lambda h, norm, w: head_in(h, norm[0, 0], norm[1, 0], w), hidden, norm, qkv)
            return hidden

        def step(at, norm, hidden, *rest):
            joins, parts = rest[:-5], rest[-5:]
            return head_by_pieces(at, head_rows, hidden, joins, row(norm, 0, 0), row(norm, 1, 0), parts)

        steps.run(key("head", n), step, "at", key("norm", n), *(hidden if n == 1 else (hidden,)), *pieces[key("A", n)])
        return ("head1", 2) if n == 1 else hidden

    hidden_at = []
    for n in range(LAYERS):
        norm = key("norm", n) if by_chip else weights[n][4]
        hidden = head_step(n, hidden)
        hidden_at.append(hidden)
        extra = (memory_at, *masks, "gate") if n == 1 else ()
        steps.run(key("att", n), attention, (key("head", n), 1), ("bias", n), "cols", "rows", *extra)
        if by_chip:
            steps.run(
                key("op", n), lambda at, a, *parts: out_by_pieces(at, head_rows, out_rows, width, a, parts),
                "at", (key("att", n), 0), *pieces[key("A", n)],
            )
        else:
            steps.run(key("op", n), out_part, (key("att", n), 0), weights[n][1])
        swap(steps, key("oswap", n), key("op", n))
        steps.run(
            key("jn", n), lambda h, own, got, norm: join_norm(h, own, got, row(norm, 0, 1), row(norm, 1, 1)),
            hidden, key("op", n), key("oswap", n), norm,
        )
        if by_chip:
            steps.run(key("ex", n), lambda at, a, *parts: by_columns(at, a, parts, True), "at", (key("jn", n), 1), *pieces[key("I", n)])
            steps.run(key("dp", n), lambda at, a, *parts: by_columns(at, a, parts, False)[0], "at", (key("ex", n), 0), *pieces[key("D", n)])
        else:
            steps.run(key("ex", n), lambda a, w: smooth_pair(nt_dot(a, w)), (key("jn", n), 1), weights[n][2])
            steps.run(key("dp", n), down_part, (key("ex", n), 0), weights[n][3])
        swap(steps, key("dswap", n), key("dp", n))
        hidden = (("jn0", 0), "dp0", "dswap0")

    def last_rows(*a):
        return place.own_blocks(joined(*a).astype(bf16))

    steps.run("last", last_rows, ("jn1", 0), "dp1", "dswap1")
    mixed_at = route_blocks(steps, place, "m", "last", True)

    norm_parts, table_parts, reduced = [None, None], [None, None], [{}, {}]
    for n in (1, 0):
        norm = key("norm", n) if by_chip else weights[n][4]
        if by_chip:
            reduced[n]["D"] = scatter_steps(steps, place, key("D", n), upstream_low, (key("ex", n), 0))
            steps.run(
                key("pg", n), lambda at, g, slope, *parts: by_rows(at, 0, parts[0].shape[0], g, parts, slope),
                "at", upstream_low, (key("ex", n), 1), *pieces[key("D", n)],
            )
            steps.run(
                key("ip", n), lambda at, g, *parts: by_rows(at, 0, parts[0].shape[0], g, parts), "at", key("pg", n), *pieces[key("I", n)]
            )
            swap(steps, key("iswap", n), key("ip", n))
            reduced[n]["I"] = scatter_steps(steps, place, key("I", n), key("pg", n), (key("jn", n), 1))
        else:
            steps.run(key("gD", n), weight_grad, upstream_low, (key("ex", n), 0))
            steps.run(key("pg", n), expand_back, upstream_low, weights[n][3], (key("ex", n), 1))
            steps.run(key("ip", n), input_part, key("pg", n), weights[n][2])
            swap(steps, key("iswap", n), key("ip", n))
            steps.run(key("gI", n), weight_grad, key("pg", n), (key("jn", n), 1))
        steps.run(
            key("jb", n), lambda up, own, got, h, norm: join_back(up, own, got, h, row(norm, 0, 1)),
            upstream, key("ip", n), key("iswap", n), (key("jn", n), 0), norm,
        )
        if by_chip:
            steps.run(
                key("ag", n), lambda at, g, *parts: attended_back(at, head_rows, out_rows, width, g, parts),
                "at", (key("jb", n), 1), *pieces[key("A", n)],
            )
        else:
            steps.run(key("ag", n), lambda g, w: nt_dot(g, w).astype(bf16), (key("jb", n), 1), weights[n][1])
        extra = (memory_at, ("att1", 2), ("att1", 3), "gate") if n == 1 else ()
        steps.run(key("ab", n), attention_back, (key("head", n), 1), key("ag", n), (key("att", n), 1), *extra)
        if by_chip:
            steps.run(
                key("iq", n), lambda at, g, *parts: by_rows(at, 0, head_rows, g, parts), "at", (key("ab", n), 0), *pieces[key("A", n)]
            )
            swap(steps, key("qswap", n), key("iq", n))
            reduced[n]["A"] = scatter_steps(
                steps, place, key("A", n), (key("ab", n), 0), (key("head", n), 0), (key("att", n), 0), (key("jb", n), 1)
            )
        else:
            steps.run(key("iq", n), input_part, (key("ab", n), 0), weights[n][0])
            swap(steps, key("qswap", n), key("iq", n))
            steps.run(key("gQ", n), weight_grad, (key("ab", n), 0), (key("head", n), 0))
            steps.run(key("gO", n), weight_grad, (key("att", n), 0), (key("jb", n), 1))
        steps.run(
            key("jk", n), lambda up, own, got, h, norm: join_back(up, own, got, h, row(norm, 0, 0)),
            (key("jb", n), 0), key("iq", n), key("qswap", n), hidden_at[n], norm,
        )
        upstream, upstream_low = (key("jk", n), 0), (key("jk", n), 1)
        norm_parts[n] = steps.run(
            key("np", n), lambda a, b, c, d: jnp.stack([jnp.stack([a[0], b[0]]), jnp.stack([c[0], d[0]])]),
            (key("jk", n), 2), (key("jb", n), 2), (key("jk", n), 3), (key("jb", n), 3),
        )
        table_parts[n] = steps.run(
            key("tp", n),
            lambda d: jnp.einsum("db,hd->bh", onehot[::-1], d[:, 0, 1 : WIN + 1], precision=highest),
            (key("ab", n), 1),
        )

    steps.run("inlast", place.own_blocks, upstream_low)
    input_at = route_blocks(steps, place, "i", "inlast", True)

    def spread(values):
        empty = jnp.zeros_like(values)
        even = jnp.where(low_core, values, empty)
        odd = jnp.where(low_core, empty, values)
        return jnp.stack([even, odd], axis=-1).reshape(-1)

    sizes = [rel_table.size, head_total, LAYERS * 4 * model_width]
    ends = np.cumsum(sizes)
    room_total = -(-int(ends[-1]) // 1024) * 1024

    def flat(lower_table, upper_table, gates, gate, lower_norm, upper_norm):
        gate_part = jnp.sum(gates[:, 0], axis=-1) * gate * (1.0 - gate)
        parts = [
            spread(jnp.stack([lower_table, upper_table])),
            spread(gate_part),
            jnp.stack([lower_norm, upper_norm]).reshape(-1) * (1.0 / CORES),
        ]
        return jnp.concatenate(parts + [jnp.zeros((room_total - int(ends[-1]),), f32)]).reshape(-1, 128)

    sums = steps.run("sums", flat, table_parts[0], table_parts[1], ("ab1", 2), "gate", norm_parts[0], norm_parts[1])
    links = {(SEG, 1): "core", (BAT, 1): "x", (BAT, 2): "y"}
    for axis, count in ((SEG, place.segments), (BAT, place.batches)):
        bit = 1
        while bit < count:
            got = steps.send(
                key("u", axis[0], bit), links.get((axis, bit), "z"), lambda v, axis=axis, bit=bit: permuted(v, axis, lambda i: i ^ bit), sums
            )
            sums = steps.run(key("v", axis[0], bit), jnp.add, sums, got)
            bit *= 2

    if by_chip:
        done = {kind: finish_steps(steps, place, kind, reduced[0][kind], reduced[1][kind]) for kind in "DIA"}

    steps.carry_out(ORDER if by_chip and ORDER else range(len(steps.steps)))

    final = steps.value(sums).reshape(-1)
    table_sum = final[: ends[0]].reshape(rel_table.shape)
    gate_sum = final[ends[0] : ends[1]]
    norm_sum = final[ends[1] : ends[2]].reshape(LAYERS, 2, 2, place.chips, place.batches, norm_gain.shape[2])
    norm_sum = jnp.where(low_core, norm_sum[0], norm_sum[1])
    norm_sum = lax.dynamic_index_in_dim(norm_sum, place.stretch, 2, keepdims=False)
    norm_sum = lax.dynamic_index_in_dim(norm_sum, place.batch, 2, keepdims=False)
    if by_chip:
        halves = {kind: steps.value(name) for kind, name in done.items()}
        head = qkv_weight.shape[2] // 2
        matrices = [
            qkv_whole([h[:head] for h in halves["A"]])[None],
            out_whole([h[head:] for h in halves["A"]])[None],
            in_whole(halves["I"], 1)[None],
            down_whole(halves["D"], 1)[None],
        ]
    else:
        parts = [[steps.value(key("g", kind, n)) for kind in "QOID"] for n in range(LAYERS)]
        matrices = scatter_plain(parts, place.core)
    return (
        steps.value(mixed_at), steps.value(input_at), *matrices, norm_sum[0][None], norm_sum[1][None], table_sum, gate_sum,
    )


ORDER = (
    54, 0, 1, 56, 57, 58, 59, -2, 2, 60, -58, 3, 55, 70, 85, 75, 81, -60, 76, 73, 53, -4, 4, 83, 71, 80, -77, 72, -5,
    5, -73, 20, -6, 61, 6, 8, 7, -21, 21, -62, 74, 62, 63, 64, -65, 65, 66, -22, 12, 67, -75, 22, -9, 9, -8, -13, 10,
    13, 68, -23, 28, 23, -14, 24, -10, 25, 14, 69, -11, 11, 77, 78, -29, 29, -15, 37, -79, 15, 17, 79, 90, -25, 16,
    91, -26, -30, -38, 27, 30, 26, 92, -18, 93, -31, 82, -17, -94, 18, 19, -28, 45, 31, -27, -83, -46, 32, 33, 46,
    -19, 84, -20, 94, 95, -47, 38, 96, -33, -85, 35, -34, -39, 39, 34, 97, 86, -98, -40, 47, 40, 42, -36, -87, 41, 87,
    -35, 88, 36, 98, -48, -89, 48, 49, 50, 99, -43, -42, 44, 43, 100, 101, 89, -50, -51, 52, -102, 51, 102, -45, -44,
    103, -53, -52, 104, 105, 130, -106, 133, 135, 134, 131, 132, 115, 117, 116, -136, -133, 148, -135, 136, 138, 137,
    139, -118, 118, -117, 120, 119, 121, 106, 110, 111, 112, 108, 107, 149, 150, -139, -140, -112, 113, 109, 151,
    -121, -122, 152, 153, 155, 154, -153, 168, -114, -110, 170, 171, 173, 172, -156, 140, -155, 157, 159, 141, 142,
    156, 158, -174, -173, 174, 176, -143, 143, 144, 186, -145, 145, 146, 189, 191, -160, 122, -147, 147, 123, 124,
    175, 177, 187, -192, -125, 188, 125, 126, 192, -159, 194, -189, 160, -177, -127, 190, 161, 162, 127, 128, 204,
    -178, 205, 178, -163, 179, -129, 180, 163, 164, 206, -191, -181, 181, 182, -165, 209, -195, 211, 210, 165, 166,
    207, -183, 208, 183, 184, 193, -167, 195, -212, -209, 224, -211, -185, 227, 212, 214, 231, 232, 213, 215, 167,
    185, 228, 225, 233, 234, 229, 226, -233, 230, -196, 196, 197, 169, 236, -235, 237, 198, -215, 129, -238, 238,
    -231, 239, 235, 114, 247, -240, 248, 240, 241, -199, 199, -216, -249, 200, 216, -242, 217, 218, 242, 243, 249,
    -201, 201, 202, -244, 244, 245, -219, 219, 220, -246, 246, -203, 203, 250, 251, -221, 221, 222, -252, 252, -223,
    223, 253, 254, -255, 255,
)


def solution(mesh):
    placed = (
        P(BAT, SEG, None),
        P(BAT, None),
        P(BAT, SEG, None, None),
        P(SEG, None),
        P(SEG, None),
        P(SEG, None, BAT),
        P(SEG, None, BAT),
        P(SEG, None, BAT),
        P(SEG, None, BAT),
        P(SEG, None, BAT),
        P(SEG, None, BAT),
        P(),
        P(),
        P(BAT, SEG, None),
    )
    return jax.shard_map(
        on_device,
        mesh=mesh,
        in_specs=placed,
        out_specs=(
            P(BAT, SEG, None),
            P(BAT, SEG, None),
            P(SEG, None, BAT),
            P(SEG, None, BAT),
            P(SEG, None, BAT),
            P(SEG, None, BAT),
            P(SEG, None, BAT),
            P(SEG, None, BAT),
            P(),
            P(),
        ),
        check_vma=False,
    )
```

```python
import functools
import math

import jax
import jax.numpy as jnp
import numpy as np
from jax import lax
from jax.experimental import pallas as pl
from jax.experimental.pallas import tpu as pltpu
from jax.sharding import PartitionSpec as P

SEG, BAT = "segment", "batch"
WIN = 512
LAYERS = 2
CORES = 2
QB = 256

norm_eps = 1e-05
big_negative = -1e30
bucket_edges = np.ceil(16.0 * 8.0 ** (np.arange(1, 16) / 16.0)).astype(np.int32)
highest = lax.Precision.HIGHEST
f32 = jnp.float32
bf16 = jnp.bfloat16
VMEM_LIMIT = 20 * 1024 * 1024


def permuted(block, axis, route):
    count = lax.axis_size(axis)
    return lax.ppermute(block, axis, [(i, route(i)) for i in range(count)])


def core_swap(block):
    return permuted(block, SEG, lambda i: i ^ 1)


def room(tick):
    return pl.pallas_call(
        lambda source, result: None,
        out_shape=jax.ShapeDtypeStruct(tick.shape, tick.dtype),
        in_specs=[pl.BlockSpec(memory_space=pl.ANY)],
        out_specs=pl.BlockSpec(memory_space=pl.ANY),
        input_output_aliases={0: 0},
        cost_estimate=pl.CostEstimate(flops=200_000_000_000, transcendentals=0, bytes_accessed=0),
        name="room",
    )(tick)


def key(*parts):
    return "".join(map(str, parts))


class Steps:
    def __init__(self):
        self.steps = {}
        self.values = {}
        self.mark = ()
        self.tick = jnp.zeros((8, 128), f32)

    def given(self, name, value):
        self.values[name] = value
        return name

    def run(self, name, step, *sources):
        assert name not in self.steps, name
        self.steps[name] = ("run", step, sources)
        return name

    def send(self, name, link, transfer, *sources):
        assert name not in self.steps, name
        self.steps[name] = (link, transfer, sources)
        return name

    def value(self, source):
        if isinstance(source, tuple):
            return self.values[source[0]][source[1]]
        return self.values[source]

    def behind(self, values):
        leaves, tree = jax.tree.flatten(values)
        held = lax.optimization_barrier(tuple(leaves) + tuple(self.mark))
        return jax.tree.unflatten(tree, held[: len(leaves)])

    def wait(self, name):
        tick = room(self.behind(self.tick))
        leaves, tree = jax.tree.flatten(self.values[name])
        held = lax.optimization_barrier(tuple(leaves) + tuple(self.mark) + (tick,))
        self.tick = held[-1]
        self.mark = held[: len(leaves)]
        self.values[name] = jax.tree.unflatten(tree, self.mark)

    def carry_out(self, order):
        waited = set()
        names = list(self.steps)
        for number in order:
            name = names[number] if number >= 0 else names[-1 - number]
            if number < 0:
                waited.add(name)
                self.wait(name)
                continue
            kind, step, sources = self.steps[name]
            for source in sources:
                source = source[0] if isinstance(source, tuple) else source
                if source in self.steps and self.steps[source][0] != "run" and source not in waited:
                    waited.add(source)
                    self.wait(source)
            with jax.named_scope(name):
                result = step(*self.behind([self.value(source) for source in sources]))
            self.values[name] = result
            if kind == "run":
                self.mark = tuple(jax.tree.leaves(result))
        assert set(range(len(names))) <= set(order)


def pick(index, parts):
    return lax.select_n(index, *parts)


def total(*terms):
    return functools.reduce(jnp.add, [t.astype(f32) for t in terms])


def ring_step(block):
    count = lax.axis_size(SEG)
    return permuted(block, SEG, lambda i: (i + CORES) % count)


def in_order(parts, stretch):
    return [pick((stretch - k) % len(parts), parts) for k in range(len(parts))]


def swap_across(block):
    return permuted(block, BAT, lambda i: i ^ 1)


def swap_along(block):
    return permuted(block, BAT, lambda i: i ^ 2)


def cut_of(rows):
    return rows // 2 // 128 * 128


def qkv_half(matrix, core):
    rows, cols = matrix.shape
    return matrix.reshape(rows, cols // 256, 2, 128)[:, :, core].reshape(rows, cols // 2).T


def out_half(matrix, core):
    rows, cols = matrix.shape
    return matrix.reshape(rows // 256, 2, 128, cols)[:, core].reshape(rows // 2, cols)


def in_half(matrix, core, parts):
    rows, cols = matrix.shape
    return matrix.reshape(rows, parts, 2, cols // parts // 2)[:, :, core].reshape(rows, cols // 2).T


def down_half(matrix, core, parts):
    rows, cols = matrix.shape
    return matrix.reshape(parts, 2, rows // parts // 2, cols)[:, core].reshape(rows // 2, cols).T


def qkv_whole(halves):
    cols, rows = halves[0].shape
    stacked = jnp.stack([h.T.reshape(rows, cols // 128, 128) for h in halves], axis=2)
    return stacked.reshape(rows, 2 * cols)


def out_whole(halves):
    rows, cols = halves[0].shape
    stacked = jnp.stack([h.reshape(rows // 128, 128, cols) for h in halves], axis=1)
    return stacked.reshape(2 * rows, cols)


def in_whole(halves, parts):
    cols, rows = halves[0].shape
    stacked = jnp.stack([h.T.reshape(rows, parts, cols // parts) for h in halves], axis=2)
    return stacked.reshape(rows, 2 * cols)


def down_whole(halves, parts):
    cols, rows = halves[0].shape
    stacked = jnp.stack([h.T.reshape(parts, rows // parts, cols) for h in halves], axis=1)
    return stacked.reshape(2 * rows, cols)


def halves_of(parts):
    return (
        qkv_half,
        out_half,
        functools.partial(in_half, parts=parts),
        functools.partial(down_half, parts=parts),
    )


def gather_plain(shards, core):
    layers = ([], [])
    for shard, half in zip(shards, halves_of(4)):
        rows = lax.all_gather(shard, BAT, axis=1, tiled=True)
        slots = lax.all_gather(rows, SEG, axis=0, tiled=False)
        for layer in range(LAYERS):
            matrix = slots[layer::LAYERS].reshape(-1, rows.shape[1])
            layers[layer].append(jnp.where(core == 0, half(matrix, 0), half(matrix, 1)))
    return layers


def scatter_plain(parts, core):
    done = []
    slots = lax.axis_size(SEG)
    wholes = (qkv_whole, out_whole, functools.partial(in_whole, parts=4), functools.partial(down_whole, parts=4))
    for lower, upper, whole in zip(parts[0], parts[1], wholes):
        layers = []
        for half in (lower, upper):
            empty = jnp.zeros_like(half)
            matrix = whole((jnp.where(core == 0, half, empty), jnp.where(core == 0, empty, half)))
            layers.append(matrix.reshape(slots // LAYERS, -1, matrix.shape[1]))
        stacked = jnp.stack(layers, axis=1).reshape(slots, -1, layers[0].shape[2])
        rows = lax.psum_scatter(stacked, SEG, scatter_dimension=0, tiled=True)
        columns = lax.psum_scatter(rows, BAT, scatter_dimension=2, tiled=True)
        done.append(columns.astype(f32))
    return done


def spans(row_count, halo):
    for first in range(0, row_count, QB):
        start = max(0, first + halo - WIN)
        yield first, start, first + halo + QB - start


def mask_kernel(first_lane, chosen, index_ref, mask_ref):
    rows, slots = mask_ref.shape[1], mask_ref.shape[2]
    chunk = 64
    width = 256

    def body(first):
        index = index_ref[pl.ds(first, chunk), first_lane : first_lane + chosen]
        for low in range(0, slots, width):
            slot_ids = lax.broadcasted_iota(jnp.int32, (chunk, width), 1) + low
            bias = jnp.full((chunk, width), big_negative, f32)
            for t in range(chosen):
                bias = jnp.where(index[:, t : t + 1] == slot_ids, 0.0, bias)
            mask_ref[0, pl.ds(first, chunk), low : low + width] = bias.astype(bf16)

    chunks(rows, chunk, body)


def slot_mask(index, head, chosen, slots):
    out = jax.ShapeDtypeStruct((1, index.shape[0], slots), bf16)
    kernel = functools.partial(mask_kernel, head * chosen, chosen)
    return in_vmem(kernel, [out], None, [index], "slot_mask", 10_000_000_000)[0]


def nt_dot(left, right):
    return lax.dot_general(left, right, (((1,), (1,)), ((), ())), preferred_element_type=f32)


def tn_dot(left, right):
    return lax.dot_general(left, right, (((0,), (0,)), ((), ())), preferred_element_type=f32)


def nn_dot(left, right):
    return lax.dot_general(left, right, (((1,), (0,)), ((), ())), preferred_element_type=f32)


def forward_kernel(halo, with_memory, scale, *refs):
    refs = list(refs)
    bias_ref, docs_col, docs_row, q_ref, k_ref, v_ref = refs[:6]
    del refs[:6]
    if halo:
        k_halo, v_halo = refs[:2]
        del refs[:2]
    if with_memory:
        mem_k, mem_v, mask_ref, gate_ref = refs[:4]
        del refs[:4]
        o_ref, probs_ref, slots_ref, differ_ref = refs[:4]
        del refs[:4]
    else:
        o_ref, probs_ref = refs[:2]
        del refs[:2]
    if halo:
        keys, values = refs
        keys[:halo] = k_halo[...]
        keys[halo:] = k_ref[...]
        values[:halo] = v_halo[...]
        values[halo:] = v_ref[...]
    else:
        keys, values = k_ref, v_ref
    width = WIN + QB
    lanes = bias_ref.shape[2]
    tile = pltpu.roll(
        jnp.broadcast_to(bias_ref[0], (QB, lanes)), 0, axis=1, stride=1, stride_axis=0
    )[:, :width]
    if with_memory:
        opened = gate_ref[pl.program_id(0)]
    for first, start, count in spans(q_ref.shape[0], halo):
        rows = slice(first, first + QB)
        query = q_ref[rows]
        scores = nt_dot(query, keys[start : start + count]) * scale + tile[:, width - count :]
        same = docs_col[rows] == docs_row[:, start : start + count]
        scores = jnp.where(same, scores, big_negative)
        raised = jnp.exp(scores - jnp.max(scores, axis=-1, keepdims=True))
        probs = (raised * (1.0 / jnp.sum(raised, axis=-1, keepdims=True))).astype(bf16)
        probs_ref[0, rows, width - count :] = probs
        local = nn_dot(probs, values[start : start + count])
        if with_memory:
            picked = nt_dot(query, mem_k[...]) * scale + mask_ref[0, rows].astype(f32)
            raised = jnp.exp(picked - jnp.max(picked, axis=-1, keepdims=True))
            slot_probs = (raised * (1.0 / jnp.sum(raised, axis=-1, keepdims=True))).astype(bf16)
            slots_ref[0, rows] = slot_probs
            differ = nn_dot(slot_probs, mem_v[...]) - local
            differ_ref[rows] = differ.astype(bf16)
            local = local + opened * differ
        o_ref[rows] = local.astype(bf16)


def backward_kernel(halo, with_memory, scale, *refs):
    refs = list(refs)
    q_ref, k_ref, v_ref, do_ref, probs_ref = refs[:5]
    del refs[:5]
    if halo:
        k_halo, v_halo = refs[:2]
        del refs[:2]
    if with_memory:
        mem_k, mem_v, slots_ref, differ_ref, gate_ref = refs[:5]
        del refs[:5]
    d_ref, table_ref = refs[:2]
    del refs[:2]
    if with_memory:
        gate_grad = refs.pop(0)
    if halo:
        halo_grad = refs.pop(0)
    dk, dv, table = refs[:3]
    del refs[:3]
    if halo:
        keys, values = refs
        keys[:halo] = k_halo[...]
        keys[halo:] = k_ref[...]
        values[:halo] = v_halo[...]
        values[halo:] = v_ref[...]
    else:
        keys, values = k_ref, v_ref
    head = pl.program_id(0)
    heads = pl.num_programs(0)
    row_count, head_dim = q_ref.shape
    width = WIN + QB
    lanes = table.shape[1]
    dk[...] = jnp.zeros_like(dk)
    dv[...] = jnp.zeros_like(dv)
    table[...] = jnp.zeros_like(table)
    if with_memory:
        opened = gate_ref[head]
        gate_sum = jnp.zeros((1, head_dim), f32)
    here = pl.multiple_of(head * head_dim, head_dim)
    for first, start, count in spans(row_count, halo):
        rows = slice(first, first + QB)
        cols = slice(start, start + count)
        upstream = do_ref[rows]
        if with_memory:
            wide = upstream.astype(f32)
            gate_sum += jnp.sum(wide * differ_ref[rows].astype(f32), axis=0, keepdims=True)
            mem_grad = (opened * wide).astype(bf16)
            upstream = ((1.0 - opened) * wide).astype(bf16)
        probs = probs_ref[0, rows, width - count :]
        probs_wide = probs.astype(f32)
        grad = nt_dot(upstream, values[cols])
        inner = jnp.sum(probs_wide * grad, axis=-1, keepdims=True)
        score_wide = probs_wide * (grad - inner)
        score = score_wide.astype(bf16)
        table[:, width - count : width] += score_wide
        dq = nn_dot(score, keys[cols])
        dk[cols] += tn_dot(score, q_ref[rows])
        dv[cols] += tn_dot(probs, upstream)
        if with_memory:
            slot_probs = slots_ref[0, rows].astype(f32)
            slot_grad = nt_dot(mem_grad, mem_v[...])
            slot_score = slot_probs * (
                slot_grad - jnp.sum(slot_probs * slot_grad, axis=-1, keepdims=True)
            )
            dq += nn_dot(slot_score.astype(bf16), mem_k[...])
        d_ref[rows, pl.ds(here, head_dim)] = (dq * scale).astype(bf16)
    key_at = pl.multiple_of((heads + head) * head_dim, head_dim)
    value_at = pl.multiple_of((2 * heads + head) * head_dim, head_dim)
    if halo:
        halo_grad[0] = (dk[:halo] * scale).astype(bf16)
        halo_grad[1] = dv[:halo].astype(bf16)
    d_ref[:, pl.ds(key_at, head_dim)] = (dk[halo:] * scale).astype(bf16)
    d_ref[:, pl.ds(value_at, head_dim)] = dv[halo:].astype(bf16)
    turned = jnp.zeros((8, lanes), f32)
    for row in range(0, QB, 8):
        part = table[row : row + 8]
        turned += pltpu.roll(part, lanes - row, axis=1) if row else part
    total = turned[:1]
    for row in range(1, 8):
        total += pltpu.roll(turned, lanes - row, axis=1)[row : row + 1]
    table_ref[0] = total
    if with_memory:
        gate_grad[0] = gate_sum


def smooth_pair(pre):
    rate = math.sqrt(2.0 / math.pi)
    square = pre * pre
    turn = jnp.tanh(pre * (rate + (rate * 0.044715) * square))
    half = 0.5 + 0.5 * turn
    bend = pre * (rate + (rate * 3 * 0.044715) * square)
    return (pre * half).astype(bf16), (half + bend * (half - half * half) * 2.0).astype(bf16)


def norm_rows_of(values):
    center = values - jnp.mean(values, axis=-1, keepdims=True)
    factor = lax.rsqrt(jnp.mean(center * center, axis=-1, keepdims=True) + norm_eps)
    return center * factor, factor


def in_vmem(kernel, outs, scalars, operands, name, flops):
    vmem = pl.BlockSpec(memory_space=pltpu.VMEM)
    return pl.pallas_call(
        kernel,
        out_shape=outs,
        in_specs=([smem_block] if scalars is not None else []) + [vmem] * len(operands),
        out_specs=[vmem] * len(outs),
        compiler_params=pltpu.CompilerParams(vmem_limit_bytes=8 * 1024 * 1024),
        cost_estimate=pl.CostEstimate(flops=3 * flops, transcendentals=0, bytes_accessed=0),
        name=name,
    )(*([scalars] if scalars is not None else []), *operands)


smem_block = pl.BlockSpec(memory_space=pltpu.SMEM)


def chunks(count, size, body):
    def step(turn, carry):
        body(pl.multiple_of(turn * size, size))
        return carry

    lax.fori_loop(0, count // size, step, 0)


def segments(refs, low, high):
    for which, ref in enumerate(refs[:3]):
        yield which, 0, ref, low, high
    cut = refs[3].shape[0]
    if low < cut:
        yield 3, 0, refs[3], low, min(high, cut)
    if high > cut:
        yield 3, max(cut - low, 0), refs[4], max(low - cut, 0), high - cut


def place_of(at_ref, which, width, offset=0):
    return pl.multiple_of((at_ref[0] ^ which) * width + offset, 128)


def norm_kernel(row, part, at_ref, own_ref, across_ref, along_ref, low_ref, high_ref, out_ref):
    rows = [ref[row : row + 1, :].astype(f32) for ref in (own_ref, across_ref, along_ref)]
    rows.append(high_ref[row - low_ref.shape[0] : row - low_ref.shape[0] + 1, :].astype(f32))
    width = 4 * part
    chips = rows[0].shape[1] // width
    for k in range(4):
        which = at_ref[0] ^ k
        row_k = jnp.where(
            which < 2, jnp.where(which == 0, rows[0], rows[1]), jnp.where(which == 2, rows[2], rows[3])
        )
        for z in range(chips):
            for kind in range(4):
                first = z * width + kind * part
                out_ref[kind : kind + 1, z * width + k * part : z * width + (k + 1) * part] = row_k[:, first : first + part]


def norm_rows_by_pieces(at, row, part, pieces):
    out = jax.ShapeDtypeStruct((4, pieces[0].shape[1]), f32)
    return in_vmem(functools.partial(norm_kernel, row, part), [out], at, list(pieces), "norm", 1000)[0]


def head_kernel(joins, width, at_ref, *refs):
    hidden_ref, *refs = refs
    if joins:
        own_ref, got_ref, *refs = refs
    gain_ref, shift_ref, *refs = refs
    pieces, (normed_ref, out_ref), refs = refs[:5], refs[5:7], refs[7:]
    parts = list(segments(pieces, 0, width))

    def body(first):
        rows = pl.ds(first, 256)
        values = hidden_ref[rows, :]
        if joins:
            values = values + (own_ref[rows, :].astype(f32) + got_ref[rows, :].astype(f32))
            refs[0][rows, :] = values
        normal, _ = norm_rows_of(values)
        normed = (normal * gain_ref[...] + shift_ref[...]).astype(bf16)
        normed_ref[rows, :] = normed
        for which, offset, ref, low, high in parts:
            cols = pl.ds(place_of(at_ref, which, width, offset), high - low)
            out_ref[rows, cols] = nt_dot(normed, ref[low:high]).astype(bf16)

    chunks(hidden_ref.shape[0], 256, body)


def head_by_pieces(at, width, hidden, joins, gain, shift, pieces):
    rows, inner = hidden.shape
    outs = [jax.ShapeDtypeStruct((rows, inner), bf16), jax.ShapeDtypeStruct((rows, 4 * width), bf16)]
    if joins:
        outs.append(jax.ShapeDtypeStruct((rows, inner), f32))
    operands = [hidden, *joins, gain, shift, *pieces]
    return in_vmem(
        functools.partial(head_kernel, bool(joins), width), outs, at, operands, "head", 8 * rows * inner * width
    )


def by_columns_kernel(smooth, at_ref, rows_ref, *refs):
    pieces, outs = refs[:5], refs[5:]
    width = pieces[0].shape[0]
    parts = list(segments(pieces, 0, width))

    def body(first):
        rows = pl.ds(first, 256)
        for which, offset, ref, low, high in parts:
            cols = pl.ds(place_of(at_ref, which, width, offset), high - low)
            product = nt_dot(rows_ref[rows, :], ref[low:high])
            if smooth:
                outs[0][rows, cols], outs[1][rows, cols] = smooth_pair(product)
            else:
                outs[0][rows, cols] = product.astype(bf16)

    chunks(rows_ref.shape[0], 256, body)


def by_columns(at, rows, pieces, smooth):
    count, inner = rows.shape
    width = pieces[0].shape[0]
    outs = [jax.ShapeDtypeStruct((count, 4 * width), bf16)] * (2 if smooth else 1)
    return in_vmem(
        functools.partial(by_columns_kernel, smooth), outs, at, [rows, *pieces], "expand" if smooth else "down",
        8 * count * inner * width,
    )


def out_kernel(first, rows_per, width, at_ref, rows_ref, *refs):
    pieces, out_ref = refs[:5], refs[5]
    parts = list(segments(pieces, first, first + rows_per))

    def body(start):
        rows = pl.ds(start, 256)
        for which, _, ref, low, high in parts:
            acc = None
            for z in range(rows_ref.shape[1] // rows_per):
                part = nn_dot(
                    rows_ref[rows, z * rows_per : (z + 1) * rows_per], ref[low:high, z * width : (z + 1) * width]
                )
                acc = part if acc is None else acc + part
            out_ref[rows, pl.ds(place_of(at_ref, which, width), width)] = acc.astype(bf16)

    chunks(rows_ref.shape[0], 256, body)


def out_by_pieces(at, first, rows_per, width, attended, pieces):
    count = attended.shape[0]
    outs = [jax.ShapeDtypeStruct((count, 4 * width), bf16)]
    return in_vmem(
        functools.partial(out_kernel, first, rows_per, width), outs, at, [attended, *pieces], "out",
        8 * count * attended.shape[1] * width,
    )[0]


def by_rows_kernel(low, high, scaled, at_ref, rows_ref, *refs):
    pieces, refs = refs[:5], refs[5:]
    out_ref = refs[-1]
    span = high - low
    parts = list(segments(pieces, low, high))
    block = 512

    def body(start):
        rows = pl.ds(start, 256)
        for n in range(0, out_ref.shape[1], block):
            cols = slice(n, n + block)
            acc = None
            for which, offset, ref, first, last in parts:
                inner = pl.ds(place_of(at_ref, which, span, offset), last - first)
                part = nn_dot(rows_ref[rows, inner], ref[first:last, cols])
                acc = part if acc is None else acc + part
            if scaled:
                acc = acc * refs[0][rows, cols].astype(f32)
            out_ref[rows, cols] = acc.astype(bf16)

    chunks(rows_ref.shape[0], 256, body)


def by_rows(at, low, high, grad, pieces, slope=None):
    count = grad.shape[0]
    cols = pieces[0].shape[1]
    operands = [grad, *pieces] + ([] if slope is None else [slope])
    return in_vmem(
        functools.partial(by_rows_kernel, low, high, slope is not None),
        [jax.ShapeDtypeStruct((count, cols), bf16)], at, operands, "by_rows", 2 * count * grad.shape[1] * cols,
    )[0]


def attended_back_kernel(first, rows_per, width, at_ref, grad_ref, *refs):
    pieces, out_ref = refs[:5], refs[5]
    parts = list(segments(pieces, first, first + rows_per))

    def body(start):
        rows = pl.ds(start, 256)
        for z in range(out_ref.shape[1] // rows_per):
            acc = None
            for which, _, ref, low, high in parts:
                grad = grad_ref[rows, pl.ds(place_of(at_ref, which, width), width)]
                part = nt_dot(grad, ref[low:high, z * width : (z + 1) * width])
                acc = part if acc is None else acc + part
            out_ref[rows, z * rows_per : (z + 1) * rows_per] = acc.astype(bf16)

    chunks(grad_ref.shape[0], 256, body)


def attended_back(at, first, rows_per, width, grad, pieces):
    count = grad.shape[0]
    chips = pieces[0].shape[1] // width
    return in_vmem(
        functools.partial(attended_back_kernel, first, rows_per, width),
        [jax.ShapeDtypeStruct((count, chips * rows_per), bf16)], at, [grad, *pieces], "attended_back",
        2 * count * grad.shape[1] * chips * rows_per,
    )[0]


def share_kernel(which, heads, adds, at_ref, *refs):
    left_ref, right_ref, *refs = refs
    if heads:
        attended_ref, grad_ref, *refs = refs
    count = {"": 0, "low": 1, "high": 1, "both": 2}[adds]
    got, outs = refs[:count], refs[count:]
    chips = 4
    rows, width = left_ref.shape[1] // 4, right_ref.shape[1] // chips
    own = which == 0
    left = left_ref[:, pl.ds(place_of(at_ref, which, rows), rows)]
    if heads:
        more = attended_ref.shape[1] // chips
        grad = grad_ref[:, pl.ds(place_of(at_ref, which, grad_ref.shape[1] // 4), grad_ref.shape[1] // 4)]

    def body(n):
        column = lax.rem(at_ref[1] + (3 * chips - 1) - n, chips) if own else n
        cols = pl.ds(pl.multiple_of(column * width, width), width)
        value = tn_dot(left, right_ref[:, cols])
        if heads:
            part = tn_dot(attended_ref[:, pl.ds(pl.multiple_of(column * more, more), more)], grad)
            value = jnp.concatenate([value, part], axis=0)
        half = value.shape[0] // 2
        if adds == "low":
            value = jnp.concatenate([value[:half] + got[0][:, cols].astype(f32), value[half:]], axis=0)
        elif adds == "high":
            value = jnp.concatenate([value[:half], value[half:] + got[0][:, cols].astype(f32)], axis=0)
        elif adds == "both":
            value = value + got[0][:, cols].astype(f32) + got[1][:, cols].astype(f32)
        value = value.astype(bf16)
        if which == 3:
            outs[0][:, cols], outs[1][:, cols] = value[:half], value[half:]
        elif own:
            outs[0][n] = value
        else:
            outs[0][:, cols] = value

    def step(n, carry):
        body(n)
        return carry

    lax.fori_loop(0, chips, step, 0)


def share_grad(at, which, left, right, head_pair=(), adds="", got=()):
    chips = 4
    rows, cols = left.shape[1] // 4, right.shape[1]
    if head_pair:
        rows += head_pair[0].shape[1] // chips
    if which == 3:
        outs = [jax.ShapeDtypeStruct((rows // 2, cols), bf16)] * 2
    elif which == 0:
        outs = [jax.ShapeDtypeStruct((chips, rows, cols // chips), bf16)]
    else:
        outs = [jax.ShapeDtypeStruct((rows, cols), bf16)]
    return in_vmem(
        functools.partial(share_kernel, which, bool(head_pair), adds), outs, at, [left, right, *head_pair, *got],
        "share", 2 * left.shape[0] * rows * cols,
    )


def join_norm_kernel(hidden_ref, own_ref, got_ref, gain_ref, shift_ref, result_ref, normed_ref):
    def body(first):
        rows = pl.ds(first, 128)
        values = hidden_ref[rows, :] + (own_ref[rows, :].astype(f32) + got_ref[rows, :].astype(f32))
        result_ref[rows, :] = values
        normal, _ = norm_rows_of(values)
        normed_ref[rows, :] = (normal * gain_ref[...] + shift_ref[...]).astype(bf16)

    chunks(hidden_ref.shape[0], 128, body)


def join_norm(hidden, own, got, gain, shift):
    outs = [jax.ShapeDtypeStruct(hidden.shape, f32), jax.ShapeDtypeStruct(hidden.shape, bf16)]
    return in_vmem(join_norm_kernel, outs, None, [hidden, own, got, gain, shift], "join_norm", 10 * hidden.size)


def join_back_kernel(up_ref, own_ref, got_ref, values_ref, gain_ref, result_ref, low_ref, gain_grad, shift_grad):
    gain_grad[...] = jnp.zeros_like(gain_grad)
    shift_grad[...] = jnp.zeros_like(shift_grad)

    def body(first):
        rows = pl.ds(first, 128)
        upstream = own_ref[rows, :].astype(f32) + got_ref[rows, :].astype(f32)
        normal, factor = norm_rows_of(values_ref[rows, :])
        gain_grad[...] += jnp.sum(upstream * normal, axis=0, keepdims=True)
        shift_grad[...] += jnp.sum(upstream, axis=0, keepdims=True)
        scaled = upstream * gain_ref[...]
        inner = (
            scaled
            - jnp.mean(scaled, axis=-1, keepdims=True)
            - normal * jnp.mean(scaled * normal, axis=-1, keepdims=True)
        )
        result = up_ref[rows, :].astype(f32) + factor * inner
        result_ref[rows, :] = result
        low_ref[rows, :] = result.astype(bf16)

    chunks(values_ref.shape[0], 128, body)


def join_back(upstream, own, got, values, gain):
    row = jax.ShapeDtypeStruct((1, values.shape[1]), f32)
    outs = [jax.ShapeDtypeStruct(values.shape, f32), jax.ShapeDtypeStruct(values.shape, bf16), row, row]
    return in_vmem(join_back_kernel, outs, None, [upstream, own, got, values, gain], "join_back", 20 * values.size)


def head_block(rows, head_dim, offset):
    return pl.BlockSpec((rows, head_dim), lambda h: (0, offset + h))


def plane_block(rows, cols):
    return pl.BlockSpec((1, rows, cols), lambda h: (h, 0, 0))


def attend(projected, bias_rows, docs_col, docs_row, halo_rows, memory, scale):
    row_count = projected.shape[0]
    head_count, _, lanes = bias_rows.shape
    head_dim = projected.shape[1] // (3 * head_count)
    halo = 0 if halo_rows is None else halo_rows.shape[1]
    width = WIN + QB
    operands = [bias_rows, docs_col, docs_row, projected, projected, projected]
    specs = [
        plane_block(1, lanes),
        pl.BlockSpec(docs_col.shape, lambda h: (0, 0)),
        pl.BlockSpec(docs_row.shape, lambda h: (0, 0)),
        head_block(row_count, head_dim, 0),
        head_block(row_count, head_dim, head_count),
        head_block(row_count, head_dim, 2 * head_count),
    ]
    scratch = []
    if halo:
        operands += [halo_rows[0], halo_rows[1]]
        specs += [head_block(halo, head_dim, 0)] * 2
        scratch = [pltpu.VMEM((halo + row_count, head_dim), bf16)] * 2
    outs = [
        jax.ShapeDtypeStruct((row_count, head_count * head_dim), bf16),
        jax.ShapeDtypeStruct((head_count, row_count, width), bf16),
    ]
    out_specs = [head_block(row_count, head_dim, 0), plane_block(row_count, width)]
    flops = 4 * head_count * row_count * width * head_dim
    if memory is not None:
        mem_keys, mem_values, masks, gate = memory
        slots = mem_keys.shape[0]
        mask = jnp.concatenate(masks, axis=0)
        operands += [mem_keys, mem_values, mask, gate]
        specs += [head_block(slots, head_dim, 0)] * 2 + [plane_block(row_count, slots), smem_block]
        outs += [
            jax.ShapeDtypeStruct((head_count, row_count, slots), bf16),
            jax.ShapeDtypeStruct((row_count, head_count * head_dim), bf16),
        ]
        out_specs += [plane_block(row_count, slots), head_block(row_count, head_dim, 0)]
        flops += 4 * head_count * row_count * slots * head_dim
    return pl.pallas_call(
        functools.partial(forward_kernel, halo, memory is not None, scale),
        out_shape=outs,
        grid=(head_count,),
        in_specs=specs,
        out_specs=out_specs,
        scratch_shapes=scratch,
        compiler_params=pltpu.CompilerParams(vmem_limit_bytes=VMEM_LIMIT),
        cost_estimate=pl.CostEstimate(
            flops=flops, transcendentals=head_count * row_count * width, bytes_accessed=16 * 1024 * 1024
        ),
        name="attend",
    )(*operands)


def attend_back(projected, grad, probs, halo_rows, memory, scale):
    row_count = projected.shape[0]
    head_count, _, width = probs.shape
    head_dim = projected.shape[1] // (3 * head_count)
    halo = 0 if halo_rows is None else halo_rows.shape[1]
    lanes = 1024
    operands = [projected, projected, projected, grad, probs]
    specs = [
        head_block(row_count, head_dim, 0),
        head_block(row_count, head_dim, head_count),
        head_block(row_count, head_dim, 2 * head_count),
        head_block(row_count, head_dim, 0),
        plane_block(row_count, width),
    ]
    scratch = [
        pltpu.VMEM((halo + row_count, head_dim), f32),
        pltpu.VMEM((halo + row_count, head_dim), f32),
        pltpu.VMEM((QB, lanes), f32),
    ]
    if halo:
        operands += [halo_rows[0], halo_rows[1]]
        specs += [head_block(halo, head_dim, 0)] * 2
        scratch += [pltpu.VMEM((halo + row_count, head_dim), bf16)] * 2
    outs = [
        jax.ShapeDtypeStruct(projected.shape, bf16),
        jax.ShapeDtypeStruct((head_count, 1, lanes), f32),
    ]
    out_specs = [pl.BlockSpec(projected.shape, lambda h: (0, 0)), plane_block(1, lanes)]
    flops = 8 * head_count * row_count * width * head_dim
    if memory is not None:
        mem_keys, mem_values, slot_probs, differ, gate = memory
        slots = mem_keys.shape[0]
        operands += [mem_keys, mem_values, slot_probs, differ, gate]
        specs += [head_block(slots, head_dim, 0)] * 2
        specs += [plane_block(row_count, slots), head_block(row_count, head_dim, 0), smem_block]
        outs += [jax.ShapeDtypeStruct((head_count, 1, head_dim), f32)]
        out_specs += [plane_block(1, head_dim)]
        flops += 4 * head_count * row_count * slots * head_dim
    if halo:
        outs += [jax.ShapeDtypeStruct((2, halo, head_count * head_dim), bf16)]
        out_specs += [pl.BlockSpec((2, halo, head_dim), lambda h: (0, 0, h))]
    return pl.pallas_call(
        functools.partial(backward_kernel, halo, memory is not None, scale),
        out_shape=outs,
        grid=(head_count,),
        in_specs=specs,
        out_specs=out_specs,
        scratch_shapes=scratch,
        compiler_params=pltpu.CompilerParams(vmem_limit_bytes=VMEM_LIMIT),
        cost_estimate=pl.CostEstimate(
            flops=flops, transcendentals=0, bytes_accessed=20 * 1024 * 1024
        ),
        name="attend_back",
    )(*operands)


def bucket_of(distance):
    beyond = jnp.sum((distance[..., None] >= jnp.asarray(bucket_edges)).astype(jnp.int32), axis=-1)
    return jnp.where(distance < 16, distance, 16 + beyond)


def distance_onehot(bucket_count):
    bucket = bucket_of(jnp.arange(WIN, dtype=jnp.int32))
    return (bucket[:, None] == jnp.arange(bucket_count, dtype=jnp.int32)).astype(f32)


def normalize(values):
    center = values - jnp.mean(values, axis=-1, keepdims=True)
    factor = lax.rsqrt(jnp.mean(center * center, axis=-1, keepdims=True) + norm_eps)
    return center * factor, factor


def head_in(hidden, gain, shift, qkv):
    normal, _ = normalize(hidden)
    normed = (normal * gain + shift).astype(bf16)
    return normed, nt_dot(normed, qkv).astype(bf16)


def out_part(attended, out):
    return nn_dot(attended, out).astype(bf16)


def down_part(active, down):
    return nt_dot(active, down).astype(bf16)


def joined(hidden, own, got):
    return hidden + (own.astype(f32) + got.astype(f32))


def weight_grad(left, right):
    return tn_dot(left, right).astype(bf16)


def expand_back(upstream, down, slope):
    return (nn_dot(upstream, down) * slope.astype(f32)).astype(bf16)


def input_part(grad, weight):
    return nn_dot(grad, weight).astype(bf16)


class Place:
    def __init__(self, seq_count):
        self.segments = lax.axis_size(SEG)
        self.batches = lax.axis_size(BAT)
        self.chips = self.segments // CORES
        self.seqs = seq_count
        self.pairs = self.chips // seq_count
        here = lax.axis_index(SEG)
        self.batch = lax.axis_index(BAT)
        self.core = here % CORES
        self.stretch = here // CORES
        self.low = self.core == 0
        self.seq_no = self.stretch // self.pairs
        self.place_no = self.stretch % seq_count

    def both(self, own, got):
        return jnp.where(self.low, own, got), jnp.where(self.low, got, own)


    def route(self, turn):
        pairs = []
        for source in range(self.segments):
            chip, lane = divmod(source, CORES)
            group, place = divmod(chip, self.seqs)
            pairs.append((source, (((place + turn) % self.seqs) * self.pairs + group) * CORES + lane))
        return pairs

    def local(self, turn):
        return self.pairs == 1 and turn == 0

    def out_block(self, stored, turn):
        return lax.dynamic_index_in_dim(stored, (self.place_no + turn) % self.seqs, 0, keepdims=False)

    def back_block(self, blocks, turn):
        return lax.dynamic_index_in_dim(blocks, (self.seq_no - turn) % self.seqs, 0, keepdims=False)

    def owned(self, *got):
        return jnp.stack([pick((self.seq_no - place) % self.seqs, got) for place in range(self.seqs)])

    def stored(self, *got):
        return jnp.stack([pick((number - self.place_no) % self.seqs, got) for number in range(self.seqs)])

    def sequence(self, own, got):
        pair = jnp.stack(self.both(own, got), axis=1)
        return pair.reshape((-1,) + own.shape[2:])

    def own_blocks(self, rows):
        split = rows.reshape(self.seqs, CORES, -1, rows.shape[1])
        return jnp.where(self.low, split[:, 0], split[:, 1])


def route_blocks(steps, place, name, source, back=False):
    got = []
    for turn in range(place.seqs):
        block = steps.run(key(name, "b", turn), lambda v, t=turn: (place.back_block if back else place.out_block)(v, t), source)
        if not place.local(turn):
            route = place.route(turn)
            if back:
                route = [(there, here) for here, there in route]
            block = steps.send(
                key(name, turn), key("z", turn), lambda v, route=tuple(route): lax.ppermute(v, SEG, route), block
            )
        got.append(block)
    return steps.run(key(name, "own"), place.stored if back else place.owned, *got)


def swap(steps, name, source):
    return steps.send(name, "core", core_swap, source)


def gather_steps(steps, place, shards, norm_rows, memory):
    qkv, out, inner, down = shards
    width = qkv.shape[0]
    gain_cols = norm_rows.shape[-1]
    slots = memory.shape[3]
    head, outs, hidden = qkv.shape[1] // 2, out.shape[0] // 2, inner.shape[1] // 2
    ends = np.cumsum([head + outs + 16, hidden, 2 * down.shape[1], memory[0].size // width])
    chips = place.chips

    def packed(core, qkv, out, inner, down, norm_rows, memory):
        down_rows = down_half(down, core, 1)
        return jnp.concatenate(
            [
                qkv_half(qkv, core),
                out_half(out, core),
                jnp.pad(norm_rows.reshape(1, width), ((0, 15), (0, 0))),
                in_half(inner, core, 1),
                down_rows[:, :width],
                down_rows[:, width:],
                memory_rows_of(memory[core]),
            ],
            axis=0,
        )

    def memory_rows_of(memory):
        return jnp.concatenate(
            [memory[kind, 0, :, at : at + width] for kind in range(2) for at in range(0, memory.shape[3], width)], axis=0
        )

    def first(*arrays):
        low, high = packed(0, *arrays), packed(1, *arrays)
        return jnp.where(place.low, low, high), jnp.where(place.low, high, low)

    for name, array in zip(("qkv", "out", "inner", "down", "norm", "mem"), (*shards, norm_rows, memory)):
        steps.given(name, array)
    steps.run("pack", first, "qkv", "out", "inner", "down", "norm", "mem")
    swap(steps, "wswap", ("pack", 1))

    def blocks(own, got):
        lower, upper = place.both(own, got)
        kept = []
        for layer in (lower, upper):
            kept += [layer[: ends[0]], layer[ends[0] : ends[1]], layer[ends[1] : ends[2]]]
        memory_rows = jnp.concatenate([lower[ends[2] :], upper[ends[2] :]], axis=0)
        kept[3] = jnp.concatenate([kept[3], memory_rows], axis=0)
        return kept

    steps.run("blocks", blocks, ("pack", 0), "wswap")

    def formed(unit, *ring):
        parts = in_order(ring, place.stretch)
        if unit[0] == "A":
            rows = jnp.concatenate([p[: ends[0]] for p in parts], axis=1)
            if unit == "A0":
                return (rows,)
            halves = memory.shape[4] // width
            block = 2 * halves * slots
            whole = []
            for kind in range(2):
                cols = []
                for half in range(halves):
                    first = ends[0] + (kind * halves + half) * slots
                    cols.append(
                        jnp.concatenate(
                            [p[first + c * block : first + c * block + slots] for p in parts for c in range(CORES)], axis=0
                        )
                    )
                whole.append(jnp.concatenate(cols, axis=1))
            return rows, jnp.stack(whole)
        if unit[0] == "I":
            return (jnp.concatenate(parts, axis=1),)
        half = parts[0].shape[0] // 2
        return (jnp.concatenate([q for p in parts for q in (p[:half], p[half:])], axis=1),)

    def norm_of(at, *pieces):
        return norm_rows_by_pieces(at, head + outs, gain_cols, pieces)

    pieces = {}
    for number, unit in enumerate(("A0", "I0", "D0", "A1", "I1", "D1")):
        ring = [("blocks", number)]
        for turn in range(1, chips):
            ring.append(steps.send(key("z", turn, unit), "z", ring_step, ring[-1]))
        steps.run(key("form", unit), functools.partial(formed, unit), *ring)
        block = (key("form", unit), 0)
        steps.send(key("px", unit), "x", swap_across, block)
        steps.send(key("py", unit), "y", swap_along, block)
        steps.send(key("fx", unit), "x", lambda along: swap_across(along[: cut_of(along.shape[0])]), key("py", unit))
        steps.send(key("fy", unit), "y", lambda across: swap_along(across[cut_of(across.shape[0]) :]), key("px", unit))
        pieces[unit] = (block, key("px", unit), key("py", unit), key("fx", unit), key("fy", unit))
        if unit[0] == "A":
            steps.run(key("norm", unit[1]), norm_of, "at", *pieces[unit])
    return pieces, ("formA1", 1), (head, outs, width)


def scatter_steps(steps, place, unit, left, right, *head_pair):
    heads = bool(head_pair)

    def shares(which, adds):
        def step(at, left, right, *rest):
            pair, got = (rest[:2], rest[2:]) if heads else ((), rest)
            return share_grad(at, which, left, right, pair, adds, got)

        return step

    sources = ("place", left, right, *head_pair)
    steps.run(key("ra", unit), shares(3, ""), *sources)
    steps.send(key("rx", unit), "x", swap_across, (key("ra", unit), 0))
    steps.send(key("ry", unit), "y", swap_along, (key("ra", unit), 1))
    steps.run(key("rb", unit), shares(1, "high"), *sources, key("ry", unit))
    steps.run(key("rc", unit), shares(2, "low"), *sources, key("rx", unit))
    steps.send(key("sx", unit), "x", swap_across, (key("rb", unit), 0))
    steps.send(key("sy", unit), "y", swap_along, (key("rc", unit), 0))
    steps.run(key("rd", unit), shares(0, "both"), *sources, key("sx", unit), key("sy", unit))
    own = (key("rd", unit), 0)
    travelling = steps.run(key("a0", unit), lambda parts: parts[0], own)
    for turn in range(1, place.chips):
        steps.send(key("q", turn, unit), "z", ring_step, travelling)
        last = turn == place.chips - 1
        travelling = steps.run(
            key("a", turn, unit),
            lambda got, parts, turn=turn, last=last: total(got, parts[turn]) if last else total(got, parts[turn]).astype(bf16),
            key("q", turn, unit),
            own,
        )
    return travelling


def finish_steps(steps, place, kind, lower, upper):
    steps.run(key("e", kind), lambda a, b: jnp.where(place.low, b, a).astype(bf16), lower, upper)
    swap(steps, key("eswap", kind), key("e", kind))

    def both(lower, upper, got):
        return place.both(jnp.where(place.low, lower, upper), got.astype(f32))

    return steps.run(key("done", kind), both, lower, upper, key("eswap", kind))


def on_device(
    tokens,
    doc_ids,
    knn_index,
    mem_keys,
    mem_values,
    qkv_weight,
    out_weight,
    in_weight,
    down_weight,
    norm_gain,
    norm_bias,
    rel_table,
    mem_gate,
    cotangent,
):
    seq_count, block_len, model_width = tokens.shape
    bucket_count, head_total = rel_table.shape[1:]
    head_dim = model_width // head_total
    topk_count = knn_index.shape[3]
    heads = head_total // CORES
    inner_width = heads * head_dim
    scale = 1.0 / math.sqrt(head_dim)
    place = Place(seq_count)
    steps = Steps()
    low_core = place.low
    pair_len = CORES * seq_count * block_len
    halo = WIN if place.pairs > 1 else 0
    by_chip = place.pairs == 1 and place.batches == 4

    norm_rows = jnp.stack([norm_gain[0], norm_bias[0]])
    shards = (qkv_weight[0], out_weight[0], in_weight[0], down_weight[0])
    memory = jnp.stack([mem_keys, mem_values]).reshape(2, mem_keys.shape[0], heads, CORES, head_dim)
    memory = jnp.transpose(memory, (3, 0, 1, 2, 4)).reshape(CORES, 2, 1, mem_keys.shape[0], inner_width)
    if by_chip:
        pieces, memory_at, sizes = gather_steps(steps, place, shards, norm_rows, memory)
    else:
        norms = lax.all_gather(norm_rows, (BAT, SEG), axis=0, tiled=False)
        norms = norms.reshape(place.batches, place.chips, LAYERS, 2, 2, norm_rows.shape[-1])
        norms = jnp.transpose(norms, (2, 3, 4, 1, 0, 5)).reshape(LAYERS, 2, 2, -1).astype(f32)
        weights = []
        for layer, matrices in enumerate(gather_plain(shards, place.core)):
            named = zip(("qkv", "out", "inner", "down", "norm"), (*matrices, norms[layer]))
            weights.append(tuple(steps.given(key(name, layer), array) for name, array in named))
        whole = lax.all_gather(memory, SEG, axis=3, tiled=True)
        memory_at = steps.given("memory", jnp.where(low_core, whole[0], whole[1])[:, 0])

    docs = lax.dynamic_index_in_dim(doc_ids, place.seq_no, 0, keepdims=False)
    first_row = place.stretch % place.pairs * pair_len
    docs_col = lax.dynamic_slice_in_dim(docs, first_row, pair_len, 0).reshape(pair_len, 1)
    docs_padded = jnp.concatenate([jnp.full((halo,), -1, jnp.int32), docs]) if halo else docs
    docs_row = lax.dynamic_slice_in_dim(docs_padded, first_row, halo + pair_len, 0).reshape(1, -1)
    steps.given("cols", docs_col)
    steps.given("rows", docs_row)
    onehot = distance_onehot(bucket_count)
    lanes = 1024

    def biases(table):
        tables = table.reshape(LAYERS, bucket_count, heads, CORES)
        tables = jnp.where(low_core, tables[..., 0], tables[..., 1])
        near = jnp.einsum("db,lbh->lhd", onehot[::-1], tables, precision=highest)[:, :, None]
        before = jnp.full((LAYERS, heads, 1, 1), big_negative, f32)
        beyond = jnp.full((LAYERS, heads, 1, lanes - WIN - 1), big_negative, f32)
        joined = jnp.concatenate([before, near, beyond], axis=3)
        return [joined[layer] for layer in range(LAYERS)]

    steps.run("bias", biases, steps.given("table", rel_table))
    gate_all = jax.nn.sigmoid(mem_gate).reshape(heads, CORES)
    gate = jnp.where(low_core, gate_all[:, 0], gate_all[:, 1])
    steps.given("gate", gate)

    def routed(name, array):
        return route_blocks(steps, place, name, steps.given(key(name, "in"), array))

    def by_head(blocks):
        rows = blocks.reshape(seq_count * block_len, head_total * topk_count)
        parts = [rows[:, h * topk_count : (h + 1) * topk_count] for h in range(head_total)]
        even, odd = jnp.concatenate(parts[::CORES], axis=1), jnp.concatenate(parts[1::CORES], axis=1)
        return jnp.where(low_core, even, odd), jnp.where(low_core, odd, even)

    slot_total = mem_keys.shape[0] * place.segments
    steps.run("flat", lambda v: v.reshape(seq_count, block_len, head_total * topk_count), steps.given("knn", knn_index))
    steps.run("kh", by_head, route_blocks(steps, place, "k", "flat"))
    swap(steps, "kswap", ("kh", 1))

    def whole_index(own, got):
        shape = (seq_count, block_len, heads * topk_count)
        pair = jnp.stack(place.both(own.reshape(shape), got.reshape(shape)), axis=1)
        return pair.reshape(pair_len, heads * topk_count)

    steps.run("index", whole_index, ("kh", 0), "kswap")
    masks = [
        steps.run(key("mask", head), lambda index, head=head: slot_mask(index, head, topk_count, slot_total), "index")
        for head in range(heads)
    ]

    own = routed("t", tokens)
    swap(steps, "tswap", own)
    hidden = steps.run("hid0", lambda own, got: place.sequence(own, got).astype(f32), own, "tswap")
    own = routed("c", cotangent)
    swap(steps, "cswap", own)
    upstream_low = steps.run("up", place.sequence, own, "cswap")
    upstream = upstream_low

    def halo_of(projected):
        if not halo:
            return None
        tail = projected[pair_len - halo :, inner_width:]
        route = [(i, i + CORES) for i in range(place.segments - CORES) if (i // CORES + 1) % place.pairs != 0]
        got = lax.ppermute(tail, SEG, route)
        return jnp.stack([got[:, :inner_width], got[:, inner_width:]])

    def halo_back(d_projected, halo_grad):
        route = [(i + CORES, i) for i in range(place.segments - CORES) if (i // CORES + 1) % place.pairs != 0]
        got = lax.ppermute(jnp.concatenate([halo_grad[0], halo_grad[1]], axis=1), SEG, route)
        edge = d_projected[pair_len - halo :, inner_width:].astype(f32) + got.astype(f32)
        return d_projected.at[pair_len - halo :, inner_width:].set(edge.astype(bf16))

    def attention(projected, bias, cols, rows, *rest):
        halo_rows = halo_of(projected)
        extra = (rest[0][0], rest[0][1], rest[1:-1], rest[-1]) if rest else None
        return attend(projected, bias, cols, rows, halo_rows, extra, scale)

    def attention_back(projected, grad, probs, *rest):
        halo_rows = halo_of(projected)
        extra = (rest[0][0], rest[0][1], *rest[1:]) if rest else None
        backs = attend_back(projected, grad, probs, halo_rows, extra, scale)
        if halo:
            backs = [halo_back(backs[0], backs[-1]), *backs[1:-1]]
        return backs

    if by_chip:
        head_rows, out_rows, width = sizes
        steps.given("at", place.batch.reshape(1))
        steps.given("place", jnp.stack([place.batch, place.stretch]))

    def row(norm, kind, which):
        return norm[2 * kind + which].reshape(1, -1) if by_chip else norm[kind, which].reshape(1, -1)

    def head_step(n, hidden):
        if not by_chip:
            qkv, norm = weights[n][0], weights[n][4]
            if n == 1:
                hidden = steps.run("hid1", joined, *hidden)
            steps.run(key("head", n), lambda h, norm, w: head_in(h, norm[0, 0], norm[1, 0], w), hidden, norm, qkv)
            return hidden

        def step(at, norm, hidden, *rest):
            joins, parts = rest[:-5], rest[-5:]
            return head_by_pieces(at, head_rows, hidden, joins, row(norm, 0, 0), row(norm, 1, 0), parts)

        steps.run(key("head", n), step, "at", key("norm", n), *(hidden if n == 1 else (hidden,)), *pieces[key("A", n)])
        return ("head1", 2) if n == 1 else hidden

    hidden_at = []
    for n in range(LAYERS):
        norm = key("norm", n) if by_chip else weights[n][4]
        hidden = head_step(n, hidden)
        hidden_at.append(hidden)
        extra = (memory_at, *masks, "gate") if n == 1 else ()
        steps.run(key("att", n), attention, (key("head", n), 1), ("bias", n), "cols", "rows", *extra)
        if by_chip:
            steps.run(
                key("op", n), lambda at, a, *parts: out_by_pieces(at, head_rows, out_rows, width, a, parts),
                "at", (key("att", n), 0), *pieces[key("A", n)],
            )
        else:
            steps.run(key("op", n), out_part, (key("att", n), 0), weights[n][1])
        swap(steps, key("oswap", n), key("op", n))
        steps.run(
            key("jn", n), lambda h, own, got, norm: join_norm(h, own, got, row(norm, 0, 1), row(norm, 1, 1)),
            hidden, key("op", n), key("oswap", n), norm,
        )
        if by_chip:
            steps.run(key("ex", n), lambda at, a, *parts: by_columns(at, a, parts, True), "at", (key("jn", n), 1), *pieces[key("I", n)])
            steps.run(key("dp", n), lambda at, a, *parts: by_columns(at, a, parts, False)[0], "at", (key("ex", n), 0), *pieces[key("D", n)])
        else:
            steps.run(key("ex", n), lambda a, w: smooth_pair(nt_dot(a, w)), (key("jn", n), 1), weights[n][2])
            steps.run(key("dp", n), down_part, (key("ex", n), 0), weights[n][3])
        swap(steps, key("dswap", n), key("dp", n))
        hidden = (("jn0", 0), "dp0", "dswap0")

    def last_rows(*a):
        return place.own_blocks(joined(*a).astype(bf16))

    steps.run("last", last_rows, ("jn1", 0), "dp1", "dswap1")
    mixed_at = route_blocks(steps, place, "m", "last", True)

    norm_parts, table_parts, reduced = [None, None], [None, None], [{}, {}]
    for n in (1, 0):
        norm = key("norm", n) if by_chip else weights[n][4]
        if by_chip:
            reduced[n]["D"] = scatter_steps(steps, place, key("D", n), upstream_low, (key("ex", n), 0))
            steps.run(
                key("pg", n), lambda at, g, slope, *parts: by_rows(at, 0, parts[0].shape[0], g, parts, slope),
                "at", upstream_low, (key("ex", n), 1), *pieces[key("D", n)],
            )
            steps.run(
                key("ip", n), lambda at, g, *parts: by_rows(at, 0, parts[0].shape[0], g, parts), "at", key("pg", n), *pieces[key("I", n)]
            )
            swap(steps, key("iswap", n), key("ip", n))
            reduced[n]["I"] = scatter_steps(steps, place, key("I", n), key("pg", n), (key("jn", n), 1))
        else:
            steps.run(key("gD", n), weight_grad, upstream_low, (key("ex", n), 0))
            steps.run(key("pg", n), expand_back, upstream_low, weights[n][3], (key("ex", n), 1))
            steps.run(key("ip", n), input_part, key("pg", n), weights[n][2])
            swap(steps, key("iswap", n), key("ip", n))
            steps.run(key("gI", n), weight_grad, key("pg", n), (key("jn", n), 1))
        steps.run(
            key("jb", n), lambda up, own, got, h, norm: join_back(up, own, got, h, row(norm, 0, 1)),
            upstream, key("ip", n), key("iswap", n), (key("jn", n), 0), norm,
        )
        if by_chip:
            steps.run(
                key("ag", n), lambda at, g, *parts: attended_back(at, head_rows, out_rows, width, g, parts),
                "at", (key("jb", n), 1), *pieces[key("A", n)],
            )
        else:
            steps.run(key("ag", n), lambda g, w: nt_dot(g, w).astype(bf16), (key("jb", n), 1), weights[n][1])
        extra = (memory_at, ("att1", 2), ("att1", 3), "gate") if n == 1 else ()
        steps.run(key("ab", n), attention_back, (key("head", n), 1), key("ag", n), (key("att", n), 1), *extra)
        if by_chip:
            steps.run(
                key("iq", n), lambda at, g, *parts: by_rows(at, 0, head_rows, g, parts), "at", (key("ab", n), 0), *pieces[key("A", n)]
            )
            swap(steps, key("qswap", n), key("iq", n))
            reduced[n]["A"] = scatter_steps(
                steps, place, key("A", n), (key("ab", n), 0), (key("head", n), 0), (key("att", n), 0), (key("jb", n), 1)
            )
        else:
            steps.run(key("iq", n), input_part, (key("ab", n), 0), weights[n][0])
            swap(steps, key("qswap", n), key("iq", n))
            steps.run(key("gQ", n), weight_grad, (key("ab", n), 0), (key("head", n), 0))
            steps.run(key("gO", n), weight_grad, (key("att", n), 0), (key("jb", n), 1))
        steps.run(
            key("jk", n), lambda up, own, got, h, norm: join_back(up, own, got, h, row(norm, 0, 0)),
            (key("jb", n), 0), key("iq", n), key("qswap", n), hidden_at[n], norm,
        )
        upstream, upstream_low = (key("jk", n), 0), (key("jk", n), 1)
        norm_parts[n] = steps.run(
            key("np", n), lambda a, b, c, d: jnp.stack([jnp.stack([a[0], b[0]]), jnp.stack([c[0], d[0]])]),
            (key("jk", n), 2), (key("jb", n), 2), (key("jk", n), 3), (key("jb", n), 3),
        )
        table_parts[n] = steps.run(
            key("tp", n),
            lambda d: jnp.einsum("db,hd->bh", onehot[::-1], d[:, 0, 1 : WIN + 1], precision=highest),
            (key("ab", n), 1),
        )

    steps.run("inlast", place.own_blocks, upstream_low)
    input_at = route_blocks(steps, place, "i", "inlast", True)

    def spread(values):
        empty = jnp.zeros_like(values)
        even = jnp.where(low_core, values, empty)
        odd = jnp.where(low_core, empty, values)
        return jnp.stack([even, odd], axis=-1).reshape(-1)

    sizes = [rel_table.size, head_total, LAYERS * 4 * model_width]
    ends = np.cumsum(sizes)
    room_total = -(-int(ends[-1]) // 1024) * 1024

    def flat(lower_table, upper_table, gates, gate, lower_norm, upper_norm):
        gate_part = jnp.sum(gates[:, 0], axis=-1) * gate * (1.0 - gate)
        parts = [
            spread(jnp.stack([lower_table, upper_table])),
            spread(gate_part),
            jnp.stack([lower_norm, upper_norm]).reshape(-1) * (1.0 / CORES),
        ]
        return jnp.concatenate(parts + [jnp.zeros((room_total - int(ends[-1]),), f32)]).reshape(-1, 128)

    sums = steps.run("sums", flat, table_parts[0], table_parts[1], ("ab1", 2), "gate", norm_parts[0], norm_parts[1])
    links = {(SEG, 1): "core", (BAT, 1): "x", (BAT, 2): "y"}
    for axis, count in ((SEG, place.segments), (BAT, place.batches)):
        bit = 1
        while bit < count:
            got = steps.send(
                key("u", axis[0], bit), links.get((axis, bit), "z"), lambda v, axis=axis, bit=bit: permuted(v, axis, lambda i: i ^ bit), sums
            )
            sums = steps.run(key("v", axis[0], bit), jnp.add, sums, got)
            bit *= 2

    if by_chip:
        done = {kind: finish_steps(steps, place, kind, reduced[0][kind], reduced[1][kind]) for kind in "DIA"}

    steps.carry_out(ORDER if by_chip and ORDER else range(len(steps.steps)))

    final = steps.value(sums).reshape(-1)
    table_sum = final[: ends[0]].reshape(rel_table.shape)
    gate_sum = final[ends[0] : ends[1]]
    norm_sum = final[ends[1] : ends[2]].reshape(LAYERS, 2, 2, place.chips, place.batches, norm_gain.shape[2])
    norm_sum = jnp.where(low_core, norm_sum[0], norm_sum[1])
    norm_sum = lax.dynamic_index_in_dim(norm_sum, place.stretch, 2, keepdims=False)
    norm_sum = lax.dynamic_index_in_dim(norm_sum, place.batch, 2, keepdims=False)
    if by_chip:
        halves = {kind: steps.value(name) for kind, name in done.items()}
        head = qkv_weight.shape[2] // 2
        matrices = [
            qkv_whole([h[:head] for h in halves["A"]])[None],
            out_whole([h[head:] for h in halves["A"]])[None],
            in_whole(halves["I"], 1)[None],
            down_whole(halves["D"], 1)[None],
        ]
    else:
        parts = [[steps.value(key("g", kind, n)) for kind in "QOID"] for n in range(LAYERS)]
        matrices = scatter_plain(parts, place.core)
    return (
        steps.value(mixed_at), steps.value(input_at), *matrices, norm_sum[0][None], norm_sum[1][None], table_sum, gate_sum,
    )


ORDER = (75, 76, 80, 71, 72, 85, 81, 83, 73, 53, 54, -77, 74, 60, 70, 56, -73, 61, 55, 0, -75, 1, 57, 58, 77, -62, 59, 78, -2, 2, -58, -79, 3, 79, -60, 37, 62, 63, 64, -4, 4, -65, 65, 68, -38, 12, 67, -5, 5, 69, -13, 13, -6, 20, 6, 7, 8, 66, -14, 14, -21, 21, -15, 28, 15, 16, -22, 17, -8, 22, -9, 10, -29, 9, -23, 82, 23, -83, 29, -17, 24, -18, 19, -30, 30, -10, 18, -11, 25, 11, 90, -31, 86, 31, -20, -87, 33, 45, -25, 32, 91, -46, -19, -26, 26, 27, 38, 92, -39, 93, -33, 39, -34, 35, -94, 34, 94, -40, 46, -27, 84, 40, -28, 41, 95, -47, -35, -36, 42, 47, 96, -85, -48, 97, 87, 88, 48, -42, -98, -89, 49, 44, -43, 50, 43, 89, 36, 98, -45, 99, -50, -44, 52, -51, 51, 100, 101, -102, 102, -53, 103, -52, 130, 131, 132, 115, 116, 117, 133, -133, 134, 135, 148, 149, -117, 119, -118, 121, 118, 120, -135, 137, -136, 139, 136, 138, 150, -122, -121, 153, 154, 155, 122, 151, 152, 104, -140, -139, -153, 105, 140, -156, -155, 141, 142, 157, -106, 159, 156, 158, -143, 143, 144, 123, 124, 170, 106, -145, 145, 146, 110, 108, 107, 168, -125, 111, 186, -147, -160, -159, 109, 187, -112, 188, 189, 190, 191, -110, 160, -189, 204, 161, 162, 171, -191, -192, 172, 173, -163, 192, 194, 163, 164, 193, -173, -165, -174, 195, 174, 176, 175, 177, 125, 126, 165, 205, 206, -127, -195, -196, 166, 196, 207, -167, 208, 197, 198, 209, -177, 210, -209, 211, 226, 167, -178, -199, 199, 200, 127, 128, 147, 178, 179, 224, -201, -211, -212, -129, 180, 213, 215, 212, -181, 214, 129, 201, 202, 181, 182, 227, 233, 231, 228, 229, 225, 169, 236, 237, 112, -203, 234, 203, -238, 250, 251, 238, -183, 230, -252, 252, -216, 183, -235, 184, -215, 216, -231, 232, 217, -185, 218, 185, 247, 248, -249, 249, -233, 113, 235, -219, 239, 219, -114, 220, -240, 114, 240, 241, -221, 221, -242, 222, 242, 243, -244, 244, 245, -223, 223, 253, 254, -246, 246, -255, 255)


def solution(mesh):
    placed = (
        P(BAT, SEG, None),
        P(BAT, None),
        P(BAT, SEG, None, None),
        P(SEG, None),
        P(SEG, None),
        P(SEG, None, BAT),
        P(SEG, None, BAT),
        P(SEG, None, BAT),
        P(SEG, None, BAT),
        P(SEG, None, BAT),
        P(SEG, None, BAT),
        P(),
        P(),
        P(BAT, SEG, None),
    )
    return jax.shard_map(
        on_device,
        mesh=mesh,
        in_specs=placed,
        out_specs=(
            P(BAT, SEG, None),
            P(BAT, SEG, None),
            P(SEG, None, BAT),
            P(SEG, None, BAT),
            P(SEG, None, BAT),
            P(SEG, None, BAT),
            P(SEG, None, BAT),
            P(SEG, None, BAT),
            P(),
            P(),
        ),
        check_vma=False,
    )
```

```python
import functools
import math

import jax
import jax.numpy as jnp
import numpy as np
from jax import lax
from jax.experimental import pallas as pl
from jax.experimental.pallas import tpu as pltpu
from jax.sharding import PartitionSpec as P

SEG, BAT = "segment", "batch"
WIN = 512
LAYERS = 2
CORES = 2
QB = 256

norm_eps = 1e-05
big_negative = -1e30
bucket_edges = np.ceil(16.0 * 8.0 ** (np.arange(1, 16) / 16.0)).astype(np.int32)
highest = lax.Precision.HIGHEST
f32 = jnp.float32
bf16 = jnp.bfloat16
VMEM_LIMIT = 20 * 1024 * 1024


def permuted(block, axis, route):
    count = lax.axis_size(axis)
    return lax.ppermute(block, axis, [(i, route(i)) for i in range(count)])


def core_swap(block):
    return permuted(block, SEG, lambda i: i ^ 1)


def room(tick):
    return pl.pallas_call(
        lambda source, result: None,
        out_shape=jax.ShapeDtypeStruct(tick.shape, tick.dtype),
        in_specs=[pl.BlockSpec(memory_space=pl.ANY)],
        out_specs=pl.BlockSpec(memory_space=pl.ANY),
        input_output_aliases={0: 0},
        cost_estimate=pl.CostEstimate(flops=200_000_000_000, transcendentals=0, bytes_accessed=0),
        name="room",
    )(tick)


def key(*parts):
    return "".join(map(str, parts))


class Steps:
    def __init__(self):
        self.steps = {}
        self.values = {}
        self.mark = ()
        self.tick = jnp.zeros((8, 128), f32)

    def given(self, name, value):
        self.values[name] = value
        return name

    def run(self, name, step, *sources):
        assert name not in self.steps, name
        self.steps[name] = ("run", step, sources)
        return name

    def send(self, name, link, transfer, *sources):
        assert name not in self.steps, name
        self.steps[name] = (link, transfer, sources)
        return name

    def value(self, source):
        if isinstance(source, tuple):
            return self.values[source[0]][source[1]]
        return self.values[source]

    def behind(self, values):
        leaves, tree = jax.tree.flatten(values)
        held = lax.optimization_barrier(tuple(leaves) + tuple(self.mark))
        return jax.tree.unflatten(tree, held[: len(leaves)])

    def wait(self, name):
        tick = room(self.behind(self.tick))
        leaves, tree = jax.tree.flatten(self.values[name])
        held = lax.optimization_barrier(tuple(leaves) + tuple(self.mark) + (tick,))
        self.tick = held[-1]
        self.mark = held[: len(leaves)]
        self.values[name] = jax.tree.unflatten(tree, self.mark)

    def carry_out(self, order):
        waited = set()
        names = list(self.steps)
        for number in order:
            name = names[number] if number >= 0 else names[-1 - number]
            if number < 0:
                waited.add(name)
                self.wait(name)
                continue
            kind, step, sources = self.steps[name]
            for source in sources:
                source = source[0] if isinstance(source, tuple) else source
                if source in self.steps and self.steps[source][0] != "run" and source not in waited:
                    waited.add(source)
                    self.wait(source)
            with jax.named_scope(name):
                result = step(*self.behind([self.value(source) for source in sources]))
            self.values[name] = result
            if kind == "run":
                self.mark = tuple(jax.tree.leaves(result))
        assert set(range(len(names))) <= set(order)


def pick(index, parts):
    return lax.select_n(index, *parts)


def total(*terms):
    return functools.reduce(jnp.add, [t.astype(f32) for t in terms])


def ring_step(block):
    count = lax.axis_size(SEG)
    return permuted(block, SEG, lambda i: (i + CORES) % count)


def in_order(parts, stretch):
    return [pick((stretch - k) % len(parts), parts) for k in range(len(parts))]


def swap_across(block):
    return permuted(block, BAT, lambda i: i ^ 1)


def swap_along(block):
    return permuted(block, BAT, lambda i: i ^ 2)


def cut_of(rows):
    return rows // 2 // 128 * 128


def qkv_half(matrix, core):
    rows, cols = matrix.shape
    return matrix.reshape(rows, cols // 256, 2, 128)[:, :, core].reshape(rows, cols // 2).T


def out_half(matrix, core):
    rows, cols = matrix.shape
    return matrix.reshape(rows // 256, 2, 128, cols)[:, core].reshape(rows // 2, cols)


def in_half(matrix, core, parts):
    rows, cols = matrix.shape
    return matrix.reshape(rows, parts, 2, cols // parts // 2)[:, :, core].reshape(rows, cols // 2).T


def down_half(matrix, core, parts):
    rows, cols = matrix.shape
    return matrix.reshape(parts, 2, rows // parts // 2, cols)[:, core].reshape(rows // 2, cols).T


def qkv_whole(halves):
    cols, rows = halves[0].shape
    stacked = jnp.stack([h.T.reshape(rows, cols // 128, 128) for h in halves], axis=2)
    return stacked.reshape(rows, 2 * cols)


def out_whole(halves):
    rows, cols = halves[0].shape
    stacked = jnp.stack([h.reshape(rows // 128, 128, cols) for h in halves], axis=1)
    return stacked.reshape(2 * rows, cols)


def in_whole(halves, parts):
    cols, rows = halves[0].shape
    stacked = jnp.stack([h.T.reshape(rows, parts, cols // parts) for h in halves], axis=2)
    return stacked.reshape(rows, 2 * cols)


def down_whole(halves, parts):
    cols, rows = halves[0].shape
    stacked = jnp.stack([h.T.reshape(parts, rows // parts, cols) for h in halves], axis=1)
    return stacked.reshape(2 * rows, cols)


def halves_of(parts):
    return (
        qkv_half,
        out_half,
        functools.partial(in_half, parts=parts),
        functools.partial(down_half, parts=parts),
    )


def gather_plain(shards, core):
    layers = ([], [])
    for shard, half in zip(shards, halves_of(4)):
        rows = lax.all_gather(shard, BAT, axis=1, tiled=True)
        slots = lax.all_gather(rows, SEG, axis=0, tiled=False)
        for layer in range(LAYERS):
            matrix = slots[layer::LAYERS].reshape(-1, rows.shape[1])
            layers[layer].append(jnp.where(core == 0, half(matrix, 0), half(matrix, 1)))
    return layers


def scatter_plain(parts, core):
    done = []
    slots = lax.axis_size(SEG)
    wholes = (qkv_whole, out_whole, functools.partial(in_whole, parts=4), functools.partial(down_whole, parts=4))
    for lower, upper, whole in zip(parts[0], parts[1], wholes):
        layers = []
        for half in (lower, upper):
            empty = jnp.zeros_like(half)
            matrix = whole((jnp.where(core == 0, half, empty), jnp.where(core == 0, empty, half)))
            layers.append(matrix.reshape(slots // LAYERS, -1, matrix.shape[1]))
        stacked = jnp.stack(layers, axis=1).reshape(slots, -1, layers[0].shape[2])
        rows = lax.psum_scatter(stacked, SEG, scatter_dimension=0, tiled=True)
        columns = lax.psum_scatter(rows, BAT, scatter_dimension=2, tiled=True)
        done.append(columns.astype(f32))
    return done


def spans(row_count, halo):
    for first in range(0, row_count, QB):
        start = max(0, first + halo - WIN)
        yield first, start, first + halo + QB - start


def mask_kernel(first_lane, chosen, index_ref, mask_ref):
    rows, slots = mask_ref.shape[1], mask_ref.shape[2]
    chunk = 64
    width = 256

    def body(first):
        index = index_ref[pl.ds(first, chunk), first_lane : first_lane + chosen]
        for low in range(0, slots, width):
            slot_ids = lax.broadcasted_iota(jnp.int32, (chunk, width), 1) + low
            bias = jnp.full((chunk, width), big_negative, f32)
            for t in range(chosen):
                bias = jnp.where(index[:, t : t + 1] == slot_ids, 0.0, bias)
            mask_ref[0, pl.ds(first, chunk), low : low + width] = bias.astype(bf16)

    chunks(rows, chunk, body)


def slot_mask(index, head, chosen, slots):
    out = jax.ShapeDtypeStruct((1, index.shape[0], slots), bf16)
    kernel = functools.partial(mask_kernel, head * chosen, chosen)
    return in_vmem(kernel, [out], None, [index], "slot_mask", 10_000_000_000)[0]


def nt_dot(left, right):
    return lax.dot_general(left, right, (((1,), (1,)), ((), ())), preferred_element_type=f32)


def tn_dot(left, right):
    return lax.dot_general(left, right, (((0,), (0,)), ((), ())), preferred_element_type=f32)


def nn_dot(left, right):
    return lax.dot_general(left, right, (((1,), (0,)), ((), ())), preferred_element_type=f32)


def forward_kernel(halo, with_memory, scale, *refs):
    refs = list(refs)
    bias_ref, docs_col, docs_row, q_ref, k_ref, v_ref = refs[:6]
    del refs[:6]
    if halo:
        k_halo, v_halo = refs[:2]
        del refs[:2]
    if with_memory:
        mem_k, mem_v, mask_ref, gate_ref = refs[:4]
        del refs[:4]
        o_ref, probs_ref, slots_ref, differ_ref = refs[:4]
        del refs[:4]
    else:
        o_ref, probs_ref = refs[:2]
        del refs[:2]
    if halo:
        keys, values = refs
        keys[:halo] = k_halo[...]
        keys[halo:] = k_ref[...]
        values[:halo] = v_halo[...]
        values[halo:] = v_ref[...]
    else:
        keys, values = k_ref, v_ref
    width = WIN + QB
    lanes = bias_ref.shape[2]
    tile = pltpu.roll(
        jnp.broadcast_to(bias_ref[0], (QB, lanes)), 0, axis=1, stride=1, stride_axis=0
    )[:, :width]
    if with_memory:
        opened = gate_ref[pl.program_id(0)]
    for first, start, count in spans(q_ref.shape[0], halo):
        rows = slice(first, first + QB)
        query = q_ref[rows]
        scores = nt_dot(query, keys[start : start + count]) * scale + tile[:, width - count :]
        same = docs_col[rows] == docs_row[:, start : start + count]
        scores = jnp.where(same, scores, big_negative)
        raised = jnp.exp(scores - jnp.max(scores, axis=-1, keepdims=True))
        probs = (raised * (1.0 / jnp.sum(raised, axis=-1, keepdims=True))).astype(bf16)
        probs_ref[0, rows, width - count :] = probs
        local = nn_dot(probs, values[start : start + count])
        if with_memory:
            picked = nt_dot(query, mem_k[...]) * scale + mask_ref[0, rows].astype(f32)
            raised = jnp.exp(picked - jnp.max(picked, axis=-1, keepdims=True))
            slot_probs = (raised * (1.0 / jnp.sum(raised, axis=-1, keepdims=True))).astype(bf16)
            slots_ref[0, rows] = slot_probs
            differ = nn_dot(slot_probs, mem_v[...]) - local
            differ_ref[rows] = differ.astype(bf16)
            local = local + opened * differ
        o_ref[rows] = local.astype(bf16)


def backward_kernel(halo, with_memory, scale, *refs):
    refs = list(refs)
    q_ref, k_ref, v_ref, do_ref, probs_ref = refs[:5]
    del refs[:5]
    if halo:
        k_halo, v_halo = refs[:2]
        del refs[:2]
    if with_memory:
        mem_k, mem_v, slots_ref, differ_ref, gate_ref = refs[:5]
        del refs[:5]
    d_ref, table_ref = refs[:2]
    del refs[:2]
    if with_memory:
        gate_grad = refs.pop(0)
    if halo:
        halo_grad = refs.pop(0)
    dk, dv, table = refs[:3]
    del refs[:3]
    if halo:
        keys, values = refs
        keys[:halo] = k_halo[...]
        keys[halo:] = k_ref[...]
        values[:halo] = v_halo[...]
        values[halo:] = v_ref[...]
    else:
        keys, values = k_ref, v_ref
    head = pl.program_id(0)
    heads = pl.num_programs(0)
    row_count, head_dim = q_ref.shape
    width = WIN + QB
    lanes = table.shape[1]
    dk[...] = jnp.zeros_like(dk)
    dv[...] = jnp.zeros_like(dv)
    table[...] = jnp.zeros_like(table)
    if with_memory:
        opened = gate_ref[head]
        gate_sum = jnp.zeros((1, head_dim), f32)
    here = pl.multiple_of(head * head_dim, head_dim)
    for first, start, count in spans(row_count, halo):
        rows = slice(first, first + QB)
        cols = slice(start, start + count)
        upstream = do_ref[rows]
        if with_memory:
            wide = upstream.astype(f32)
            gate_sum += jnp.sum(wide * differ_ref[rows].astype(f32), axis=0, keepdims=True)
            mem_grad = (opened * wide).astype(bf16)
            upstream = ((1.0 - opened) * wide).astype(bf16)
        probs = probs_ref[0, rows, width - count :]
        probs_wide = probs.astype(f32)
        grad = nt_dot(upstream, values[cols])
        inner = jnp.sum(probs_wide * grad, axis=-1, keepdims=True)
        score_wide = probs_wide * (grad - inner)
        score = score_wide.astype(bf16)
        table[:, width - count : width] += score_wide
        dq = nn_dot(score, keys[cols])
        dk[cols] += tn_dot(score, q_ref[rows])
        dv[cols] += tn_dot(probs, upstream)
        if with_memory:
            slot_probs = slots_ref[0, rows].astype(f32)
            slot_grad = nt_dot(mem_grad, mem_v[...])
            slot_score = slot_probs * (
                slot_grad - jnp.sum(slot_probs * slot_grad, axis=-1, keepdims=True)
            )
            dq += nn_dot(slot_score.astype(bf16), mem_k[...])
        d_ref[rows, pl.ds(here, head_dim)] = (dq * scale).astype(bf16)
    key_at = pl.multiple_of((heads + head) * head_dim, head_dim)
    value_at = pl.multiple_of((2 * heads + head) * head_dim, head_dim)
    if halo:
        halo_grad[0] = (dk[:halo] * scale).astype(bf16)
        halo_grad[1] = dv[:halo].astype(bf16)
    d_ref[:, pl.ds(key_at, head_dim)] = (dk[halo:] * scale).astype(bf16)
    d_ref[:, pl.ds(value_at, head_dim)] = dv[halo:].astype(bf16)
    turned = jnp.zeros((8, lanes), f32)
    for row in range(0, QB, 8):
        part = table[row : row + 8]
        turned += pltpu.roll(part, lanes - row, axis=1) if row else part
    total = turned[:1]
    for row in range(1, 8):
        total += pltpu.roll(turned, lanes - row, axis=1)[row : row + 1]
    table_ref[0] = total
    if with_memory:
        gate_grad[0] = gate_sum


def smooth_pair(pre):
    rate = math.sqrt(2.0 / math.pi)
    square = pre * pre
    turn = jnp.tanh(pre * (rate + (rate * 0.044715) * square))
    half = 0.5 + 0.5 * turn
    bend = pre * (rate + (rate * 3 * 0.044715) * square)
    return (pre * half).astype(bf16), (half + bend * (half - half * half) * 2.0).astype(bf16)


def norm_rows_of(values):
    center = values - jnp.mean(values, axis=-1, keepdims=True)
    factor = lax.rsqrt(jnp.mean(center * center, axis=-1, keepdims=True) + norm_eps)
    return center * factor, factor


def in_vmem(kernel, outs, scalars, operands, name, flops):
    vmem = pl.BlockSpec(memory_space=pltpu.VMEM)
    return pl.pallas_call(
        kernel,
        out_shape=outs,
        in_specs=([smem_block] if scalars is not None else []) + [vmem] * len(operands),
        out_specs=[vmem] * len(outs),
        compiler_params=pltpu.CompilerParams(vmem_limit_bytes=8 * 1024 * 1024),
        cost_estimate=pl.CostEstimate(flops=3 * flops, transcendentals=0, bytes_accessed=0),
        name=name,
    )(*([scalars] if scalars is not None else []), *operands)


smem_block = pl.BlockSpec(memory_space=pltpu.SMEM)


def chunks(count, size, body):
    def step(turn, carry):
        body(pl.multiple_of(turn * size, size))
        return carry

    lax.fori_loop(0, count // size, step, 0)


def segments(refs, low, high):
    for which, ref in enumerate(refs[:3]):
        yield which, 0, ref, low, high
    cut = refs[3].shape[0]
    if low < cut:
        yield 3, 0, refs[3], low, min(high, cut)
    if high > cut:
        yield 3, max(cut - low, 0), refs[4], max(low - cut, 0), high - cut


def place_of(at_ref, which, width, offset=0):
    return pl.multiple_of((at_ref[0] ^ which) * width + offset, 128)


def norm_kernel(row, part, at_ref, own_ref, across_ref, along_ref, low_ref, high_ref, out_ref):
    rows = [ref[row : row + 1, :].astype(f32) for ref in (own_ref, across_ref, along_ref)]
    rows.append(high_ref[row - low_ref.shape[0] : row - low_ref.shape[0] + 1, :].astype(f32))
    width = 4 * part
    chips = rows[0].shape[1] // width
    for k in range(4):
        which = at_ref[0] ^ k
        row_k = jnp.where(
            which < 2, jnp.where(which == 0, rows[0], rows[1]), jnp.where(which == 2, rows[2], rows[3])
        )
        for z in range(chips):
            for kind in range(4):
                first = z * width + kind * part
                out_ref[kind : kind + 1, z * width + k * part : z * width + (k + 1) * part] = row_k[:, first : first + part]


def norm_rows_by_pieces(at, row, part, pieces):
    out = jax.ShapeDtypeStruct((4, pieces[0].shape[1]), f32)
    return in_vmem(functools.partial(norm_kernel, row, part), [out], at, list(pieces), "norm", 1000)[0]


def head_kernel(joins, width, at_ref, *refs):
    hidden_ref, *refs = refs
    if joins:
        own_ref, got_ref, *refs = refs
    gain_ref, shift_ref, *refs = refs
    pieces, (normed_ref, out_ref), refs = refs[:5], refs[5:7], refs[7:]
    parts = list(segments(pieces, 0, width))

    def body(first):
        rows = pl.ds(first, 256)
        values = hidden_ref[rows, :]
        if joins:
            values = values + (own_ref[rows, :].astype(f32) + got_ref[rows, :].astype(f32))
            refs[0][rows, :] = values
        normal, _ = norm_rows_of(values)
        normed = (normal * gain_ref[...] + shift_ref[...]).astype(bf16)
        normed_ref[rows, :] = normed
        for which, offset, ref, low, high in parts:
            cols = pl.ds(place_of(at_ref, which, width, offset), high - low)
            out_ref[rows, cols] = nt_dot(normed, ref[low:high]).astype(bf16)

    chunks(hidden_ref.shape[0], 256, body)


def head_by_pieces(at, width, hidden, joins, gain, shift, pieces):
    rows, inner = hidden.shape
    outs = [jax.ShapeDtypeStruct((rows, inner), bf16), jax.ShapeDtypeStruct((rows, 4 * width), bf16)]
    if joins:
        outs.append(jax.ShapeDtypeStruct((rows, inner), f32))
    operands = [hidden, *joins, gain, shift, *pieces]
    return in_vmem(
        functools.partial(head_kernel, bool(joins), width), outs, at, operands, "head", 8 * rows * inner * width
    )


def by_columns_kernel(smooth, at_ref, rows_ref, *refs):
    pieces, outs = refs[:5], refs[5:]
    width = pieces[0].shape[0]
    parts = list(segments(pieces, 0, width))

    def body(first):
        rows = pl.ds(first, 256)
        for which, offset, ref, low, high in parts:
            cols = pl.ds(place_of(at_ref, which, width, offset), high - low)
            product = nt_dot(rows_ref[rows, :], ref[low:high])
            if smooth:
                outs[0][rows, cols], outs[1][rows, cols] = smooth_pair(product)
            else:
                outs[0][rows, cols] = product.astype(bf16)

    chunks(rows_ref.shape[0], 256, body)


def by_columns(at, rows, pieces, smooth):
    count, inner = rows.shape
    width = pieces[0].shape[0]
    outs = [jax.ShapeDtypeStruct((count, 4 * width), bf16)] * (2 if smooth else 1)
    return in_vmem(
        functools.partial(by_columns_kernel, smooth), outs, at, [rows, *pieces], "expand" if smooth else "down",
        8 * count * inner * width,
    )


def out_kernel(first, rows_per, width, at_ref, rows_ref, *refs):
    pieces, out_ref = refs[:5], refs[5]
    parts = list(segments(pieces, first, first + rows_per))

    def body(start):
        rows = pl.ds(start, 256)
        for which, _, ref, low, high in parts:
            acc = None
            for z in range(rows_ref.shape[1] // rows_per):
                part = nn_dot(
                    rows_ref[rows, z * rows_per : (z + 1) * rows_per], ref[low:high, z * width : (z + 1) * width]
                )
                acc = part if acc is None else acc + part
            out_ref[rows, pl.ds(place_of(at_ref, which, width), width)] = acc.astype(bf16)

    chunks(rows_ref.shape[0], 256, body)


def out_by_pieces(at, first, rows_per, width, attended, pieces):
    count = attended.shape[0]
    outs = [jax.ShapeDtypeStruct((count, 4 * width), bf16)]
    return in_vmem(
        functools.partial(out_kernel, first, rows_per, width), outs, at, [attended, *pieces], "out",
        8 * count * attended.shape[1] * width,
    )[0]


def by_rows_kernel(low, high, scaled, at_ref, rows_ref, *refs):
    pieces, refs = refs[:5], refs[5:]
    out_ref = refs[-1]
    span = high - low
    parts = list(segments(pieces, low, high))
    block = 512

    def body(start):
        rows = pl.ds(start, 256)
        for n in range(0, out_ref.shape[1], block):
            cols = slice(n, n + block)
            acc = None
            for which, offset, ref, first, last in parts:
                inner = pl.ds(place_of(at_ref, which, span, offset), last - first)
                part = nn_dot(rows_ref[rows, inner], ref[first:last, cols])
                acc = part if acc is None else acc + part
            if scaled:
                acc = acc * refs[0][rows, cols].astype(f32)
            out_ref[rows, cols] = acc.astype(bf16)

    chunks(rows_ref.shape[0], 256, body)


def by_rows(at, low, high, grad, pieces, slope=None):
    count = grad.shape[0]
    cols = pieces[0].shape[1]
    operands = [grad, *pieces] + ([] if slope is None else [slope])
    return in_vmem(
        functools.partial(by_rows_kernel, low, high, slope is not None),
        [jax.ShapeDtypeStruct((count, cols), bf16)], at, operands, "by_rows", 2 * count * grad.shape[1] * cols,
    )[0]


def attended_back_kernel(first, rows_per, width, at_ref, grad_ref, *refs):
    pieces, out_ref = refs[:5], refs[5]
    parts = list(segments(pieces, first, first + rows_per))

    def body(start):
        rows = pl.ds(start, 256)
        for z in range(out_ref.shape[1] // rows_per):
            acc = None
            for which, _, ref, low, high in parts:
                grad = grad_ref[rows, pl.ds(place_of(at_ref, which, width), width)]
                part = nt_dot(grad, ref[low:high, z * width : (z + 1) * width])
                acc = part if acc is None else acc + part
            out_ref[rows, z * rows_per : (z + 1) * rows_per] = acc.astype(bf16)

    chunks(grad_ref.shape[0], 256, body)


def attended_back(at, first, rows_per, width, grad, pieces):
    count = grad.shape[0]
    chips = pieces[0].shape[1] // width
    return in_vmem(
        functools.partial(attended_back_kernel, first, rows_per, width),
        [jax.ShapeDtypeStruct((count, chips * rows_per), bf16)], at, [grad, *pieces], "attended_back",
        2 * count * grad.shape[1] * chips * rows_per,
    )[0]


def share_kernel(which, heads, adds, at_ref, *refs):
    left_ref, right_ref, *refs = refs
    if heads:
        attended_ref, grad_ref, *refs = refs
    count = {"": 0, "low": 1, "high": 1, "both": 2}[adds]
    got, outs = refs[:count], refs[count:]
    chips = 4
    rows, width = left_ref.shape[1] // 4, right_ref.shape[1] // chips
    own = which == 0
    left = left_ref[:, pl.ds(place_of(at_ref, which, rows), rows)]
    if heads:
        more = attended_ref.shape[1] // chips
        grad = grad_ref[:, pl.ds(place_of(at_ref, which, grad_ref.shape[1] // 4), grad_ref.shape[1] // 4)]

    def body(n):
        column = lax.rem(at_ref[1] + (3 * chips - 1) - n, chips) if own else n
        cols = pl.ds(pl.multiple_of(column * width, width), width)
        value = tn_dot(left, right_ref[:, cols])
        if heads:
            part = tn_dot(attended_ref[:, pl.ds(pl.multiple_of(column * more, more), more)], grad)
            value = jnp.concatenate([value, part], axis=0)
        half = value.shape[0] // 2
        if adds == "low":
            value = jnp.concatenate([value[:half] + got[0][:, cols].astype(f32), value[half:]], axis=0)
        elif adds == "high":
            value = jnp.concatenate([value[:half], value[half:] + got[0][:, cols].astype(f32)], axis=0)
        elif adds == "both":
            value = value + got[0][:, cols].astype(f32) + got[1][:, cols].astype(f32)
        value = value.astype(bf16)
        if which == 3:
            outs[0][:, cols], outs[1][:, cols] = value[:half], value[half:]
        elif own:
            outs[0][n] = value
        else:
            outs[0][:, cols] = value

    def step(n, carry):
        body(n)
        return carry

    lax.fori_loop(0, chips, step, 0)


def share_grad(at, which, left, right, head_pair=(), adds="", got=()):
    chips = 4
    rows, cols = left.shape[1] // 4, right.shape[1]
    if head_pair:
        rows += head_pair[0].shape[1] // chips
    if which == 3:
        outs = [jax.ShapeDtypeStruct((rows // 2, cols), bf16)] * 2
    elif which == 0:
        outs = [jax.ShapeDtypeStruct((chips, rows, cols // chips), bf16)]
    else:
        outs = [jax.ShapeDtypeStruct((rows, cols), bf16)]
    return in_vmem(
        functools.partial(share_kernel, which, bool(head_pair), adds), outs, at, [left, right, *head_pair, *got],
        "share", 2 * left.shape[0] * rows * cols,
    )


def join_norm_kernel(hidden_ref, own_ref, got_ref, gain_ref, shift_ref, result_ref, normed_ref):
    def body(first):
        rows = pl.ds(first, 128)
        values = hidden_ref[rows, :] + (own_ref[rows, :].astype(f32) + got_ref[rows, :].astype(f32))
        result_ref[rows, :] = values
        normal, _ = norm_rows_of(values)
        normed_ref[rows, :] = (normal * gain_ref[...] + shift_ref[...]).astype(bf16)

    chunks(hidden_ref.shape[0], 128, body)


def join_norm(hidden, own, got, gain, shift):
    outs = [jax.ShapeDtypeStruct(hidden.shape, f32), jax.ShapeDtypeStruct(hidden.shape, bf16)]
    return in_vmem(join_norm_kernel, outs, None, [hidden, own, got, gain, shift], "join_norm", 10 * hidden.size)


def join_back_kernel(up_ref, own_ref, got_ref, values_ref, gain_ref, result_ref, low_ref, gain_grad, shift_grad):
    gain_grad[...] = jnp.zeros_like(gain_grad)
    shift_grad[...] = jnp.zeros_like(shift_grad)

    def body(first):
        rows = pl.ds(first, 128)
        upstream = own_ref[rows, :].astype(f32) + got_ref[rows, :].astype(f32)
        normal, factor = norm_rows_of(values_ref[rows, :])
        gain_grad[...] += jnp.sum(upstream * normal, axis=0, keepdims=True)
        shift_grad[...] += jnp.sum(upstream, axis=0, keepdims=True)
        scaled = upstream * gain_ref[...]
        inner = (
            scaled
            - jnp.mean(scaled, axis=-1, keepdims=True)
            - normal * jnp.mean(scaled * normal, axis=-1, keepdims=True)
        )
        result = up_ref[rows, :].astype(f32) + factor * inner
        result_ref[rows, :] = result
        low_ref[rows, :] = result.astype(bf16)

    chunks(values_ref.shape[0], 128, body)


def join_back(upstream, own, got, values, gain):
    row = jax.ShapeDtypeStruct((1, values.shape[1]), f32)
    outs = [jax.ShapeDtypeStruct(values.shape, f32), jax.ShapeDtypeStruct(values.shape, bf16), row, row]
    return in_vmem(join_back_kernel, outs, None, [upstream, own, got, values, gain], "join_back", 20 * values.size)


def head_block(rows, head_dim, offset):
    return pl.BlockSpec((rows, head_dim), lambda h: (0, offset + h))


def plane_block(rows, cols):
    return pl.BlockSpec((1, rows, cols), lambda h: (h, 0, 0))


def attend(projected, bias_rows, docs_col, docs_row, halo_rows, memory, scale):
    row_count = projected.shape[0]
    head_count, _, lanes = bias_rows.shape
    head_dim = projected.shape[1] // (3 * head_count)
    halo = 0 if halo_rows is None else halo_rows.shape[1]
    width = WIN + QB
    operands = [bias_rows, docs_col, docs_row, projected, projected, projected]
    specs = [
        plane_block(1, lanes),
        pl.BlockSpec(docs_col.shape, lambda h: (0, 0)),
        pl.BlockSpec(docs_row.shape, lambda h: (0, 0)),
        head_block(row_count, head_dim, 0),
        head_block(row_count, head_dim, head_count),
        head_block(row_count, head_dim, 2 * head_count),
    ]
    scratch = []
    if halo:
        operands += [halo_rows[0], halo_rows[1]]
        specs += [head_block(halo, head_dim, 0)] * 2
        scratch = [pltpu.VMEM((halo + row_count, head_dim), bf16)] * 2
    outs = [
        jax.ShapeDtypeStruct((row_count, head_count * head_dim), bf16),
        jax.ShapeDtypeStruct((head_count, row_count, width), bf16),
    ]
    out_specs = [head_block(row_count, head_dim, 0), plane_block(row_count, width)]
    flops = 4 * head_count * row_count * width * head_dim
    if memory is not None:
        mem_keys, mem_values, masks, gate = memory
        slots = mem_keys.shape[0]
        mask = jnp.concatenate(masks, axis=0)
        operands += [mem_keys, mem_values, mask, gate]
        specs += [head_block(slots, head_dim, 0)] * 2 + [plane_block(row_count, slots), smem_block]
        outs += [
            jax.ShapeDtypeStruct((head_count, row_count, slots), bf16),
            jax.ShapeDtypeStruct((row_count, head_count * head_dim), bf16),
        ]
        out_specs += [plane_block(row_count, slots), head_block(row_count, head_dim, 0)]
        flops += 4 * head_count * row_count * slots * head_dim
    return pl.pallas_call(
        functools.partial(forward_kernel, halo, memory is not None, scale),
        out_shape=outs,
        grid=(head_count,),
        in_specs=specs,
        out_specs=out_specs,
        scratch_shapes=scratch,
        compiler_params=pltpu.CompilerParams(vmem_limit_bytes=VMEM_LIMIT),
        cost_estimate=pl.CostEstimate(
            flops=flops, transcendentals=head_count * row_count * width, bytes_accessed=16 * 1024 * 1024
        ),
        name="attend",
    )(*operands)


def attend_back(projected, grad, probs, halo_rows, memory, scale):
    row_count = projected.shape[0]
    head_count, _, width = probs.shape
    head_dim = projected.shape[1] // (3 * head_count)
    halo = 0 if halo_rows is None else halo_rows.shape[1]
    lanes = 1024
    operands = [projected, projected, projected, grad, probs]
    specs = [
        head_block(row_count, head_dim, 0),
        head_block(row_count, head_dim, head_count),
        head_block(row_count, head_dim, 2 * head_count),
        head_block(row_count, head_dim, 0),
        plane_block(row_count, width),
    ]
    scratch = [
        pltpu.VMEM((halo + row_count, head_dim), f32),
        pltpu.VMEM((halo + row_count, head_dim), f32),
        pltpu.VMEM((QB, lanes), f32),
    ]
    if halo:
        operands += [halo_rows[0], halo_rows[1]]
        specs += [head_block(halo, head_dim, 0)] * 2
        scratch += [pltpu.VMEM((halo + row_count, head_dim), bf16)] * 2
    outs = [
        jax.ShapeDtypeStruct(projected.shape, bf16),
        jax.ShapeDtypeStruct((head_count, 1, lanes), f32),
    ]
    out_specs = [pl.BlockSpec(projected.shape, lambda h: (0, 0)), plane_block(1, lanes)]
    flops = 8 * head_count * row_count * width * head_dim
    if memory is not None:
        mem_keys, mem_values, slot_probs, differ, gate = memory
        slots = mem_keys.shape[0]
        operands += [mem_keys, mem_values, slot_probs, differ, gate]
        specs += [head_block(slots, head_dim, 0)] * 2
        specs += [plane_block(row_count, slots), head_block(row_count, head_dim, 0), smem_block]
        outs += [jax.ShapeDtypeStruct((head_count, 1, head_dim), f32)]
        out_specs += [plane_block(1, head_dim)]
        flops += 4 * head_count * row_count * slots * head_dim
    if halo:
        outs += [jax.ShapeDtypeStruct((2, halo, head_count * head_dim), bf16)]
        out_specs += [pl.BlockSpec((2, halo, head_dim), lambda h: (0, 0, h))]
    return pl.pallas_call(
        functools.partial(backward_kernel, halo, memory is not None, scale),
        out_shape=outs,
        grid=(head_count,),
        in_specs=specs,
        out_specs=out_specs,
        scratch_shapes=scratch,
        compiler_params=pltpu.CompilerParams(vmem_limit_bytes=VMEM_LIMIT),
        cost_estimate=pl.CostEstimate(
            flops=flops, transcendentals=0, bytes_accessed=20 * 1024 * 1024
        ),
        name="attend_back",
    )(*operands)


def bucket_of(distance):
    beyond = jnp.sum((distance[..., None] >= jnp.asarray(bucket_edges)).astype(jnp.int32), axis=-1)
    return jnp.where(distance < 16, distance, 16 + beyond)


def distance_onehot(bucket_count):
    bucket = bucket_of(jnp.arange(WIN, dtype=jnp.int32))
    return (bucket[:, None] == jnp.arange(bucket_count, dtype=jnp.int32)).astype(f32)


def normalize(values):
    center = values - jnp.mean(values, axis=-1, keepdims=True)
    factor = lax.rsqrt(jnp.mean(center * center, axis=-1, keepdims=True) + norm_eps)
    return center * factor, factor


def head_in(hidden, gain, shift, qkv):
    normal, _ = normalize(hidden)
    normed = (normal * gain + shift).astype(bf16)
    return normed, nt_dot(normed, qkv).astype(bf16)


def out_part(attended, out):
    return nn_dot(attended, out).astype(bf16)


def down_part(active, down):
    return nt_dot(active, down).astype(bf16)


def joined(hidden, own, got):
    return hidden + (own.astype(f32) + got.astype(f32))


def weight_grad(left, right):
    return tn_dot(left, right).astype(bf16)


def expand_back(upstream, down, slope):
    return (nn_dot(upstream, down) * slope.astype(f32)).astype(bf16)


def input_part(grad, weight):
    return nn_dot(grad, weight).astype(bf16)


class Place:
    def __init__(self, seq_count):
        self.segments = lax.axis_size(SEG)
        self.batches = lax.axis_size(BAT)
        self.chips = self.segments // CORES
        self.seqs = seq_count
        self.pairs = self.chips // seq_count
        here = lax.axis_index(SEG)
        self.batch = lax.axis_index(BAT)
        self.core = here % CORES
        self.stretch = here // CORES
        self.low = self.core == 0
        self.seq_no = self.stretch // self.pairs
        self.place_no = self.stretch % seq_count

    def both(self, own, got):
        return jnp.where(self.low, own, got), jnp.where(self.low, got, own)


    def route(self, turn):
        pairs = []
        for source in range(self.segments):
            chip, lane = divmod(source, CORES)
            group, place = divmod(chip, self.seqs)
            pairs.append((source, (((place + turn) % self.seqs) * self.pairs + group) * CORES + lane))
        return pairs

    def local(self, turn):
        return self.pairs == 1 and turn == 0

    def out_block(self, stored, turn):
        return lax.dynamic_index_in_dim(stored, (self.place_no + turn) % self.seqs, 0, keepdims=False)

    def back_block(self, blocks, turn):
        return lax.dynamic_index_in_dim(blocks, (self.seq_no - turn) % self.seqs, 0, keepdims=False)

    def owned(self, *got):
        return jnp.stack([pick((self.seq_no - place) % self.seqs, got) for place in range(self.seqs)])

    def stored(self, *got):
        return jnp.stack([pick((number - self.place_no) % self.seqs, got) for number in range(self.seqs)])

    def sequence(self, own, got):
        pair = jnp.stack(self.both(own, got), axis=1)
        return pair.reshape((-1,) + own.shape[2:])

    def own_blocks(self, rows):
        split = rows.reshape(self.seqs, CORES, -1, rows.shape[1])
        return jnp.where(self.low, split[:, 0], split[:, 1])


def route_blocks(steps, place, name, source, back=False):
    got = []
    for turn in range(place.seqs):
        block = steps.run(key(name, "b", turn), lambda v, t=turn: (place.back_block if back else place.out_block)(v, t), source)
        if not place.local(turn):
            route = place.route(turn)
            if back:
                route = [(there, here) for here, there in route]
            block = steps.send(
                key(name, turn), key("z", turn), lambda v, route=tuple(route): lax.ppermute(v, SEG, route), block
            )
        got.append(block)
    return steps.run(key(name, "own"), place.stored if back else place.owned, *got)


def swap(steps, name, source):
    return steps.send(name, "core", core_swap, source)


def gather_steps(steps, place, shards, norm_rows, memory):
    qkv, out, inner, down = shards
    width = qkv.shape[0]
    gain_cols = norm_rows.shape[-1]
    slots = memory.shape[3]
    head, outs, hidden = qkv.shape[1] // 2, out.shape[0] // 2, inner.shape[1] // 2
    ends = np.cumsum([head + outs + 16, hidden, 2 * down.shape[1], memory[0].size // width])
    chips = place.chips

    def packed(core, qkv, out, inner, down, norm_rows, memory):
        down_rows = down_half(down, core, 1)
        return jnp.concatenate(
            [
                qkv_half(qkv, core),
                out_half(out, core),
                jnp.pad(norm_rows.reshape(1, width), ((0, 15), (0, 0))),
                in_half(inner, core, 1),
                down_rows[:, :width],
                down_rows[:, width:],
                memory_rows_of(memory[core]),
            ],
            axis=0,
        )

    def memory_rows_of(memory):
        return jnp.concatenate(
            [memory[kind, 0, :, at : at + width] for kind in range(2) for at in range(0, memory.shape[3], width)], axis=0
        )

    def first(*arrays):
        low, high = packed(0, *arrays), packed(1, *arrays)
        return jnp.where(place.low, low, high), jnp.where(place.low, high, low)

    for name, array in zip(("qkv", "out", "inner", "down", "norm", "mem"), (*shards, norm_rows, memory)):
        steps.given(name, array)
    steps.run("pack", first, "qkv", "out", "inner", "down", "norm", "mem")
    swap(steps, "wswap", ("pack", 1))

    def blocks(own, got):
        lower, upper = place.both(own, got)
        kept = []
        for layer in (lower, upper):
            kept += [layer[: ends[0]], layer[ends[0] : ends[1]], layer[ends[1] : ends[2]]]
        memory_rows = jnp.concatenate([lower[ends[2] :], upper[ends[2] :]], axis=0)
        kept[3] = jnp.concatenate([kept[3], memory_rows], axis=0)
        return kept

    steps.run("blocks", blocks, ("pack", 0), "wswap")

    def formed(unit, *ring):
        parts = in_order(ring, place.stretch)
        if unit[0] == "A":
            rows = jnp.concatenate([p[: ends[0]] for p in parts], axis=1)
            if unit == "A0":
                return (rows,)
            halves = memory.shape[4] // width
            block = 2 * halves * slots
            whole = []
            for kind in range(2):
                cols = []
                for half in range(halves):
                    first = ends[0] + (kind * halves + half) * slots
                    cols.append(
                        jnp.concatenate(
                            [p[first + c * block : first + c * block + slots] for p in parts for c in range(CORES)], axis=0
                        )
                    )
                whole.append(jnp.concatenate(cols, axis=1))
            return rows, jnp.stack(whole)
        if unit[0] == "I":
            return (jnp.concatenate(parts, axis=1),)
        half = parts[0].shape[0] // 2
        return (jnp.concatenate([q for p in parts for q in (p[:half], p[half:])], axis=1),)

    def norm_of(at, *pieces):
        return norm_rows_by_pieces(at, head + outs, gain_cols, pieces)

    pieces = {}
    for number, unit in enumerate(("A0", "I0", "D0", "A1", "I1", "D1")):
        ring = [("blocks", number)]
        for turn in range(1, chips):
            ring.append(steps.send(key("z", turn, unit), "z", ring_step, ring[-1]))
        steps.run(key("form", unit), functools.partial(formed, unit), *ring)
        block = (key("form", unit), 0)
        steps.send(key("px", unit), "x", swap_across, block)
        steps.send(key("py", unit), "y", swap_along, block)
        steps.send(key("fx", unit), "x", lambda along: swap_across(along[: cut_of(along.shape[0])]), key("py", unit))
        steps.send(key("fy", unit), "y", lambda across: swap_along(across[cut_of(across.shape[0]) :]), key("px", unit))
        pieces[unit] = (block, key("px", unit), key("py", unit), key("fx", unit), key("fy", unit))
        if unit[0] == "A":
            steps.run(key("norm", unit[1]), norm_of, "at", *pieces[unit])
    return pieces, ("formA1", 1), (head, outs, width)


def scatter_steps(steps, place, unit, left, right, *head_pair):
    heads = bool(head_pair)

    def shares(which, adds):
        def step(at, left, right, *rest):
            pair, got = (rest[:2], rest[2:]) if heads else ((), rest)
            return share_grad(at, which, left, right, pair, adds, got)

        return step

    sources = ("place", left, right, *head_pair)
    steps.run(key("ra", unit), shares(3, ""), *sources)
    steps.send(key("rx", unit), "x", swap_across, (key("ra", unit), 0))
    steps.send(key("ry", unit), "y", swap_along, (key("ra", unit), 1))
    steps.run(key("rb", unit), shares(1, "high"), *sources, key("ry", unit))
    steps.run(key("rc", unit), shares(2, "low"), *sources, key("rx", unit))
    steps.send(key("sx", unit), "x", swap_across, (key("rb", unit), 0))
    steps.send(key("sy", unit), "y", swap_along, (key("rc", unit), 0))
    steps.run(key("rd", unit), shares(0, "both"), *sources, key("sx", unit), key("sy", unit))
    own = (key("rd", unit), 0)
    travelling = steps.run(key("a0", unit), lambda parts: parts[0], own)
    for turn in range(1, place.chips):
        steps.send(key("q", turn, unit), "z", ring_step, travelling)
        last = turn == place.chips - 1
        travelling = steps.run(
            key("a", turn, unit),
            lambda got, parts, turn=turn, last=last: total(got, parts[turn]) if last else total(got, parts[turn]).astype(bf16),
            key("q", turn, unit),
            own,
        )
    return travelling


def finish_steps(steps, place, kind, lower, upper):
    steps.run(key("e", kind), lambda a, b: jnp.where(place.low, b, a).astype(bf16), lower, upper)
    swap(steps, key("eswap", kind), key("e", kind))

    def both(lower, upper, got):
        return place.both(jnp.where(place.low, lower, upper), got.astype(f32))

    return steps.run(key("done", kind), both, lower, upper, key("eswap", kind))


def on_device(
    tokens,
    doc_ids,
    knn_index,
    mem_keys,
    mem_values,
    qkv_weight,
    out_weight,
    in_weight,
    down_weight,
    norm_gain,
    norm_bias,
    rel_table,
    mem_gate,
    cotangent,
):
    seq_count, block_len, model_width = tokens.shape
    bucket_count, head_total = rel_table.shape[1:]
    head_dim = model_width // head_total
    topk_count = knn_index.shape[3]
    heads = head_total // CORES
    inner_width = heads * head_dim
    scale = 1.0 / math.sqrt(head_dim)
    place = Place(seq_count)
    steps = Steps()
    low_core = place.low
    pair_len = CORES * seq_count * block_len
    halo = WIN if place.pairs > 1 else 0
    by_chip = place.pairs == 1 and place.batches == 4

    norm_rows = jnp.stack([norm_gain[0], norm_bias[0]])
    shards = (qkv_weight[0], out_weight[0], in_weight[0], down_weight[0])
    memory = jnp.stack([mem_keys, mem_values]).reshape(2, mem_keys.shape[0], heads, CORES, head_dim)
    memory = jnp.transpose(memory, (3, 0, 1, 2, 4)).reshape(CORES, 2, 1, mem_keys.shape[0], inner_width)
    if by_chip:
        pieces, memory_at, sizes = gather_steps(steps, place, shards, norm_rows, memory)
    else:
        norms = lax.all_gather(norm_rows, (BAT, SEG), axis=0, tiled=False)
        norms = norms.reshape(place.batches, place.chips, LAYERS, 2, 2, norm_rows.shape[-1])
        norms = jnp.transpose(norms, (2, 3, 4, 1, 0, 5)).reshape(LAYERS, 2, 2, -1).astype(f32)
        weights = []
        for layer, matrices in enumerate(gather_plain(shards, place.core)):
            named = zip(("qkv", "out", "inner", "down", "norm"), (*matrices, norms[layer]))
            weights.append(tuple(steps.given(key(name, layer), array) for name, array in named))
        whole = lax.all_gather(memory, SEG, axis=3, tiled=True)
        memory_at = steps.given("memory", jnp.where(low_core, whole[0], whole[1])[:, 0])

    docs = lax.dynamic_index_in_dim(doc_ids, place.seq_no, 0, keepdims=False)
    first_row = place.stretch % place.pairs * pair_len
    docs_col = lax.dynamic_slice_in_dim(docs, first_row, pair_len, 0).reshape(pair_len, 1)
    docs_padded = jnp.concatenate([jnp.full((halo,), -1, jnp.int32), docs]) if halo else docs
    docs_row = lax.dynamic_slice_in_dim(docs_padded, first_row, halo + pair_len, 0).reshape(1, -1)
    steps.given("cols", docs_col)
    steps.given("rows", docs_row)
    onehot = distance_onehot(bucket_count)
    lanes = 1024

    def biases(table):
        tables = table.reshape(LAYERS, bucket_count, heads, CORES)
        tables = jnp.where(low_core, tables[..., 0], tables[..., 1])
        near = jnp.einsum("db,lbh->lhd", onehot[::-1], tables, precision=highest)[:, :, None]
        before = jnp.full((LAYERS, heads, 1, 1), big_negative, f32)
        beyond = jnp.full((LAYERS, heads, 1, lanes - WIN - 1), big_negative, f32)
        joined = jnp.concatenate([before, near, beyond], axis=3)
        return [joined[layer] for layer in range(LAYERS)]

    steps.run("bias", biases, steps.given("table", rel_table))
    gate_all = jax.nn.sigmoid(mem_gate).reshape(heads, CORES)
    gate = jnp.where(low_core, gate_all[:, 0], gate_all[:, 1])
    steps.given("gate", gate)

    def routed(name, array):
        return route_blocks(steps, place, name, steps.given(key(name, "in"), array))

    def by_head(blocks):
        rows = blocks.reshape(seq_count * block_len, head_total * topk_count)
        parts = [rows[:, h * topk_count : (h + 1) * topk_count] for h in range(head_total)]
        even, odd = jnp.concatenate(parts[::CORES], axis=1), jnp.concatenate(parts[1::CORES], axis=1)
        return jnp.where(low_core, even, odd), jnp.where(low_core, odd, even)

    slot_total = mem_keys.shape[0] * place.segments
    steps.run("flat", lambda v: v.reshape(seq_count, block_len, head_total * topk_count), steps.given("knn", knn_index))
    steps.run("kh", by_head, route_blocks(steps, place, "k", "flat"))
    swap(steps, "kswap", ("kh", 1))

    def whole_index(own, got):
        shape = (seq_count, block_len, heads * topk_count)
        pair = jnp.stack(place.both(own.reshape(shape), got.reshape(shape)), axis=1)
        return pair.reshape(pair_len, heads * topk_count)

    steps.run("index", whole_index, ("kh", 0), "kswap")
    masks = [
        steps.run(key("mask", head), lambda index, head=head: slot_mask(index, head, topk_count, slot_total), "index")
        for head in range(heads)
    ]

    own = routed("t", tokens)
    swap(steps, "tswap", own)
    hidden = steps.run("hid0", lambda own, got: place.sequence(own, got).astype(f32), own, "tswap")
    own = routed("c", cotangent)
    swap(steps, "cswap", own)
    upstream_low = steps.run("up", place.sequence, own, "cswap")
    upstream = upstream_low

    def halo_of(projected):
        if not halo:
            return None
        tail = projected[pair_len - halo :, inner_width:]
        route = [(i, i + CORES) for i in range(place.segments - CORES) if (i // CORES + 1) % place.pairs != 0]
        got = lax.ppermute(tail, SEG, route)
        return jnp.stack([got[:, :inner_width], got[:, inner_width:]])

    def halo_back(d_projected, halo_grad):
        route = [(i + CORES, i) for i in range(place.segments - CORES) if (i // CORES + 1) % place.pairs != 0]
        got = lax.ppermute(jnp.concatenate([halo_grad[0], halo_grad[1]], axis=1), SEG, route)
        edge = d_projected[pair_len - halo :, inner_width:].astype(f32) + got.astype(f32)
        return d_projected.at[pair_len - halo :, inner_width:].set(edge.astype(bf16))

    def attention(projected, bias, cols, rows, *rest):
        halo_rows = halo_of(projected)
        extra = (rest[0][0], rest[0][1], rest[1:-1], rest[-1]) if rest else None
        return attend(projected, bias, cols, rows, halo_rows, extra, scale)

    def attention_back(projected, grad, probs, *rest):
        halo_rows = halo_of(projected)
        extra = (rest[0][0], rest[0][1], *rest[1:]) if rest else None
        backs = attend_back(projected, grad, probs, halo_rows, extra, scale)
        if halo:
            backs = [halo_back(backs[0], backs[-1]), *backs[1:-1]]
        return backs

    if by_chip:
        head_rows, out_rows, width = sizes
        steps.given("at", place.batch.reshape(1))
        steps.given("place", jnp.stack([place.batch, place.stretch]))

    def row(norm, kind, which):
        return norm[2 * kind + which].reshape(1, -1) if by_chip else norm[kind, which].reshape(1, -1)

    def head_step(n, hidden):
        if not by_chip:
            qkv, norm = weights[n][0], weights[n][4]
            if n == 1:
                hidden = steps.run("hid1", joined, *hidden)
            steps.run(key("head", n), lambda h, norm, w: head_in(h, norm[0, 0], norm[1, 0], w), hidden, norm, qkv)
            return hidden

        def step(at, norm, hidden, *rest):
            joins, parts = rest[:-5], rest[-5:]
            return head_by_pieces(at, head_rows, hidden, joins, row(norm, 0, 0), row(norm, 1, 0), parts)

        steps.run(key("head", n), step, "at", key("norm", n), *(hidden if n == 1 else (hidden,)), *pieces[key("A", n)])
        return ("head1", 2) if n == 1 else hidden

    hidden_at = []
    for n in range(LAYERS):
        norm = key("norm", n) if by_chip else weights[n][4]
        hidden = head_step(n, hidden)
        hidden_at.append(hidden)
        extra = (memory_at, *masks, "gate") if n == 1 else ()
        steps.run(key("att", n), attention, (key("head", n), 1), ("bias", n), "cols", "rows", *extra)
        if by_chip:
            steps.run(
                key("op", n), lambda at, a, *parts: out_by_pieces(at, head_rows, out_rows, width, a, parts),
                "at", (key("att", n), 0), *pieces[key("A", n)],
            )
        else:
            steps.run(key("op", n), out_part, (key("att", n), 0), weights[n][1])
        swap(steps, key("oswap", n), key("op", n))
        steps.run(
            key("jn", n), lambda h, own, got, norm: join_norm(h, own, got, row(norm, 0, 1), row(norm, 1, 1)),
            hidden, key("op", n), key("oswap", n), norm,
        )
        if by_chip:
            steps.run(key("ex", n), lambda at, a, *parts: by_columns(at, a, parts, True), "at", (key("jn", n), 1), *pieces[key("I", n)])
            steps.run(key("dp", n), lambda at, a, *parts: by_columns(at, a, parts, False)[0], "at", (key("ex", n), 0), *pieces[key("D", n)])
        else:
            steps.run(key("ex", n), lambda a, w: smooth_pair(nt_dot(a, w)), (key("jn", n), 1), weights[n][2])
            steps.run(key("dp", n), down_part, (key("ex", n), 0), weights[n][3])
        swap(steps, key("dswap", n), key("dp", n))
        hidden = (("jn0", 0), "dp0", "dswap0")

    def last_rows(*a):
        return place.own_blocks(joined(*a).astype(bf16))

    steps.run("last", last_rows, ("jn1", 0), "dp1", "dswap1")
    mixed_at = route_blocks(steps, place, "m", "last", True)

    norm_parts, table_parts, reduced = [None, None], [None, None], [{}, {}]
    for n in (1, 0):
        norm = key("norm", n) if by_chip else weights[n][4]
        if by_chip:
            reduced[n]["D"] = scatter_steps(steps, place, key("D", n), upstream_low, (key("ex", n), 0))
            steps.run(
                key("pg", n), lambda at, g, slope, *parts: by_rows(at, 0, parts[0].shape[0], g, parts, slope),
                "at", upstream_low, (key("ex", n), 1), *pieces[key("D", n)],
            )
            steps.run(
                key("ip", n), lambda at, g, *parts: by_rows(at, 0, parts[0].shape[0], g, parts), "at", key("pg", n), *pieces[key("I", n)]
            )
            swap(steps, key("iswap", n), key("ip", n))
            reduced[n]["I"] = scatter_steps(steps, place, key("I", n), key("pg", n), (key("jn", n), 1))
        else:
            steps.run(key("gD", n), weight_grad, upstream_low, (key("ex", n), 0))
            steps.run(key("pg", n), expand_back, upstream_low, weights[n][3], (key("ex", n), 1))
            steps.run(key("ip", n), input_part, key("pg", n), weights[n][2])
            swap(steps, key("iswap", n), key("ip", n))
            steps.run(key("gI", n), weight_grad, key("pg", n), (key("jn", n), 1))
        steps.run(
            key("jb", n), lambda up, own, got, h, norm: join_back(up, own, got, h, row(norm, 0, 1)),
            upstream, key("ip", n), key("iswap", n), (key("jn", n), 0), norm,
        )
        if by_chip:
            steps.run(
                key("ag", n), lambda at, g, *parts: attended_back(at, head_rows, out_rows, width, g, parts),
                "at", (key("jb", n), 1), *pieces[key("A", n)],
            )
        else:
            steps.run(key("ag", n), lambda g, w: nt_dot(g, w).astype(bf16), (key("jb", n), 1), weights[n][1])
        extra = (memory_at, ("att1", 2), ("att1", 3), "gate") if n == 1 else ()
        steps.run(key("ab", n), attention_back, (key("head", n), 1), key("ag", n), (key("att", n), 1), *extra)
        if by_chip:
            steps.run(
                key("iq", n), lambda at, g, *parts: by_rows(at, 0, head_rows, g, parts), "at", (key("ab", n), 0), *pieces[key("A", n)]
            )
            swap(steps, key("qswap", n), key("iq", n))
            reduced[n]["A"] = scatter_steps(
                steps, place, key("A", n), (key("ab", n), 0), (key("head", n), 0), (key("att", n), 0), (key("jb", n), 1)
            )
        else:
            steps.run(key("iq", n), input_part, (key("ab", n), 0), weights[n][0])
            swap(steps, key("qswap", n), key("iq", n))
            steps.run(key("gQ", n), weight_grad, (key("ab", n), 0), (key("head", n), 0))
            steps.run(key("gO", n), weight_grad, (key("att", n), 0), (key("jb", n), 1))
        steps.run(
            key("jk", n), lambda up, own, got, h, norm: join_back(up, own, got, h, row(norm, 0, 0)),
            (key("jb", n), 0), key("iq", n), key("qswap", n), hidden_at[n], norm,
        )
        upstream, upstream_low = (key("jk", n), 0), (key("jk", n), 1)
        norm_parts[n] = steps.run(
            key("np", n), lambda a, b, c, d: jnp.stack([jnp.stack([a[0], b[0]]), jnp.stack([c[0], d[0]])]),
            (key("jk", n), 2), (key("jb", n), 2), (key("jk", n), 3), (key("jb", n), 3),
        )
        table_parts[n] = steps.run(
            key("tp", n),
            lambda d: jnp.einsum("db,hd->bh", onehot[::-1], d[:, 0, 1 : WIN + 1], precision=highest),
            (key("ab", n), 1),
        )

    steps.run("inlast", place.own_blocks, upstream_low)
    input_at = route_blocks(steps, place, "i", "inlast", True)

    def spread(values):
        empty = jnp.zeros_like(values)
        even = jnp.where(low_core, values, empty)
        odd = jnp.where(low_core, empty, values)
        return jnp.stack([even, odd], axis=-1).reshape(-1)

    sizes = [rel_table.size, head_total, LAYERS * 4 * model_width]
    ends = np.cumsum(sizes)
    room_total = -(-int(ends[-1]) // 1024) * 1024

    def flat(lower_table, upper_table, gates, gate, lower_norm, upper_norm):
        gate_part = jnp.sum(gates[:, 0], axis=-1) * gate * (1.0 - gate)
        parts = [
            spread(jnp.stack([lower_table, upper_table])),
            spread(gate_part),
            jnp.stack([lower_norm, upper_norm]).reshape(-1) * (1.0 / CORES),
        ]
        return jnp.concatenate(parts + [jnp.zeros((room_total - int(ends[-1]),), f32)]).reshape(-1, 128)

    sums = steps.run("sums", flat, table_parts[0], table_parts[1], ("ab1", 2), "gate", norm_parts[0], norm_parts[1])
    links = {(SEG, 1): "core", (BAT, 1): "x", (BAT, 2): "y"}
    for axis, count in ((SEG, place.segments), (BAT, place.batches)):
        bit = 1
        while bit < count:
            got = steps.send(
                key("u", axis[0], bit), links.get((axis, bit), "z"), lambda v, axis=axis, bit=bit: permuted(v, axis, lambda i: i ^ bit), sums
            )
            sums = steps.run(key("v", axis[0], bit), jnp.add, sums, got)
            bit *= 2

    if by_chip:
        done = {kind: finish_steps(steps, place, kind, reduced[0][kind], reduced[1][kind]) for kind in "DIA"}

    steps.carry_out(ORDER if by_chip and ORDER else range(len(steps.steps)))

    final = steps.value(sums).reshape(-1)
    table_sum = final[: ends[0]].reshape(rel_table.shape)
    gate_sum = final[ends[0] : ends[1]]
    norm_sum = final[ends[1] : ends[2]].reshape(LAYERS, 2, 2, place.chips, place.batches, norm_gain.shape[2])
    norm_sum = jnp.where(low_core, norm_sum[0], norm_sum[1])
    norm_sum = lax.dynamic_index_in_dim(norm_sum, place.stretch, 2, keepdims=False)
    norm_sum = lax.dynamic_index_in_dim(norm_sum, place.batch, 2, keepdims=False)
    if by_chip:
        halves = {kind: steps.value(name) for kind, name in done.items()}
        head = qkv_weight.shape[2] // 2
        matrices = [
            qkv_whole([h[:head] for h in halves["A"]])[None],
            out_whole([h[head:] for h in halves["A"]])[None],
            in_whole(halves["I"], 1)[None],
            down_whole(halves["D"], 1)[None],
        ]
    else:
        parts = [[steps.value(key("g", kind, n)) for kind in "QOID"] for n in range(LAYERS)]
        matrices = scatter_plain(parts, place.core)
    return (
        steps.value(mixed_at), steps.value(input_at), *matrices, norm_sum[0][None], norm_sum[1][None], table_sum, gate_sum,
    )


ORDER = (75, 76, 80, 71, 72, 85, 81, 83, 73, 53, 54, -77, 74, 60, 70, 56, -73, 61, 55, 0, -75, 1, 57, 58, 77, -62, 59, 78, -2, 2, -58, -79, 3, 79, -60, 37, 62, 63, 64, -4, 4, -65, 65, 68, -38, 12, 67, -5, 5, 69, -13, 13, -6, 20, 6, 7, 8, 66, -14, 14, -21, 21, -15, 28, 15, 16, -22, 17, -8, 22, -9, 10, -29, 9, -23, 82, 23, -83, 29, -17, 24, -18, 19, -30, 30, -10, 18, -11, 25, 11, 90, -31, 86, 31, -20, -87, 33, 45, -25, 32, 91, -46, -19, -26, 26, 27, 38, 92, -39, 93, -33, 39, -34, 35, -94, 34, 94, -40, 46, -27, 84, 40, -28, 41, 95, -47, -35, -36, 42, 47, 96, -85, -48, 97, 87, 88, 48, -42, -98, -89, 49, 44, -43, 50, 43, 89, 36, 98, -45, 99, -50, -44, 52, -51, 51, 100, 101, -102, 102, -53, 103, -52, 130, 131, 132, 115, 116, 117, 133, -133, 134, 135, 148, 149, -117, 119, -118, 121, 118, 120, -135, 137, -136, 139, 136, 138, 150, -122, -121, 153, 154, 155, 122, 151, 152, 104, -140, -139, -153, 105, 140, -156, -155, 141, 142, 157, -106, 159, 156, 158, -143, 143, 144, 123, 124, 170, 106, -145, 145, 146, 110, 108, 107, 168, -125, 111, 186, -147, -160, -159, 109, 187, -112, 188, 189, 190, 191, -110, 160, -189, 204, 161, 162, 171, -191, -192, 172, 173, -163, 192, 194, 163, 164, 193, -173, -165, -174, 195, 174, 176, 175, 177, 125, 126, 165, 205, 206, -127, -195, -196, 166, 196, 207, -167, 208, 197, 198, 209, -177, 210, -209, 211, 226, 167, -178, -199, 199, 200, 127, 128, 147, 178, 179, 224, -201, -211, -212, -129, 180, 213, 215, 212, -181, 214, 201, 202, 129, 181, 182, 227, 233, 231, 228, 229, 225, 169, 236, -203, 234, 237, 203, 250, 112, -238, 251, 238, -183, 230, -252, 252, -216, 183, -235, 184, -215, 216, -231, 232, 217, -185, 218, 185, 247, 248, -249, 249, -233, 113, 235, -219, 239, 219, -114, 220, -240, 114, 240, 241, -221, 221, -242, 222, 242, 243, -244, 244, 245, -223, 223, 253, 254, -246, 246, -255, 255)


def solution(mesh):
    placed = (
        P(BAT, SEG, None),
        P(BAT, None),
        P(BAT, SEG, None, None),
        P(SEG, None),
        P(SEG, None),
        P(SEG, None, BAT),
        P(SEG, None, BAT),
        P(SEG, None, BAT),
        P(SEG, None, BAT),
        P(SEG, None, BAT),
        P(SEG, None, BAT),
        P(),
        P(),
        P(BAT, SEG, None),
    )
    return jax.shard_map(
        on_device,
        mesh=mesh,
        in_specs=placed,
        out_specs=(
            P(BAT, SEG, None),
            P(BAT, SEG, None),
            P(SEG, None, BAT),
            P(SEG, None, BAT),
            P(SEG, None, BAT),
            P(SEG, None, BAT),
            P(SEG, None, BAT),
            P(SEG, None, BAT),
            P(),
            P(),
        ),
        check_vma=False,
    )
```
